128 devices in a mesh: row: 16 (over y, z_hi, core), col: 8 (over x, z_lo).
Axes of the slice: x: 4, y: 4, z: 4 (z_hi: 2, z_lo: 2; z = z_hi * 2 + z_lo), core: 2. Of those that a mesh axis runs over, the one named last changes fastest.
Arguments:
- orbitals: bfloat16 [24576, 2, 2048], P(('row', 'col')), may hold values from -6 to 6
- applied_orbitals: bfloat16 [24576, 2, 2048], P(('row', 'col')), may hold values from -6 to 6
- ritz_matrix: bfloat16 [2, 2048, 2048], P(None, 'row', 'col'), may hold values from -0.09375 to 0.09375
Outputs:
- rotated_orbitals: bfloat16 [24576, 2, 2048], P(('row', 'col'))
- rotated_applied: bfloat16 [24576, 2, 2048], P(('row', 'col'))
The draws below stay inside these ranges and needn't reach their ends.
All inputs are finite; a program needn't handle non-finite values.
Results may differ from the reference program's by a relative error of at most 0.001.
Values may be sent and summed in bfloat16 or wider, within the bound.
A program may use at most 128 MiB of HBM per device.

```python
import jax
import jax.numpy as jnp

NB = 2048
NG = 24576


def level_of(own_key, dims, cuts, low, top_value):
    level, own = 1.0, jax.random.fold_in(own_key, 6)
    for dim, parts in cuts:
        draws = jnp.exp(jax.random.uniform(jax.random.fold_in(own, dim), (parts,), jnp.float32, low / len(cuts), top_value / len(cuts)))
        level = level * jnp.repeat(draws, dims[dim] // parts).reshape([-1 if axis == dim else 1 for axis in range(len(dims))])
    return level


def bell_draw(rng, extent, spread, most, cuts=(), held_as=jnp.bfloat16):
    result = jax.random.normal(rng, extent, jnp.float32) * spread
    if len(cuts) > 0:
        result = level_of(rng, extent, cuts, -0.22, 0.18) * result
    return jnp.clip(result, min=-most, max=most).astype(held_as)


def setup_inputs(seed: int = 0) -> dict:
    arg_keys = jax.random.split(jax.random.key(seed), 4)
    orbitals = bell_draw(arg_keys[0], (NG, 2, NB), 1.0, 6.0, ((0, 128),))
    applied_orbitals = bell_draw(arg_keys[1], (NG, 2, NB), 1.0, 6.0, ((0, 128),))
    ritz_matrix = bell_draw(arg_keys[2], (2, NB, NB), (2 * NB) ** -0.5, 0.09375, ((1, 16), (2, 8)))
    return dict(orbitals=orbitals, applied_orbitals=applied_orbitals, ritz_matrix=ritz_matrix)


def rotate(wavefunction, ritz_matrix):
    row_count = wavefunction.shape[0]
    flattened = wavefunction.reshape(row_count, 2 * NB)
    real_part = ritz_matrix[0]
    imag_part = ritz_matrix[1]
    upper_half = jnp.concatenate([real_part, imag_part], 1)
    lower_half = jnp.concatenate([-imag_part, real_part], 1)
    real_block = jnp.concatenate([upper_half, lower_half], 0)
    product = jnp.dot(flattened, real_block, preferred_element_type=jnp.float32)
    return product.reshape(row_count, 2, NB).astype(jnp.bfloat16)


def reference(orbitals, applied_orbitals, ritz_matrix):
    return rotate(orbitals, ritz_matrix), rotate(applied_orbitals, ritz_matrix)
```

```python
import jax
import jax.numpy as jnp
from jax import lax
from jax.sharding import Mesh
from jax.sharding import PartitionSpec as P


def shards(orbitals, applied_orbitals, ritz_matrix):
    me = lax.axis_index("core")
    other = 1 - me
    rows = orbitals.shape[0]
    band_count = orbitals.shape[2]
    cols = ritz_matrix.shape[2]
    half = cols // 2
    col_blocks = band_count // cols

    stacked = jnp.stack([orbitals, applied_orbitals])
    both = lax.all_gather(stacked, "core")
    chip_block = lax.all_gather(ritz_matrix, "core")
    mine = lax.dynamic_slice_in_dim(chip_block, me * half, half, axis=3)
    gathered = lax.all_gather(mine, ("col", "rc"))
    gathered = gathered.reshape(col_blocks, -1, 2, 2, ritz_matrix.shape[1], half)

    lhs = both.reshape(2, 2, rows, 2, -1, 2, ritz_matrix.shape[1])
    prod = jnp.einsum(
        "xanqrok,cropkj->xanqpcj", lhs, gathered, preferred_element_type=jnp.float32
    )
    real = prod[:, :, :, 0, 0] - prod[:, :, :, 1, 1]
    imag = prod[:, :, :, 0, 1] + prod[:, :, :, 1, 0]
    result = jnp.stack([real, imag], 3).astype(jnp.bfloat16)

    own = lax.dynamic_index_in_dim(result, me, 0, keepdims=False)
    send = lax.dynamic_index_in_dim(result, other, 0, keepdims=False)
    recv = lax.ppermute(send, "core", [(0, 1), (1, 0)])
    first = jnp.where(me == 0, own, recv)
    second = jnp.where(me == 0, recv, own)
    out = jnp.stack([first, second], -2).reshape(2, rows, 2, band_count)
    return out[0], out[1]


def solution(mesh):
    devices = mesh.devices
    split = Mesh(
        devices.reshape(devices.shape[0] // 2, 2, devices.shape[1]), ("rc", "core", "col")
    )
    flat = ("rc", "core", "col")
    in_specs = (P(flat, None, None), P(flat, None, None), P(None, ("rc", "core"), "col"))
    out_specs = (P(flat, None, None), P(flat, None, None))
    return jax.shard_map(shards, mesh=split, in_specs=in_specs, out_specs=out_specs, check_vma=False)
```

```python
import jax
import jax.numpy as jnp
from jax import lax
from jax.sharding import Mesh
from jax.sharding import PartitionSpec as P


def shards(orbitals, applied_orbitals, ritz_matrix):
    me = lax.axis_index("core")
    other = 1 - me
    rows = orbitals.shape[0]
    band_count = orbitals.shape[2]
    cols = ritz_matrix.shape[2]
    half = cols // 2

    stacked = jnp.stack([orbitals, applied_orbitals])
    partner = lax.ppermute(stacked, "core", [(0, 1), (1, 0)])
    both = jnp.where(me == 0, jnp.stack([stacked, partner]), jnp.stack([partner, stacked]))
    chip_block = lax.all_gather(ritz_matrix, "core")
    mine = lax.dynamic_slice_in_dim(chip_block, me * half, half, axis=3)
    gathered = lax.all_gather(lax.all_gather(mine, "col"), "rc")

    lhs = both.reshape(2, 2, rows, 2, -1, 2, ritz_matrix.shape[1])
    prod = jnp.einsum(
        "xanqrok,rcopkj->xanqpcj", lhs, gathered, preferred_element_type=jnp.float32
    )
    real = prod[:, :, :, 0, 0] - prod[:, :, :, 1, 1]
    imag = prod[:, :, :, 0, 1] + prod[:, :, :, 1, 0]
    result = jnp.stack([real, imag], 3).astype(jnp.bfloat16)

    own = lax.dynamic_index_in_dim(result, me, 0, keepdims=False)
    send = lax.dynamic_index_in_dim(result, other, 0, keepdims=False)
    recv = lax.ppermute(send, "core", [(0, 1), (1, 0)])
    first = jnp.where(me == 0, own, recv)
    second = jnp.where(me == 0, recv, own)
    out = jnp.stack([first, second], -2).reshape(2, rows, 2, band_count)
    return out[0], out[1]


def solution(mesh):
    devices = mesh.devices
    split = Mesh(
        devices.reshape(devices.shape[0] // 2, 2, devices.shape[1]), ("rc", "core", "col")
    )
    flat = ("rc", "core", "col")
    in_specs = (P(flat, None, None), P(flat, None, None), P(None, ("rc", "core"), "col"))
    out_specs = (P(flat, None, None), P(flat, None, None))
    return jax.shard_map(shards, mesh=split, in_specs=in_specs, out_specs=out_specs, check_vma=False)
```

```python
import jax
import jax.numpy as jnp
from jax import lax
from jax.experimental import pallas as pl
from jax.experimental.pallas import tpu as pltpu
from jax.sharding import Mesh
from jax.sharding import PartitionSpec as P

SWAP = [(0, 1), (1, 0)]


def rotate_kernel(own_ref, partner_ref, ritz_ref, own_out, partner_out):
    rows = own_ref.shape[1]
    width = own_out.shape[-1]
    weights = ritz_ref[...].reshape(-1, 2 * width)
    for src, dst in ((own_ref, own_out), (partner_ref, partner_out)):
        lhs = src[...].reshape(2 * rows, -1)
        prod = jnp.dot(lhs, weights, preferred_element_type=jnp.float32)
        real = prod[:rows, :width] - prod[rows:, width:]
        imag = prod[:rows, width:] + prod[rows:, :width]
        dst[0] = real.astype(dst.dtype)
        dst[1] = imag.astype(dst.dtype)


def rotate(own, partner, gathered):
    q, rows, band = own.shape
    rc, cb, co, k, width2 = gathered.shape
    width = width2 // 2
    x_spec = pl.BlockSpec((q, rows, band), lambda c: (0, 0, 0))
    g_spec = pl.BlockSpec((rc, None, co, k, width2), lambda c: (0, c, 0, 0, 0))
    o_spec = pl.BlockSpec((2, None, rows, width), lambda c: (0, c, 0, 0))
    out = jax.ShapeDtypeStruct((2, cb, rows, width), jnp.bfloat16)
    flops = 2 * 2 * (2 * rows) * band * width2
    moved = 2 * own.size * 2 + gathered.size * 2 + 4 * rows * band * 2
    return pl.pallas_call(
        rotate_kernel,
        grid=(cb,),
        in_specs=[x_spec, x_spec, g_spec],
        out_specs=[o_spec, o_spec],
        out_shape=[out, out],
        compiler_params=pltpu.CompilerParams(vmem_limit_bytes=48 * 1024 * 1024),
        cost_estimate=pl.CostEstimate(flops=flops, transcendentals=0, bytes_accessed=moved),
    )(own, partner, gathered)


def shards(orbitals, applied_orbitals, ritz_matrix):
    me = lax.axis_index("core")
    rows = orbitals.shape[0]
    band_count = orbitals.shape[2]
    depth = ritz_matrix.shape[1]
    half = ritz_matrix.shape[2] // 2

    own = jnp.stack([orbitals, applied_orbitals]).transpose(2, 0, 1, 3).reshape(2, 2 * rows, band_count)
    partner = lax.ppermute(own, "core", SWAP)

    chip_block = lax.all_gather(ritz_matrix, "core")
    mine = lax.dynamic_slice_in_dim(chip_block, me * half, half, axis=3)
    mine = mine.transpose(0, 2, 1, 3).reshape(2, depth, 2 * half)
    gathered = lax.all_gather(lax.all_gather(mine, "col"), "rc")

    y_own, y_send = rotate(own, partner, gathered)
    recv = lax.ppermute(y_send, "core", SWAP)
    first = jnp.where(me == 0, y_own, recv)
    second = jnp.where(me == 0, recv, y_own)
    full = jnp.stack([first, second], 2)
    full = full.transpose(3, 0, 1, 2, 4).reshape(2, rows, 2, band_count)
    return full[0], full[1]


def solution(mesh):
    devices = mesh.devices
    split = Mesh(
        devices.reshape(devices.shape[0] // 2, 2, devices.shape[1]), ("rc", "core", "col")
    )
    flat = ("rc", "core", "col")
    in_specs = (P(flat, None, None), P(flat, None, None), P(None, ("rc", "core"), "col"))
    out_specs = (P(flat, None, None), P(flat, None, None))
    return jax.shard_map(shards, mesh=split, in_specs=in_specs, out_specs=out_specs, check_vma=False)
```

```python
import functools

import jax
import jax.numpy as jnp
from jax import lax
from jax.experimental import pallas as pl
from jax.experimental.pallas import tpu as pltpu
from jax.sharding import Mesh
from jax.sharding import PartitionSpec as P

SWAP = [(0, 1), (1, 0)]
AXES = ("rc", "core", "col")
MESH = pl.DeviceIdType.MESH


def peer(axis, index):
    ids = [lax.axis_index(a) for a in AXES]
    ids[AXES.index(axis)] = index
    return tuple(ids)


def gather_kernel(axis, n, x_ref, out_ref, send_sem, recv_sem, local_sem):
    me = lax.axis_index(axis)
    barrier = pltpu.get_barrier_semaphore()
    for d in range(1, n):
        pl.semaphore_signal(barrier, 1, device_id=peer(axis, lax.rem(me + d, n)), device_id_type=MESH)
    pl.semaphore_wait(barrier, n - 1)
    local = pltpu.make_async_copy(x_ref, out_ref.at[me], local_sem)
    local.start()
    copies = []
    for d in range(1, n):
        copy = pltpu.make_async_remote_copy(
            src_ref=x_ref,
            dst_ref=out_ref.at[me],
            send_sem=send_sem.at[d],
            recv_sem=recv_sem.at[d],
            device_id=peer(axis, lax.rem(me + d, n)),
            device_id_type=MESH,
        )
        copy.start()
        copies.append(copy)
    for d, copy in enumerate(copies, 1):
        copy.wait_send()
        src = lax.rem(me + n - d, n)
        incoming = pltpu.make_async_remote_copy(
            src_ref=x_ref,
            dst_ref=out_ref.at[src],
            send_sem=send_sem.at[d],
            recv_sem=recv_sem.at[d],
            device_id=peer(axis, src),
            device_id_type=MESH,
        )
        incoming.wait_recv()
    local.wait()


def gather(x, axis, n, cid):
    return pl.pallas_call(
        functools.partial(gather_kernel, axis, n),
        out_shape=jax.ShapeDtypeStruct((n,) + x.shape, x.dtype),
        in_specs=[pl.BlockSpec(memory_space=pl.ANY)],
        out_specs=pl.BlockSpec(memory_space=pl.ANY),
        scratch_shapes=[
            pltpu.SemaphoreType.DMA((n,)),
            pltpu.SemaphoreType.DMA((n,)),
            pltpu.SemaphoreType.DMA(()),
        ],
        compiler_params=pltpu.CompilerParams(collective_id=cid, has_side_effects=True),
    )(x)


def rotate_kernel(own_ref, partner_ref, ritz_ref, own_out, partner_out):
    rows = own_ref.shape[1]
    width = own_out.shape[-1]
    weights = ritz_ref[...].reshape(-1, 2 * width)
    for src, dst in ((own_ref, own_out), (partner_ref, partner_out)):
        lhs = src[...].reshape(2 * rows, -1)
        prod = jnp.dot(lhs, weights, preferred_element_type=jnp.float32)
        real = prod[:rows, :width] - prod[rows:, width:]
        imag = prod[:rows, width:] + prod[rows:, :width]
        dst[0] = real.astype(dst.dtype)
        dst[1] = imag.astype(dst.dtype)


def rotate(own, partner, gathered):
    q, rows, band = own.shape
    rc, cb, co, k, width2 = gathered.shape
    width = width2 // 2
    x_spec = pl.BlockSpec((q, rows, band), lambda c: (0, 0, 0))
    g_spec = pl.BlockSpec((rc, None, co, k, width2), lambda c: (0, c, 0, 0, 0))
    o_spec = pl.BlockSpec((2, None, rows, width), lambda c: (0, c, 0, 0))
    out = jax.ShapeDtypeStruct((2, cb, rows, width), jnp.bfloat16)
    flops = 2 * 2 * (2 * rows) * band * width2
    moved = 2 * own.size * 2 + gathered.size * 2 + 4 * rows * band * 2
    return pl.pallas_call(
        rotate_kernel,
        grid=(cb,),
        in_specs=[x_spec, x_spec, g_spec],
        out_specs=[o_spec, o_spec],
        out_shape=[out, out],
        compiler_params=pltpu.CompilerParams(vmem_limit_bytes=48 * 1024 * 1024),
        cost_estimate=pl.CostEstimate(flops=flops, transcendentals=0, bytes_accessed=moved),
    )(own, partner, gathered)


def shards(rc_count, col_count, orbitals, applied_orbitals, ritz_matrix):
    me = lax.axis_index("core")
    rows = orbitals.shape[0]
    band_count = orbitals.shape[2]
    depth = ritz_matrix.shape[1]
    half = ritz_matrix.shape[2] // 2

    own = jnp.stack([orbitals, applied_orbitals]).transpose(2, 0, 1, 3).reshape(2, 2 * rows, band_count)
    partner = lax.ppermute(own, "core", SWAP)

    chip_block = lax.all_gather(ritz_matrix, "core")
    mine = lax.dynamic_slice_in_dim(chip_block, me * half, half, axis=3)
    mine = mine.transpose(0, 2, 1, 3).reshape(2, depth, 2 * half)
    gathered = gather(gather(mine, "col", col_count, 0), "rc", rc_count, 1)

    y_own, y_send = rotate(own, partner, gathered)
    recv = lax.ppermute(y_send, "core", SWAP)
    first = jnp.where(me == 0, y_own, recv)
    second = jnp.where(me == 0, recv, y_own)
    full = jnp.stack([first, second], 2)
    full = full.transpose(3, 0, 1, 2, 4).reshape(2, rows, 2, band_count)
    return full[0], full[1]


def solution(mesh):
    devices = mesh.devices
    split = Mesh(
        devices.reshape(devices.shape[0] // 2, 2, devices.shape[1]), ("rc", "core", "col")
    )
    flat = ("rc", "core", "col")
    in_specs = (P(flat, None, None), P(flat, None, None), P(None, ("rc", "core"), "col"))
    out_specs = (P(flat, None, None), P(flat, None, None))
    body = functools.partial(shards, devices.shape[0] // 2, devices.shape[1])
    return jax.shard_map(body, mesh=split, in_specs=in_specs, out_specs=out_specs, check_vma=False)
```

```python
import functools

import jax
import jax.numpy as jnp
from jax import lax
from jax.experimental import pallas as pl
from jax.experimental.pallas import tpu as pltpu
from jax.sharding import Mesh
from jax.sharding import PartitionSpec as P

SWAP = [(0, 1), (1, 0)]
AXES = ("rc", "core", "col")
MESH = pl.DeviceIdType.MESH


def peer(axis, index):
    ids = [lax.axis_index(a) for a in AXES]
    ids[AXES.index(axis)] = index
    return tuple(ids)


def gather_kernel(axis, n, x_ref, out_ref, send_sem, recv_sem, local_sem):
    me = lax.axis_index(axis)
    barrier = pltpu.get_barrier_semaphore()
    for d in range(1, n):
        pl.semaphore_signal(barrier, 1, device_id=peer(axis, lax.rem(me + d, n)), device_id_type=MESH)
    pl.semaphore_wait(barrier, n - 1)
    local = pltpu.make_async_copy(x_ref, out_ref.at[me], local_sem)
    local.start()
    copies = []
    for d in range(1, n):
        copy = pltpu.make_async_remote_copy(
            src_ref=x_ref,
            dst_ref=out_ref.at[me],
            send_sem=send_sem.at[d],
            recv_sem=recv_sem.at[d],
            device_id=peer(axis, lax.rem(me + d, n)),
            device_id_type=MESH,
        )
        copy.start()
        copies.append(copy)
    for d, copy in enumerate(copies, 1):
        copy.wait_send()
        src = lax.rem(me + n - d, n)
        incoming = pltpu.make_async_remote_copy(
            src_ref=x_ref,
            dst_ref=out_ref.at[src],
            send_sem=send_sem.at[d],
            recv_sem=recv_sem.at[d],
            device_id=peer(axis, src),
            device_id_type=MESH,
        )
        incoming.wait_recv()
    local.wait()


def gather(x, axis, n, cid):
    return pl.pallas_call(
        functools.partial(gather_kernel, axis, n),
        out_shape=jax.ShapeDtypeStruct((n,) + x.shape, x.dtype),
        in_specs=[pl.BlockSpec(memory_space=pl.ANY)],
        out_specs=pl.BlockSpec(memory_space=pl.ANY),
        scratch_shapes=[
            pltpu.SemaphoreType.DMA((n,)),
            pltpu.SemaphoreType.DMA((n,)),
            pltpu.SemaphoreType.DMA(()),
        ],
        compiler_params=pltpu.CompilerParams(collective_id=cid, has_side_effects=True),
    )(x)


def rotate_kernel(own_ref, partner_ref, ritz_ref, own_out, partner_out):
    rows = own_ref.shape[1]
    width = own_out.shape[-1]
    weights = ritz_ref[...].reshape(-1, 2 * width)
    for src, dst in ((own_ref, own_out), (partner_ref, partner_out)):
        lhs = src[...].reshape(2 * rows, -1)
        prod = jnp.dot(lhs, weights, preferred_element_type=jnp.float32)
        real = prod[:rows, :width] - prod[rows:, width:]
        imag = prod[:rows, width:] + prod[rows:, :width]
        dst[0] = real.astype(dst.dtype)
        dst[1] = imag.astype(dst.dtype)


def rotate(own, partner, gathered):
    q, rows, band = own.shape
    rc, cb, co, k, width2 = gathered.shape
    width = width2 // 2
    x_spec = pl.BlockSpec((q, rows, band), lambda c: (0, 0, 0))
    g_spec = pl.BlockSpec((rc, None, co, k, width2), lambda c: (0, c, 0, 0, 0))
    o_spec = pl.BlockSpec((2, None, rows, width), lambda c: (0, c, 0, 0))
    out = jax.ShapeDtypeStruct((2, cb, rows, width), jnp.bfloat16)
    flops = 2 * 2 * (2 * rows) * band * width2
    moved = 2 * own.size * 2 + gathered.size * 2 + 4 * rows * band * 2
    return pl.pallas_call(
        rotate_kernel,
        grid=(cb,),
        in_specs=[x_spec, x_spec, g_spec],
        out_specs=[o_spec, o_spec],
        out_shape=[out, out],
        compiler_params=pltpu.CompilerParams(vmem_limit_bytes=48 * 1024 * 1024),
        cost_estimate=pl.CostEstimate(flops=flops, transcendentals=0, bytes_accessed=moved),
    )(own, partner, gathered)


def shards(rc_count, col_count, orbitals, applied_orbitals, ritz_matrix):
    me = lax.axis_index("core")
    rows = orbitals.shape[0]
    band_count = orbitals.shape[2]
    depth = ritz_matrix.shape[1]
    half = ritz_matrix.shape[2] // 2

    own = jnp.stack([orbitals, applied_orbitals]).transpose(2, 0, 1, 3).reshape(2, 2 * rows, band_count)
    partner = lax.ppermute(own, "core", SWAP)

    chip_block = lax.all_gather(ritz_matrix, "core")
    mine = lax.dynamic_slice_in_dim(chip_block, me * half, half, axis=3)
    mine = mine.transpose(0, 2, 1, 3).reshape(2, depth, 2 * half)
    strip = gather(mine, "col", col_count, 0)
    split = (5 * col_count) // 8
    offloaded = lax.all_gather(strip[:split], "rc")
    direct = gather(strip[split:], "rc", rc_count, 1)

    first_own, first_send = rotate(own, partner, offloaded)
    second_own, second_send = rotate(own, partner, direct)
    y_own = jnp.concatenate([first_own, second_own], 1)
    y_send = jnp.concatenate([first_send, second_send], 1)
    recv = lax.ppermute(y_send, "core", SWAP)
    first = jnp.where(me == 0, y_own, recv)
    second = jnp.where(me == 0, recv, y_own)
    full = jnp.stack([first, second], 2)
    full = full.transpose(3, 0, 1, 2, 4).reshape(2, rows, 2, band_count)
    return full[0], full[1]


def solution(mesh):
    devices = mesh.devices
    split = Mesh(
        devices.reshape(devices.shape[0] // 2, 2, devices.shape[1]), ("rc", "core", "col")
    )
    flat = ("rc", "core", "col")
    in_specs = (P(flat, None, None), P(flat, None, None), P(None, ("rc", "core"), "col"))
    out_specs = (P(flat, None, None), P(flat, None, None))
    body = functools.partial(shards, devices.shape[0] // 2, devices.shape[1])
    return jax.shard_map(body, mesh=split, in_specs=in_specs, out_specs=out_specs, check_vma=False)
```

```python
import functools

import jax
import jax.numpy as jnp
from jax import lax
from jax.experimental import pallas as pl
from jax.experimental.pallas import tpu as pltpu
from jax.sharding import Mesh
from jax.sharding import PartitionSpec as P

SWAP = [(0, 1), (1, 0)]
AXES = ("rc", "core", "col")
MESH = pl.DeviceIdType.MESH


RING = 4
ORDERS = (("x", "y", "z"), ("y", "z", "x"))
DIMS = ("y", "z_hi", "x", "z_lo")


def ring_gather_kernel(x_ref, g_ref, send_sem, recv_sem, local_sem):
    rc = lax.axis_index("rc")
    core = lax.axis_index("core")
    col = lax.axis_index("col")
    here = {"y": rc // 2, "z": (rc % 2) * 2 + col % 2, "x": col // 2}

    def device(axis, delta):
        at = dict(here)
        at[axis] = lax.rem(at[axis] + delta + RING, RING)
        return (at["y"] * 2 + at["z"] // 2, core, at["x"] * 2 + at["z"] % 2)

    def view(held, axis=None, delta=0, half=None):
        at = dict(here)
        if axis is not None:
            at[axis] = lax.rem(at[axis] + delta + RING, RING)
        index = []
        split = half is not None
        for dim in DIMS:
            phys = "z" if dim.startswith("z") else dim
            if phys in held:
                size = 2 if phys == "z" else RING
                if split:
                    index.append(pl.ds(half * (size // 2), size // 2))
                    split = False
                else:
                    index.append(slice(None))
            elif dim == "z_hi":
                index.append(at["z"] // 2)
            elif dim == "z_lo":
                index.append(at["z"] % 2)
            else:
                index.append(at[phys])
        if split:
            index.append(pl.ds(half, 1))
        return g_ref.at[tuple(index)]

    def remote(src, dst, slot, axis, delta):
        return pltpu.make_async_remote_copy(
            src_ref=src,
            dst_ref=dst,
            send_sem=send_sem.at[slot],
            recv_sem=recv_sem.at[slot],
            device_id=device(axis, delta),
            device_id_type=MESH,
        )

    barrier = pltpu.get_barrier_semaphore()
    for axis in ("x", "y", "z"):
        for delta in (1, -1):
            pl.semaphore_signal(barrier, 1, device_id=device(axis, delta), device_id_type=MESH)
    pl.semaphore_wait(barrier, 6)

    local = pltpu.make_async_copy(x_ref, view(()), local_sem)
    local.start()

    def run(order):
        held = ()
        for stage, axis in enumerate(order):
            base = stage * 4
            src = x_ref if stage == 0 else view(held)
            out = [
                remote(src, view(held), base + 0, axis, 1),
                remote(src, view(held), base + 1, axis, -1),
            ]
            for copy in out:
                copy.start()
            remote(src, view(held, axis, -1), base + 0, axis, -1).wait_recv()
            remote(src, view(held, axis, 1), base + 1, axis, 1).wait_recv()
            fwd = [
                remote(view(held, axis, 1, 0), view(held, axis, 1, 0), base + 2, axis, -1),
                remote(view(held, axis, -1, 1), view(held, axis, -1, 1), base + 3, axis, 1),
            ]
            for copy in fwd:
                copy.start()
            remote(view(held, axis, 2, 0), view(held, axis, 2, 0), base + 2, axis, 1).wait_recv()
            remote(view(held, axis, 2, 1), view(held, axis, 2, 1), base + 3, axis, -1).wait_recv()
            for copy in out + fwd:
                copy.wait_send()
            if stage == 0:
                local.wait()
            held = held + (axis,)

    for index, order in enumerate(ORDERS):
        @pl.when(core == index)
        def _():
            run(order)


def ring_gather(x):
    shape = (RING, 2, RING, 2) + x.shape
    return pl.pallas_call(
        ring_gather_kernel,
        out_shape=jax.ShapeDtypeStruct(shape, x.dtype),
        in_specs=[pl.BlockSpec(memory_space=pl.ANY)],
        out_specs=pl.BlockSpec(memory_space=pl.ANY),
        scratch_shapes=[
            pltpu.SemaphoreType.DMA((12,)),
            pltpu.SemaphoreType.DMA((12,)),
            pltpu.SemaphoreType.DMA(()),
        ],
        compiler_params=pltpu.CompilerParams(collective_id=0, has_side_effects=True),
    )(x)


def rotate_kernel(own_ref, partner_ref, ritz_ref, own_out, partner_out):
    rows = own_ref.shape[1]
    width = own_out.shape[-1]
    weights = ritz_ref[...].reshape(-1, 2 * width)
    for src, dst in ((own_ref, own_out), (partner_ref, partner_out)):
        lhs = src[...].reshape(2 * rows, -1)
        prod = jnp.dot(lhs, weights, preferred_element_type=jnp.float32)
        real = prod[:rows, :width] - prod[rows:, width:]
        imag = prod[:rows, width:] + prod[rows:, :width]
        dst[0] = real.astype(dst.dtype)
        dst[1] = imag.astype(dst.dtype)


def rotate(own, partner, gathered):
    q, rows, band = own.shape
    rc, cb, co, k, width2 = gathered.shape
    width = width2 // 2
    x_spec = pl.BlockSpec((q, rows, band), lambda c: (0, 0, 0))
    g_spec = pl.BlockSpec((rc, None, co, k, width2), lambda c: (0, c, 0, 0, 0))
    o_spec = pl.BlockSpec((2, None, rows, width), lambda c: (0, c, 0, 0))
    out = jax.ShapeDtypeStruct((2, cb, rows, width), jnp.bfloat16)
    flops = 2 * 2 * (2 * rows) * band * width2
    moved = 2 * own.size * 2 + gathered.size * 2 + 4 * rows * band * 2
    return pl.pallas_call(
        rotate_kernel,
        grid=(cb,),
        in_specs=[x_spec, x_spec, g_spec],
        out_specs=[o_spec, o_spec],
        out_shape=[out, out],
        compiler_params=pltpu.CompilerParams(vmem_limit_bytes=48 * 1024 * 1024),
        cost_estimate=pl.CostEstimate(flops=flops, transcendentals=0, bytes_accessed=moved),
    )(own, partner, gathered)


def shards(rc_count, col_count, orbitals, applied_orbitals, ritz_matrix):
    me = lax.axis_index("core")
    rows = orbitals.shape[0]
    band_count = orbitals.shape[2]
    depth = ritz_matrix.shape[1]
    half = ritz_matrix.shape[2] // 2

    own = jnp.stack([orbitals, applied_orbitals]).transpose(2, 0, 1, 3).reshape(2, 2 * rows, band_count)
    partner = lax.ppermute(own, "core", SWAP)

    chip_block = lax.all_gather(ritz_matrix, "core")
    mine = lax.dynamic_slice_in_dim(chip_block, me * half, half, axis=3)
    mine = mine.transpose(0, 2, 1, 3).reshape(2, depth, 2 * half)
    gathered = ring_gather(mine)
    gathered = gathered.reshape((-1, gathered.shape[2] * gathered.shape[3]) + mine.shape)
    y_own, y_send = rotate(own, partner, gathered)
    recv = lax.ppermute(y_send, "core", SWAP)
    first = jnp.where(me == 0, y_own, recv)
    second = jnp.where(me == 0, recv, y_own)
    full = jnp.stack([first, second], 2)
    full = full.transpose(3, 0, 1, 2, 4).reshape(2, rows, 2, band_count)
    return full[0], full[1]


def solution(mesh):
    devices = mesh.devices
    split = Mesh(
        devices.reshape(devices.shape[0] // 2, 2, devices.shape[1]), ("rc", "core", "col")
    )
    flat = ("rc", "core", "col")
    in_specs = (P(flat, None, None), P(flat, None, None), P(None, ("rc", "core"), "col"))
    out_specs = (P(flat, None, None), P(flat, None, None))
    body = functools.partial(shards, devices.shape[0] // 2, devices.shape[1])
    return jax.shard_map(body, mesh=split, in_specs=in_specs, out_specs=out_specs, check_vma=False)
```

```python
import functools

import jax
import jax.numpy as jnp
from jax import lax
from jax.experimental import pallas as pl
from jax.experimental.pallas import tpu as pltpu
from jax.sharding import Mesh
from jax.sharding import PartitionSpec as P

SWAP = [(0, 1), (1, 0)]
AXES = ("rc", "core", "col")
MESH = pl.DeviceIdType.MESH


RING = 4
ORDERS = (("x", "y", "z"), ("y", "z", "x"))
DIMS = ("y", "z_hi", "x", "z_lo")


def ring_gather_kernel(x_ref, g_ref, send_sem, recv_sem, local_sem):
    rc = lax.axis_index("rc")
    core = lax.axis_index("core")
    col = lax.axis_index("col")
    here = {"y": rc // 2, "z": (rc % 2) * 2 + col % 2, "x": col // 2}

    def device(axis, delta):
        at = dict(here)
        at[axis] = lax.rem(at[axis] + delta + RING, RING)
        return (at["y"] * 2 + at["z"] // 2, core, at["x"] * 2 + at["z"] % 2)

    def view(held, axis=None, delta=0, half=None):
        at = dict(here)
        if axis is not None:
            at[axis] = lax.rem(at[axis] + delta + RING, RING)
        index = []
        split = half is not None
        for dim in DIMS:
            phys = "z" if dim.startswith("z") else dim
            if phys in held:
                size = 2 if phys == "z" else RING
                if split:
                    index.append(pl.ds(half * (size // 2), size // 2))
                    split = False
                else:
                    index.append(slice(None))
            elif dim == "z_hi":
                index.append(at["z"] // 2)
            elif dim == "z_lo":
                index.append(at["z"] % 2)
            else:
                index.append(at[phys])
        if split:
            index.append(pl.ds(half, 1))
        return g_ref.at[tuple(index)]

    def remote(src, dst, slot, axis, delta):
        return pltpu.make_async_remote_copy(
            src_ref=src,
            dst_ref=dst,
            send_sem=send_sem.at[slot],
            recv_sem=recv_sem.at[slot],
            device_id=device(axis, delta),
            device_id_type=MESH,
        )

    partner = (rc, 1 - core, col)
    barrier = pltpu.get_barrier_semaphore()
    for axis in ("x", "y", "z"):
        for delta in (1, -1):
            pl.semaphore_signal(barrier, 1, device_id=device(axis, delta), device_id_type=MESH)
    pl.semaphore_signal(barrier, 1, device_id=partner, device_id_type=MESH)
    pl.semaphore_wait(barrier, 7)

    width = x_ref.shape[2] // 2
    unit = view(())
    keep = pl.multiple_of(core * width, width)
    give = pl.multiple_of((1 - core) * width, width)
    moves = []
    for p in range(2):
        dst = unit.at[core, :, pl.ds(p * width, width)]
        local = pltpu.make_async_copy(x_ref.at[p, :, pl.ds(keep, width)], dst, local_sem.at[p])
        local.start()
        swap = pltpu.make_async_remote_copy(
            src_ref=x_ref.at[p, :, pl.ds(give, width)],
            dst_ref=dst,
            send_sem=send_sem.at[12 + p],
            recv_sem=recv_sem.at[12 + p],
            device_id=partner,
            device_id_type=MESH,
        )
        swap.start()
        moves.append((local, swap, unit.at[1 - core, :, pl.ds(p * width, width)], p))
    for local, swap, dst, p in moves:
        local.wait()
        swap.wait_send()
        pltpu.make_async_remote_copy(
            src_ref=x_ref.at[p, :, pl.ds(give, width)],
            dst_ref=dst,
            send_sem=send_sem.at[12 + p],
            recv_sem=recv_sem.at[12 + p],
            device_id=partner,
            device_id_type=MESH,
        ).wait_recv()

    def run(order):
        held = ()
        for stage, axis in enumerate(order):
            base = stage * 4
            src = view(held)
            out = [
                remote(src, view(held), base + 0, axis, 1),
                remote(src, view(held), base + 1, axis, -1),
            ]
            for copy in out:
                copy.start()
            remote(src, view(held, axis, -1), base + 0, axis, -1).wait_recv()
            remote(src, view(held, axis, 1), base + 1, axis, 1).wait_recv()
            fwd = [
                remote(view(held, axis, 1, 0), view(held, axis, 1, 0), base + 2, axis, -1),
                remote(view(held, axis, -1, 1), view(held, axis, -1, 1), base + 3, axis, 1),
            ]
            for copy in fwd:
                copy.start()
            remote(view(held, axis, 2, 0), view(held, axis, 2, 0), base + 2, axis, 1).wait_recv()
            remote(view(held, axis, 2, 1), view(held, axis, 2, 1), base + 3, axis, -1).wait_recv()
            for copy in out + fwd:
                copy.wait_send()
            held = held + (axis,)

    for index, order in enumerate(ORDERS):
        @pl.when(core == index)
        def _():
            run(order)


def ring_gather(x):
    shape = (RING, 2, RING, 2, 2, x.shape[1], x.shape[2])
    return pl.pallas_call(
        ring_gather_kernel,
        out_shape=jax.ShapeDtypeStruct(shape, x.dtype),
        in_specs=[pl.BlockSpec(memory_space=pl.ANY)],
        out_specs=pl.BlockSpec(memory_space=pl.ANY),
        scratch_shapes=[
            pltpu.SemaphoreType.DMA((14,)),
            pltpu.SemaphoreType.DMA((14,)),
            pltpu.SemaphoreType.DMA((2,)),
        ],
        compiler_params=pltpu.CompilerParams(collective_id=0, has_side_effects=True),
    )(x)


def rotate_kernel(own_ref, partner_ref, ritz_ref, own_out, partner_out):
    band = own_ref.shape[1] // 2
    width = own_out.shape[-1]
    weights = ritz_ref[...].reshape(-1, 2 * width)
    for src, dst in ((own_ref, own_out), (partner_ref, partner_out)):
        first = jnp.dot(src[:, :band], weights, preferred_element_type=jnp.float32)
        second = jnp.dot(src[:, band:], weights, preferred_element_type=jnp.float32)
        real = first[:, :width] - second[:, width:]
        imag = first[:, width:] + second[:, :width]
        dst[0] = real.astype(dst.dtype)
        dst[1] = imag.astype(dst.dtype)


def rotate(own, partner, gathered):
    rows, band2 = own.shape
    rc, cb, co, k, width2 = gathered.shape
    width = width2 // 2
    x_spec = pl.BlockSpec((rows, band2), lambda c: (0, 0))
    g_spec = pl.BlockSpec((rc, None, co, k, width2), lambda c: (0, c, 0, 0, 0))
    o_spec = pl.BlockSpec((2, None, rows, width), lambda c: (0, c, 0, 0))
    out = jax.ShapeDtypeStruct((2, cb, rows, width), jnp.bfloat16)
    flops = 2 * 2 * rows * band2 * width2
    moved = 2 * own.size * 2 + gathered.size * 2 + 2 * own.size * 2
    return pl.pallas_call(
        rotate_kernel,
        grid=(cb,),
        in_specs=[x_spec, x_spec, g_spec],
        out_specs=[o_spec, o_spec],
        out_shape=[out, out],
        compiler_params=pltpu.CompilerParams(vmem_limit_bytes=48 * 1024 * 1024),
        cost_estimate=pl.CostEstimate(flops=flops, transcendentals=0, bytes_accessed=moved),
    )(own, partner, gathered)


def shards(rc_count, col_count, orbitals, applied_orbitals, ritz_matrix):
    me = lax.axis_index("core")
    rows = orbitals.shape[0]
    band_count = orbitals.shape[2]

    gathered = ring_gather(ritz_matrix)
    gathered = gathered.reshape((-1, gathered.shape[2] * gathered.shape[3]) + gathered.shape[4:])
    own = jnp.concatenate([orbitals.reshape(rows, -1), applied_orbitals.reshape(rows, -1)])
    partner = lax.ppermute(own, "core", SWAP)
    y_own, y_send = rotate(own, partner, gathered)
    recv = lax.ppermute(y_send, "core", SWAP)
    first = jnp.where(me == 0, y_own, recv)
    second = jnp.where(me == 0, recv, y_own)
    full = jnp.stack([first, second], 2)
    full = full.reshape(2, -1, 2, 2, rows, full.shape[-1])
    full = full.transpose(3, 4, 0, 1, 2, 5).reshape(2, rows, 2, band_count)
    return full[0], full[1]


def solution(mesh):
    devices = mesh.devices
    split = Mesh(
        devices.reshape(devices.shape[0] // 2, 2, devices.shape[1]), ("rc", "core", "col")
    )
    flat = ("rc", "core", "col")
    in_specs = (P(flat, None, None), P(flat, None, None), P(None, ("rc", "core"), "col"))
    out_specs = (P(flat, None, None), P(flat, None, None))
    body = functools.partial(shards, devices.shape[0] // 2, devices.shape[1])
    return jax.shard_map(body, mesh=split, in_specs=in_specs, out_specs=out_specs, check_vma=False)
```

```python
import functools

import jax
import jax.numpy as jnp
from jax import lax
from jax.experimental import pallas as pl
from jax.experimental.pallas import tpu as pltpu
from jax.sharding import Mesh
from jax.sharding import PartitionSpec as P

SWAP = [(0, 1), (1, 0)]
AXES = ("rc", "core", "col")
MESH = pl.DeviceIdType.MESH


RING = 4
ORDERS = (("x", "y", "z"), ("y", "z", "x"))
DIMS = ("y", "z_hi", "x", "z_lo")


def ring_rotate_kernel(x_ref, own_ref, own_out, send_out, g_ref, partner_ref, acc, send_sem, recv_sem, local_sem):
    rc = lax.axis_index("rc")
    core = lax.axis_index("core")
    col = lax.axis_index("col")
    here = {"y": rc // 2, "z": (rc % 2) * 2 + col % 2, "x": col // 2}

    def device(axis, delta):
        at = dict(here)
        at[axis] = lax.rem(at[axis] + delta + RING, RING)
        return (at["y"] * 2 + at["z"] // 2, core, at["x"] * 2 + at["z"] % 2)

    def view(held, axis=None, delta=0, half=None):
        at = dict(here)
        if axis is not None:
            at[axis] = lax.rem(at[axis] + delta + RING, RING)
        index = []
        split = half is not None
        for dim in DIMS:
            phys = "z" if dim.startswith("z") else dim
            if phys in held:
                size = 2 if phys == "z" else RING
                if split:
                    index.append(pl.ds(half * (size // 2), size // 2))
                    split = False
                else:
                    index.append(slice(None))
            elif dim == "z_hi":
                index.append(at["z"] // 2)
            elif dim == "z_lo":
                index.append(at["z"] % 2)
            else:
                index.append(at[phys])
        if split:
            index.append(pl.ds(half, 1))
        return g_ref.at[tuple(index)]

    def remote(src, dst, slot, axis, delta):
        return pltpu.make_async_remote_copy(
            src_ref=src,
            dst_ref=dst,
            send_sem=send_sem.at[slot],
            recv_sem=recv_sem.at[slot],
            device_id=device(axis, delta),
            device_id_type=MESH,
        )

    partner = (rc, 1 - core, col)
    barrier = pltpu.get_barrier_semaphore()
    for axis in ("x", "y", "z"):
        for delta in (1, -1):
            pl.semaphore_signal(barrier, 1, device_id=device(axis, delta), device_id_type=MESH)
    pl.semaphore_signal(barrier, 1, device_id=partner, device_id_type=MESH)
    pl.semaphore_wait(barrier, 7)

    acc[...] = jnp.zeros_like(acc)
    lend = pltpu.make_async_remote_copy(
        src_ref=own_ref,
        dst_ref=partner_ref,
        send_sem=send_sem.at[14],
        recv_sem=recv_sem.at[14],
        device_id=partner,
        device_id_type=MESH,
    )
    lend.start()

    band = own_ref.shape[1] // 2
    width = x_ref.shape[2] // 2
    depth = 2 * x_ref.shape[1]

    def compute(y, z, x):
        w = g_ref[y, z // 2, x, z % 2].reshape(depth, 2 * width)
        koff = pl.multiple_of((y * 2 + z // 2) * depth, depth)
        block = x * 2 + z % 2
        for src, rows in enumerate((own_ref, partner_ref)):
            first = jnp.dot(rows[:, pl.ds(koff, depth)], w, preferred_element_type=jnp.float32)
            second = jnp.dot(rows[:, pl.ds(band + koff, depth)], w, preferred_element_type=jnp.float32)
            acc[src, 0, block] += first[:, :width] - second[:, width:]
            acc[src, 1, block] += first[:, width:] + second[:, :width]

    def compute_block(held, axis=None, delta=0):
        at = dict(here)
        if axis is not None:
            at[axis] = lax.rem(at[axis] + delta + RING, RING)
        full = [d for d in ("y", "z", "x") if d in held]

        def body(i, carry):
            c = dict(at)
            rest = i
            for d in full:
                c[d] = rest % RING
                rest = rest // RING
            compute(c["y"], c["z"], c["x"])
            return carry

        lax.fori_loop(0, RING ** len(full), body, 0)

    unit = view(())
    keep = pl.multiple_of(core * width, width)
    give = pl.multiple_of((1 - core) * width, width)
    moves = []
    for p in range(2):
        dst = unit.at[core, :, pl.ds(p * width, width)]
        local = pltpu.make_async_copy(x_ref.at[p, :, pl.ds(keep, width)], dst, local_sem.at[p])
        local.start()
        swap = pltpu.make_async_remote_copy(
            src_ref=x_ref.at[p, :, pl.ds(give, width)],
            dst_ref=dst,
            send_sem=send_sem.at[12 + p],
            recv_sem=recv_sem.at[12 + p],
            device_id=partner,
            device_id_type=MESH,
        )
        swap.start()
        moves.append((local, swap, unit.at[1 - core, :, pl.ds(p * width, width)], p))
    for local, swap, dst, p in moves:
        local.wait()
        swap.wait_send()
        pltpu.make_async_remote_copy(
            src_ref=x_ref.at[p, :, pl.ds(give, width)],
            dst_ref=dst,
            send_sem=send_sem.at[12 + p],
            recv_sem=recv_sem.at[12 + p],
            device_id=partner,
            device_id_type=MESH,
        ).wait_recv()

    def run(order):
        held = ()
        for stage, axis in enumerate(order):
            base = stage * 4
            src = view(held)
            out = [
                remote(src, view(held), base + 0, axis, 1),
                remote(src, view(held), base + 1, axis, -1),
            ]
            for copy in out:
                copy.start()
            if stage == 2:
                lend.wait_send()
                pltpu.make_async_remote_copy(
                    src_ref=own_ref,
                    dst_ref=partner_ref,
                    send_sem=send_sem.at[14],
                    recv_sem=recv_sem.at[14],
                    device_id=partner,
                    device_id_type=MESH,
                ).wait_recv()
                compute_block(held)
            remote(src, view(held, axis, -1), base + 0, axis, -1).wait_recv()
            remote(src, view(held, axis, 1), base + 1, axis, 1).wait_recv()
            fwd = [
                remote(view(held, axis, 1, 0), view(held, axis, 1, 0), base + 2, axis, -1),
                remote(view(held, axis, -1, 1), view(held, axis, -1, 1), base + 3, axis, 1),
            ]
            for copy in fwd:
                copy.start()
            if stage == 2:
                compute_block(held, axis, -1)
                compute_block(held, axis, 1)
            remote(view(held, axis, 2, 0), view(held, axis, 2, 0), base + 2, axis, 1).wait_recv()
            remote(view(held, axis, 2, 1), view(held, axis, 2, 1), base + 3, axis, -1).wait_recv()
            for copy in out + fwd:
                copy.wait_send()
            if stage == 2:
                compute_block(held, axis, 2)
            held = held + (axis,)

    for index, order in enumerate(ORDERS):
        @pl.when(core == index)
        def _():
            run(order)

    own_out[...] = acc[0].astype(own_out.dtype)
    send_out[...] = acc[1].astype(send_out.dtype)


def ring_rotate(ritz, own):
    rows, band2 = own.shape
    units = (RING, 2, RING, 2, 2, ritz.shape[1], ritz.shape[2])
    width = ritz.shape[2] // 2
    out = jax.ShapeDtypeStruct((2, 2 * RING, rows, width), jnp.bfloat16)
    vmem = pl.BlockSpec(memory_space=pltpu.VMEM)
    flops = 2 * 2 * rows * band2 * 2 * ritz.shape[2] * 2 * RING
    return pl.pallas_call(
        ring_rotate_kernel,
        out_shape=[out, out],
        in_specs=[pl.BlockSpec(memory_space=pl.ANY), vmem],
        out_specs=[vmem, vmem],
        scratch_shapes=[
            pltpu.VMEM(units, ritz.dtype),
            pltpu.VMEM((rows, band2), own.dtype),
            pltpu.VMEM((2, 2, 2 * RING, rows, width), jnp.float32),
            pltpu.SemaphoreType.DMA((15,)),
            pltpu.SemaphoreType.DMA((15,)),
            pltpu.SemaphoreType.DMA((2,)),
        ],
        compiler_params=pltpu.CompilerParams(
            collective_id=0, has_side_effects=True, vmem_limit_bytes=60 * 1024 * 1024
        ),
        cost_estimate=pl.CostEstimate(flops=flops, transcendentals=0, bytes_accessed=4 * own.size * 2),
    )(ritz, own)


def rotate_kernel(own_ref, partner_ref, ritz_ref, own_out, partner_out):
    band = own_ref.shape[1] // 2
    width = own_out.shape[-1]
    weights = ritz_ref[...].reshape(-1, 2 * width)
    for src, dst in ((own_ref, own_out), (partner_ref, partner_out)):
        first = jnp.dot(src[:, :band], weights, preferred_element_type=jnp.float32)
        second = jnp.dot(src[:, band:], weights, preferred_element_type=jnp.float32)
        real = first[:, :width] - second[:, width:]
        imag = first[:, width:] + second[:, :width]
        dst[0] = real.astype(dst.dtype)
        dst[1] = imag.astype(dst.dtype)


def rotate(own, partner, gathered):
    rows, band2 = own.shape
    rc, cb, co, k, width2 = gathered.shape
    width = width2 // 2
    x_spec = pl.BlockSpec((rows, band2), lambda c: (0, 0))
    g_spec = pl.BlockSpec((rc, None, co, k, width2), lambda c: (0, c, 0, 0, 0))
    o_spec = pl.BlockSpec((2, None, rows, width), lambda c: (0, c, 0, 0))
    out = jax.ShapeDtypeStruct((2, cb, rows, width), jnp.bfloat16)
    flops = 2 * 2 * rows * band2 * width2
    moved = 2 * own.size * 2 + gathered.size * 2 + 2 * own.size * 2
    return pl.pallas_call(
        rotate_kernel,
        grid=(cb,),
        in_specs=[x_spec, x_spec, g_spec],
        out_specs=[o_spec, o_spec],
        out_shape=[out, out],
        compiler_params=pltpu.CompilerParams(vmem_limit_bytes=48 * 1024 * 1024),
        cost_estimate=pl.CostEstimate(flops=flops, transcendentals=0, bytes_accessed=moved),
    )(own, partner, gathered)


def shards(rc_count, col_count, orbitals, applied_orbitals, ritz_matrix):
    me = lax.axis_index("core")
    rows = orbitals.shape[0]
    band_count = orbitals.shape[2]

    own = jnp.concatenate([orbitals.reshape(rows, -1), applied_orbitals.reshape(rows, -1)])
    y_own, y_send = ring_rotate(ritz_matrix, own)
    recv = lax.ppermute(y_send, "core", SWAP)
    first = jnp.where(me == 0, y_own, recv)
    second = jnp.where(me == 0, recv, y_own)
    full = jnp.stack([first, second], 2)
    full = full.reshape(2, -1, 2, 2, rows, full.shape[-1])
    full = full.transpose(3, 4, 0, 1, 2, 5).reshape(2, rows, 2, band_count)
    return full[0], full[1]


def solution(mesh):
    devices = mesh.devices
    split = Mesh(
        devices.reshape(devices.shape[0] // 2, 2, devices.shape[1]), ("rc", "core", "col")
    )
    flat = ("rc", "core", "col")
    in_specs = (P(flat, None, None), P(flat, None, None), P(None, ("rc", "core"), "col"))
    out_specs = (P(flat, None, None), P(flat, None, None))
    body = functools.partial(shards, devices.shape[0] // 2, devices.shape[1])
    return jax.shard_map(body, mesh=split, in_specs=in_specs, out_specs=out_specs, check_vma=False)
```

```python
import functools

import jax
import jax.numpy as jnp
from jax import lax
from jax.experimental import pallas as pl
from jax.experimental.pallas import tpu as pltpu
from jax.sharding import Mesh
from jax.sharding import PartitionSpec as P

SWAP = [(0, 1), (1, 0)]
AXES = ("rc", "core", "col")
MESH = pl.DeviceIdType.MESH


RING = 4
ORDERS = (("x", "y", "z"), ("y", "z", "x"))
DIMS = ("y", "z_hi", "x", "z_lo")


def ring_rotate_kernel(
    x_ref, own_ref, orb_out, app_out, g_ref, partner_ref, acc, lent, back, send_sem, recv_sem, local_sem
):
    rc = lax.axis_index("rc")
    core = lax.axis_index("core")
    col = lax.axis_index("col")
    here = {"y": rc // 2, "z": (rc % 2) * 2 + col % 2, "x": col // 2}

    def device(axis, delta):
        at = dict(here)
        at[axis] = lax.rem(at[axis] + delta + RING, RING)
        return (at["y"] * 2 + at["z"] // 2, core, at["x"] * 2 + at["z"] % 2)

    def view(held, axis=None, delta=0, half=None):
        at = dict(here)
        if axis is not None:
            at[axis] = lax.rem(at[axis] + delta + RING, RING)
        index = []
        split = half is not None
        for dim in DIMS:
            phys = "z" if dim.startswith("z") else dim
            if phys in held:
                size = 2 if phys == "z" else RING
                if split:
                    index.append(pl.ds(half * (size // 2), size // 2))
                    split = False
                else:
                    index.append(slice(None))
            elif dim == "z_hi":
                index.append(at["z"] // 2)
            elif dim == "z_lo":
                index.append(at["z"] % 2)
            else:
                index.append(at[phys])
        if split:
            index.append(pl.ds(half, 1))
        return g_ref.at[tuple(index)]

    def remote(src, dst, slot, axis, delta):
        return pltpu.make_async_remote_copy(
            src_ref=src,
            dst_ref=dst,
            send_sem=send_sem.at[slot],
            recv_sem=recv_sem.at[slot],
            device_id=device(axis, delta),
            device_id_type=MESH,
        )

    partner = (rc, 1 - core, col)
    barrier = pltpu.get_barrier_semaphore()
    for axis in ("x", "y", "z"):
        for delta in (1, -1):
            pl.semaphore_signal(barrier, 1, device_id=device(axis, delta), device_id_type=MESH)
    pl.semaphore_signal(barrier, 1, device_id=partner, device_id_type=MESH)
    pl.semaphore_wait(barrier, 7)

    acc[...] = jnp.zeros_like(acc)
    lend = pltpu.make_async_remote_copy(
        src_ref=own_ref,
        dst_ref=partner_ref,
        send_sem=send_sem.at[14],
        recv_sem=recv_sem.at[14],
        device_id=partner,
        device_id_type=MESH,
    )
    lend.start()

    band = own_ref.shape[1] // 2
    width = x_ref.shape[2] // 2
    depth = 2 * x_ref.shape[1]

    def compute(y, z, x):
        w = g_ref[y, z // 2, x, z % 2].reshape(depth, 2 * width)
        koff = pl.multiple_of((y * 2 + z // 2) * depth, depth)
        block = x * 2 + z % 2
        for src, rows in enumerate((own_ref, partner_ref)):
            first = jnp.dot(rows[:, pl.ds(koff, depth)], w, preferred_element_type=jnp.float32)
            second = jnp.dot(rows[:, pl.ds(band + koff, depth)], w, preferred_element_type=jnp.float32)
            acc[src, 0, block] += first[:, :width] - second[:, width:]
            acc[src, 1, block] += first[:, width:] + second[:, :width]

    def compute_block(held, axis=None, delta=0):
        at = dict(here)
        if axis is not None:
            at[axis] = lax.rem(at[axis] + delta + RING, RING)
        full = [d for d in ("y", "z", "x") if d in held]

        def body(i, carry):
            c = dict(at)
            rest = i
            for d in full:
                c[d] = rest % RING
                rest = rest // RING
            compute(c["y"], c["z"], c["x"])
            return carry

        lax.fori_loop(0, RING ** len(full), body, 0)

    unit = view(())
    keep = pl.multiple_of(core * width, width)
    give = pl.multiple_of((1 - core) * width, width)
    moves = []
    for p in range(2):
        dst = unit.at[core, :, pl.ds(p * width, width)]
        local = pltpu.make_async_copy(x_ref.at[p, :, pl.ds(keep, width)], dst, local_sem.at[p])
        local.start()
        swap = pltpu.make_async_remote_copy(
            src_ref=x_ref.at[p, :, pl.ds(give, width)],
            dst_ref=dst,
            send_sem=send_sem.at[12 + p],
            recv_sem=recv_sem.at[12 + p],
            device_id=partner,
            device_id_type=MESH,
        )
        swap.start()
        moves.append((local, swap, unit.at[1 - core, :, pl.ds(p * width, width)], p))
    for local, swap, dst, p in moves:
        local.wait()
        swap.wait_send()
        pltpu.make_async_remote_copy(
            src_ref=x_ref.at[p, :, pl.ds(give, width)],
            dst_ref=dst,
            send_sem=send_sem.at[12 + p],
            recv_sem=recv_sem.at[12 + p],
            device_id=partner,
            device_id_type=MESH,
        ).wait_recv()

    def run(order):
        held = ()
        for stage, axis in enumerate(order):
            base = stage * 4
            src = view(held)
            out = [
                remote(src, view(held), base + 0, axis, 1),
                remote(src, view(held), base + 1, axis, -1),
            ]
            for copy in out:
                copy.start()
            if stage == 2:
                lend.wait_send()
                pltpu.make_async_remote_copy(
                    src_ref=own_ref,
                    dst_ref=partner_ref,
                    send_sem=send_sem.at[14],
                    recv_sem=recv_sem.at[14],
                    device_id=partner,
                    device_id_type=MESH,
                ).wait_recv()
                compute_block(held)
            remote(src, view(held, axis, -1), base + 0, axis, -1).wait_recv()
            remote(src, view(held, axis, 1), base + 1, axis, 1).wait_recv()
            fwd = [
                remote(view(held, axis, 1, 0), view(held, axis, 1, 0), base + 2, axis, -1),
                remote(view(held, axis, -1, 1), view(held, axis, -1, 1), base + 3, axis, 1),
            ]
            for copy in fwd:
                copy.start()
            if stage == 2:
                compute_block(held, axis, -1)
                compute_block(held, axis, 1)
            remote(view(held, axis, 2, 0), view(held, axis, 2, 0), base + 2, axis, 1).wait_recv()
            remote(view(held, axis, 2, 1), view(held, axis, 2, 1), base + 3, axis, -1).wait_recv()
            for copy in out + fwd:
                copy.wait_send()
            if stage == 2:
                compute_block(held, axis, 2)
            held = held + (axis,)

    for index, order in enumerate(ORDERS):
        @pl.when(core == index)
        def _():
            run(order)

    lent[...] = acc[1].astype(lent.dtype)
    give_back = pltpu.make_async_remote_copy(
        src_ref=lent,
        dst_ref=back,
        send_sem=send_sem.at[15],
        recv_sem=recv_sem.at[15],
        device_id=partner,
        device_id_type=MESH,
    )
    give_back.start()
    rows = orb_out.shape[0]
    blocks = acc.shape[2]

    def store(values, h):
        for a, out in enumerate((orb_out, app_out)):
            for c in range(blocks):
                lane = pl.multiple_of(c * 2 * width + h * width, width)
                part = [values[p, c, pl.ds(a * rows, rows), :].astype(out.dtype) for p in range(2)]
                out[:, :, pl.ds(lane, width)] = jnp.stack(part, axis=1)

    store(acc.at[0], core)
    give_back.wait_send()
    pltpu.make_async_remote_copy(
        src_ref=lent,
        dst_ref=back,
        send_sem=send_sem.at[15],
        recv_sem=recv_sem.at[15],
        device_id=partner,
        device_id_type=MESH,
    ).wait_recv()
    store(back, 1 - core)


def ring_rotate(ritz, own):
    rows, band2 = own.shape
    units = (RING, 2, RING, 2, 2, ritz.shape[1], ritz.shape[2])
    width = ritz.shape[2] // 2
    out = jax.ShapeDtypeStruct((rows // 2, 2, band2 // 2), jnp.bfloat16)
    vmem = pl.BlockSpec(memory_space=pltpu.VMEM)
    flops = 2 * 2 * rows * band2 * 2 * ritz.shape[2] * 2 * RING
    return pl.pallas_call(
        ring_rotate_kernel,
        out_shape=[out, out],
        in_specs=[pl.BlockSpec(memory_space=pl.ANY), vmem],
        out_specs=[vmem, vmem],
        scratch_shapes=[
            pltpu.VMEM(units, ritz.dtype),
            pltpu.VMEM((rows, band2), own.dtype),
            pltpu.VMEM((2, 2, 2 * RING, rows, width), jnp.float32),
            pltpu.VMEM((2, 2 * RING, rows, width), jnp.bfloat16),
            pltpu.VMEM((2, 2 * RING, rows, width), jnp.bfloat16),
            pltpu.SemaphoreType.DMA((16,)),
            pltpu.SemaphoreType.DMA((16,)),
            pltpu.SemaphoreType.DMA((2,)),
        ],
        compiler_params=pltpu.CompilerParams(
            collective_id=0, has_side_effects=True, vmem_limit_bytes=60 * 1024 * 1024
        ),
        cost_estimate=pl.CostEstimate(flops=flops, transcendentals=0, bytes_accessed=4 * own.size * 2),
    )(ritz, own)


def rotate_kernel(own_ref, partner_ref, ritz_ref, own_out, partner_out):
    band = own_ref.shape[1] // 2
    width = own_out.shape[-1]
    weights = ritz_ref[...].reshape(-1, 2 * width)
    for src, dst in ((own_ref, own_out), (partner_ref, partner_out)):
        first = jnp.dot(src[:, :band], weights, preferred_element_type=jnp.float32)
        second = jnp.dot(src[:, band:], weights, preferred_element_type=jnp.float32)
        real = first[:, :width] - second[:, width:]
        imag = first[:, width:] + second[:, :width]
        dst[0] = real.astype(dst.dtype)
        dst[1] = imag.astype(dst.dtype)


def rotate(own, partner, gathered):
    rows, band2 = own.shape
    rc, cb, co, k, width2 = gathered.shape
    width = width2 // 2
    x_spec = pl.BlockSpec((rows, band2), lambda c: (0, 0))
    g_spec = pl.BlockSpec((rc, None, co, k, width2), lambda c: (0, c, 0, 0, 0))
    o_spec = pl.BlockSpec((2, None, rows, width), lambda c: (0, c, 0, 0))
    out = jax.ShapeDtypeStruct((2, cb, rows, width), jnp.bfloat16)
    flops = 2 * 2 * rows * band2 * width2
    moved = 2 * own.size * 2 + gathered.size * 2 + 2 * own.size * 2
    return pl.pallas_call(
        rotate_kernel,
        grid=(cb,),
        in_specs=[x_spec, x_spec, g_spec],
        out_specs=[o_spec, o_spec],
        out_shape=[out, out],
        compiler_params=pltpu.CompilerParams(vmem_limit_bytes=48 * 1024 * 1024),
        cost_estimate=pl.CostEstimate(flops=flops, transcendentals=0, bytes_accessed=moved),
    )(own, partner, gathered)


def shards(rc_count, col_count, orbitals, applied_orbitals, ritz_matrix):
    me = lax.axis_index("core")
    rows = orbitals.shape[0]
    band_count = orbitals.shape[2]

    own = jnp.concatenate([orbitals.reshape(rows, -1), applied_orbitals.reshape(rows, -1)])
    orb_out, app_out = ring_rotate(ritz_matrix, own)
    return orb_out, app_out


def solution(mesh):
    devices = mesh.devices
    split = Mesh(
        devices.reshape(devices.shape[0] // 2, 2, devices.shape[1]), ("rc", "core", "col")
    )
    flat = ("rc", "core", "col")
    in_specs = (P(flat, None, None), P(flat, None, None), P(None, ("rc", "core"), "col"))
    out_specs = (P(flat, None, None), P(flat, None, None))
    body = functools.partial(shards, devices.shape[0] // 2, devices.shape[1])
    return jax.shard_map(body, mesh=split, in_specs=in_specs, out_specs=out_specs, check_vma=False)
```

```python
import functools

import jax
import jax.numpy as jnp
from jax import lax
from jax.experimental import pallas as pl
from jax.experimental.pallas import tpu as pltpu
from jax.sharding import Mesh
from jax.sharding import PartitionSpec as P

SWAP = [(0, 1), (1, 0)]
AXES = ("rc", "core", "col")
MESH = pl.DeviceIdType.MESH


RING = 4
ORDERS = (("x", "y", "z"), ("y", "z", "x"))
DIMS = ("y", "z_hi", "x", "z_lo")


def ring_rotate_kernel(
    x_ref, orb_ref, app_ref, orb_out, app_out, g_ref, own_ref, partner_ref, acc, lent, back, send_sem, recv_sem,
    local_sem,
):
    rc = lax.axis_index("rc")
    core = lax.axis_index("core")
    col = lax.axis_index("col")
    here = {"y": rc // 2, "z": (rc % 2) * 2 + col % 2, "x": col // 2}

    def device(axis, delta):
        at = dict(here)
        at[axis] = lax.rem(at[axis] + delta + RING, RING)
        return (at["y"] * 2 + at["z"] // 2, core, at["x"] * 2 + at["z"] % 2)

    def view(held, axis=None, delta=0, half=None):
        at = dict(here)
        if axis is not None:
            at[axis] = lax.rem(at[axis] + delta + RING, RING)
        index = []
        split = half is not None
        for dim in DIMS:
            phys = "z" if dim.startswith("z") else dim
            if phys in held:
                size = 2 if phys == "z" else RING
                if split:
                    index.append(pl.ds(half * (size // 2), size // 2))
                    split = False
                else:
                    index.append(slice(None))
            elif dim == "z_hi":
                index.append(at["z"] // 2)
            elif dim == "z_lo":
                index.append(at["z"] % 2)
            else:
                index.append(at[phys])
        if split:
            index.append(pl.ds(half, 1))
        return g_ref.at[tuple(index)]

    def remote(src, dst, slot, axis, delta):
        return pltpu.make_async_remote_copy(
            src_ref=src,
            dst_ref=dst,
            send_sem=send_sem.at[slot],
            recv_sem=recv_sem.at[slot],
            device_id=device(axis, delta),
            device_id_type=MESH,
        )

    partner = (rc, 1 - core, col)
    barrier = pltpu.get_barrier_semaphore()
    for axis in ("x", "y", "z"):
        for delta in (1, -1):
            pl.semaphore_signal(barrier, 1, device_id=device(axis, delta), device_id_type=MESH)
    pl.semaphore_signal(barrier, 1, device_id=partner, device_id_type=MESH)
    pl.semaphore_wait(barrier, 7)

    lend = pltpu.make_async_remote_copy(
        src_ref=own_ref,
        dst_ref=partner_ref,
        send_sem=send_sem.at[14],
        recv_sem=recv_sem.at[14],
        device_id=partner,
        device_id_type=MESH,
    )

    def build():
        count = orb_ref.shape[0]
        step = 32
        for a, raw in enumerate((orb_ref, app_ref)):
            for n in range(0, count, step):
                v = raw[pl.ds(n, step)]
                for q in range(2):
                    own_ref[pl.ds(a * count + n, step), pl.ds(q * band, band)] = v[:, q, :]

    band = own_ref.shape[1] // 2
    width = x_ref.shape[2] // 2
    depth = 2 * x_ref.shape[1]

    def compute(y, z, x):
        w = g_ref[y, z // 2, x, z % 2].reshape(depth, 2 * width)
        koff = pl.multiple_of((y * 2 + z // 2) * depth, depth)
        block = x * 2 + z % 2
        for src, rows in enumerate((own_ref, partner_ref)):
            first = jnp.dot(rows[:, pl.ds(koff, depth)], w, preferred_element_type=jnp.float32)
            second = jnp.dot(rows[:, pl.ds(band + koff, depth)], w, preferred_element_type=jnp.float32)
            acc[src, 0, block] += first[:, :width] - second[:, width:]
            acc[src, 1, block] += first[:, width:] + second[:, :width]

    def compute_block(held, axis=None, delta=0):
        at = dict(here)
        if axis is not None:
            at[axis] = lax.rem(at[axis] + delta + RING, RING)
        full = [d for d in ("y", "z", "x") if d in held]

        def body(i, carry):
            c = dict(at)
            rest = i
            for d in full:
                c[d] = rest % RING
                rest = rest // RING
            compute(c["y"], c["z"], c["x"])
            return carry

        lax.fori_loop(0, RING ** len(full), body, 0)

    unit = view(())
    keep = pl.multiple_of(core * width, width)
    give = pl.multiple_of((1 - core) * width, width)
    moves = []
    for p in range(2):
        dst = unit.at[core, :, pl.ds(p * width, width)]
        local = pltpu.make_async_copy(x_ref.at[p, :, pl.ds(keep, width)], dst, local_sem.at[p])
        local.start()
        swap = pltpu.make_async_remote_copy(
            src_ref=x_ref.at[p, :, pl.ds(give, width)],
            dst_ref=dst,
            send_sem=send_sem.at[12 + p],
            recv_sem=recv_sem.at[12 + p],
            device_id=partner,
            device_id_type=MESH,
        )
        swap.start()
        moves.append((local, swap, unit.at[1 - core, :, pl.ds(p * width, width)], p))
    for local, swap, dst, p in moves:
        local.wait()
        swap.wait_send()
        pltpu.make_async_remote_copy(
            src_ref=x_ref.at[p, :, pl.ds(give, width)],
            dst_ref=dst,
            send_sem=send_sem.at[12 + p],
            recv_sem=recv_sem.at[12 + p],
            device_id=partner,
            device_id_type=MESH,
        ).wait_recv()

    def run(order):
        held = ()
        for stage, axis in enumerate(order):
            base = stage * 4
            src = view(held)
            out = [
                remote(src, view(held), base + 0, axis, 1),
                remote(src, view(held), base + 1, axis, -1),
            ]
            for copy in out:
                copy.start()
            if stage == 0:
                build()
            if stage == 1:
                acc[...] = jnp.zeros_like(acc)
            if stage == 2:
                lend.wait_send()
                pltpu.make_async_remote_copy(
                    src_ref=own_ref,
                    dst_ref=partner_ref,
                    send_sem=send_sem.at[14],
                    recv_sem=recv_sem.at[14],
                    device_id=partner,
                    device_id_type=MESH,
                ).wait_recv()
                compute_block(held)
            remote(src, view(held, axis, -1), base + 0, axis, -1).wait_recv()
            remote(src, view(held, axis, 1), base + 1, axis, 1).wait_recv()
            fwd = [
                remote(view(held, axis, 1, 0), view(held, axis, 1, 0), base + 2, axis, -1),
                remote(view(held, axis, -1, 1), view(held, axis, -1, 1), base + 3, axis, 1),
            ]
            for copy in fwd:
                copy.start()
            if stage == 2:
                compute_block(held, axis, -1)
                compute_block(held, axis, 1)
            remote(view(held, axis, 2, 0), view(held, axis, 2, 0), base + 2, axis, 1).wait_recv()
            remote(view(held, axis, 2, 1), view(held, axis, 2, 1), base + 3, axis, -1).wait_recv()
            for copy in out + fwd:
                copy.wait_send()
            if stage == 0:
                lend.start()
            if stage == 2:
                compute_block(held, axis, 2)
            held = held + (axis,)

    for index, order in enumerate(ORDERS):
        @pl.when(core == index)
        def _():
            run(order)

    lent[...] = acc[1].astype(lent.dtype)
    give_back = pltpu.make_async_remote_copy(
        src_ref=lent,
        dst_ref=back,
        send_sem=send_sem.at[15],
        recv_sem=recv_sem.at[15],
        device_id=partner,
        device_id_type=MESH,
    )
    give_back.start()
    rows = orb_out.shape[0]
    blocks = acc.shape[2]

    def store(values, h):
        for a, out in enumerate((orb_out, app_out)):
            for c in range(blocks):
                lane = pl.multiple_of(c * 2 * width + h * width, width)
                part = [values[p, c, pl.ds(a * rows, rows), :].astype(out.dtype) for p in range(2)]
                out[:, :, pl.ds(lane, width)] = jnp.stack(part, axis=1)

    store(acc.at[0], core)
    give_back.wait_send()
    pltpu.make_async_remote_copy(
        src_ref=lent,
        dst_ref=back,
        send_sem=send_sem.at[15],
        recv_sem=recv_sem.at[15],
        device_id=partner,
        device_id_type=MESH,
    ).wait_recv()
    store(back, 1 - core)


def ring_rotate(ritz, orbitals, applied_orbitals):
    rows, band2 = 2 * orbitals.shape[0], 2 * orbitals.shape[2]
    own = orbitals
    units = (RING, 2, RING, 2, 2, ritz.shape[1], ritz.shape[2])
    width = ritz.shape[2] // 2
    out = jax.ShapeDtypeStruct((rows // 2, 2, band2 // 2), jnp.bfloat16)
    vmem = pl.BlockSpec(memory_space=pltpu.VMEM)
    flops = 2 * 2 * rows * band2 * 2 * ritz.shape[2] * 2 * RING
    return pl.pallas_call(
        ring_rotate_kernel,
        out_shape=[out, out],
        in_specs=[pl.BlockSpec(memory_space=pl.ANY), vmem, vmem],
        out_specs=[vmem, vmem],
        scratch_shapes=[
            pltpu.VMEM(units, ritz.dtype),
            pltpu.VMEM((rows, band2), own.dtype),
            pltpu.VMEM((rows, band2), own.dtype),
            pltpu.VMEM((2, 2, 2 * RING, rows, width), jnp.float32),
            pltpu.VMEM((2, 2 * RING, rows, width), jnp.bfloat16),
            pltpu.VMEM((2, 2 * RING, rows, width), jnp.bfloat16),
            pltpu.SemaphoreType.DMA((16,)),
            pltpu.SemaphoreType.DMA((16,)),
            pltpu.SemaphoreType.DMA((2,)),
        ],
        compiler_params=pltpu.CompilerParams(
            collective_id=0, has_side_effects=True, vmem_limit_bytes=60 * 1024 * 1024
        ),
        cost_estimate=pl.CostEstimate(flops=flops, transcendentals=0, bytes_accessed=8 * own.size * 2),
    )(ritz, orbitals, applied_orbitals)


def rotate_kernel(own_ref, partner_ref, ritz_ref, own_out, partner_out):
    band = own_ref.shape[1] // 2
    width = own_out.shape[-1]
    weights = ritz_ref[...].reshape(-1, 2 * width)
    for src, dst in ((own_ref, own_out), (partner_ref, partner_out)):
        first = jnp.dot(src[:, :band], weights, preferred_element_type=jnp.float32)
        second = jnp.dot(src[:, band:], weights, preferred_element_type=jnp.float32)
        real = first[:, :width] - second[:, width:]
        imag = first[:, width:] + second[:, :width]
        dst[0] = real.astype(dst.dtype)
        dst[1] = imag.astype(dst.dtype)


def rotate(own, partner, gathered):
    rows, band2 = own.shape
    rc, cb, co, k, width2 = gathered.shape
    width = width2 // 2
    x_spec = pl.BlockSpec((rows, band2), lambda c: (0, 0))
    g_spec = pl.BlockSpec((rc, None, co, k, width2), lambda c: (0, c, 0, 0, 0))
    o_spec = pl.BlockSpec((2, None, rows, width), lambda c: (0, c, 0, 0))
    out = jax.ShapeDtypeStruct((2, cb, rows, width), jnp.bfloat16)
    flops = 2 * 2 * rows * band2 * width2
    moved = 2 * own.size * 2 + gathered.size * 2 + 2 * own.size * 2
    return pl.pallas_call(
        rotate_kernel,
        grid=(cb,),
        in_specs=[x_spec, x_spec, g_spec],
        out_specs=[o_spec, o_spec],
        out_shape=[out, out],
        compiler_params=pltpu.CompilerParams(vmem_limit_bytes=48 * 1024 * 1024),
        cost_estimate=pl.CostEstimate(flops=flops, transcendentals=0, bytes_accessed=moved),
    )(own, partner, gathered)


def shards(rc_count, col_count, orbitals, applied_orbitals, ritz_matrix):
    me = lax.axis_index("core")
    rows = orbitals.shape[0]
    band_count = orbitals.shape[2]

    orb_out, app_out = ring_rotate(ritz_matrix, orbitals, applied_orbitals)
    return orb_out, app_out


def solution(mesh):
    devices = mesh.devices
    split = Mesh(
        devices.reshape(devices.shape[0] // 2, 2, devices.shape[1]), ("rc", "core", "col")
    )
    flat = ("rc", "core", "col")
    in_specs = (P(flat, None, None), P(flat, None, None), P(None, ("rc", "core"), "col"))
    out_specs = (P(flat, None, None), P(flat, None, None))
    body = functools.partial(shards, devices.shape[0] // 2, devices.shape[1])
    return jax.shard_map(body, mesh=split, in_specs=in_specs, out_specs=out_specs, check_vma=False)
```

```python
import functools

import jax
import jax.numpy as jnp
from jax import lax
from jax.experimental import pallas as pl
from jax.experimental.pallas import tpu as pltpu
from jax.sharding import Mesh
from jax.sharding import PartitionSpec as P

SWAP = [(0, 1), (1, 0)]
AXES = ("rc", "core", "col")
MESH = pl.DeviceIdType.MESH


RING = 4
ORDERS = (("x", "y", "z"), ("y", "z", "x"))
DIMS = ("y", "z_hi", "x", "z_lo")


def ring_rotate_kernel(
    x_ref, orb_ref, app_ref, orb_out, app_out, g_ref, own_ref, partner_ref, acc, lent, back, send_sem, recv_sem,
    local_sem,
):
    rc = lax.axis_index("rc")
    core = lax.axis_index("core")
    col = lax.axis_index("col")
    here = {"y": rc // 2, "z": (rc % 2) * 2 + col % 2, "x": col // 2}

    def device(axis, delta):
        at = dict(here)
        at[axis] = lax.rem(at[axis] + delta + RING, RING)
        return (at["y"] * 2 + at["z"] // 2, core, at["x"] * 2 + at["z"] % 2)

    def view(held, axis=None, delta=0, half=None):
        at = dict(here)
        if axis is not None:
            at[axis] = lax.rem(at[axis] + delta + RING, RING)
        index = []
        split = half is not None
        for dim in DIMS:
            phys = "z" if dim.startswith("z") else dim
            if phys in held:
                size = 2 if phys == "z" else RING
                if split:
                    index.append(pl.ds(half * (size // 2), size // 2))
                    split = False
                else:
                    index.append(slice(None))
            elif dim == "z_hi":
                index.append(at["z"] // 2)
            elif dim == "z_lo":
                index.append(at["z"] % 2)
            else:
                index.append(at[phys])
        if split:
            index.append(pl.ds(half, 1))
        return g_ref.at[tuple(index)]

    def remote(src, dst, slot, axis, delta):
        return pltpu.make_async_remote_copy(
            src_ref=src,
            dst_ref=dst,
            send_sem=send_sem.at[slot],
            recv_sem=recv_sem.at[slot],
            device_id=device(axis, delta),
            device_id_type=MESH,
        )

    partner = (rc, 1 - core, col)
    barrier = pltpu.get_barrier_semaphore()
    for axis in ("x", "y", "z"):
        for delta in (1, -1):
            pl.semaphore_signal(barrier, 1, device_id=device(axis, delta), device_id_type=MESH)
    pl.semaphore_signal(barrier, 1, device_id=partner, device_id_type=MESH)
    pl.semaphore_wait(barrier, 7)

    lend = pltpu.make_async_remote_copy(
        src_ref=own_ref,
        dst_ref=partner_ref,
        send_sem=send_sem.at[14],
        recv_sem=recv_sem.at[14],
        device_id=partner,
        device_id_type=MESH,
    )

    def build():
        count = orb_ref.shape[0]
        step = 32
        for a, raw in enumerate((orb_ref, app_ref)):
            for n in range(0, count, step):
                v = raw[pl.ds(n, step)]
                for q in range(2):
                    own_ref[pl.ds(a * count + n, step), pl.ds(q * band, band)] = v[:, q, :]

    band = own_ref.shape[1] // 2
    width = x_ref.shape[2] // 2
    depth = 2 * x_ref.shape[1]

    def compute(y, z, x, sources=(0, 1)):
        w = g_ref[y, z // 2, x, z % 2].reshape(depth, 2 * width)
        koff = pl.multiple_of((y * 2 + z // 2) * depth, depth)
        block = x * 2 + z % 2
        for src in sources:
            rows = (own_ref, partner_ref)[src]
            first = jnp.dot(rows[:, pl.ds(koff, depth)], w, preferred_element_type=jnp.float32)
            second = jnp.dot(rows[:, pl.ds(band + koff, depth)], w, preferred_element_type=jnp.float32)
            acc[src, 0, block] += first[:, :width] - second[:, width:]
            acc[src, 1, block] += first[:, width:] + second[:, :width]

    def compute_block(held, axis=None, delta=0, sources=(0, 1)):
        at = dict(here)
        if axis is not None:
            at[axis] = lax.rem(at[axis] + delta + RING, RING)
        full = [d for d in ("y", "z", "x") if d in held]

        def body(i, carry):
            c = dict(at)
            rest = i
            for d in full:
                c[d] = rest % RING
                rest = rest // RING
            compute(c["y"], c["z"], c["x"], sources)
            return carry

        lax.fori_loop(0, RING ** len(full), body, 0)

    unit = view(())
    keep = pl.multiple_of(core * width, width)
    give = pl.multiple_of((1 - core) * width, width)
    moves = []
    for p in range(2):
        dst = unit.at[core, :, pl.ds(p * width, width)]
        local = pltpu.make_async_copy(x_ref.at[p, :, pl.ds(keep, width)], dst, local_sem.at[p])
        local.start()
        swap = pltpu.make_async_remote_copy(
            src_ref=x_ref.at[p, :, pl.ds(give, width)],
            dst_ref=dst,
            send_sem=send_sem.at[12 + p],
            recv_sem=recv_sem.at[12 + p],
            device_id=partner,
            device_id_type=MESH,
        )
        swap.start()
        moves.append((local, swap, unit.at[1 - core, :, pl.ds(p * width, width)], p))
    for local, swap, dst, p in moves:
        local.wait()
        swap.wait_send()
        pltpu.make_async_remote_copy(
            src_ref=x_ref.at[p, :, pl.ds(give, width)],
            dst_ref=dst,
            send_sem=send_sem.at[12 + p],
            recv_sem=recv_sem.at[12 + p],
            device_id=partner,
            device_id_type=MESH,
        ).wait_recv()

    def finish(last):
        lent[...] = acc[1].astype(lent.dtype)
        give_back = pltpu.make_async_remote_copy(
            src_ref=lent,
            dst_ref=back,
            send_sem=send_sem.at[15],
            recv_sem=recv_sem.at[15],
            device_id=partner,
            device_id_type=MESH,
        )
        give_back.start()
        last()
        rows = orb_out.shape[0]
        blocks = acc.shape[2]

        def store(values, h):
            for a, out in enumerate((orb_out, app_out)):
                for c in range(blocks):
                    lane = pl.multiple_of(c * 2 * width + h * width, width)
                    part = [values[p, c, pl.ds(a * rows, rows), :].astype(out.dtype) for p in range(2)]
                    out[:, :, pl.ds(lane, width)] = jnp.stack(part, axis=1)

        store(acc.at[0], core)
        give_back.wait_send()
        pltpu.make_async_remote_copy(
            src_ref=lent,
            dst_ref=back,
            send_sem=send_sem.at[15],
            recv_sem=recv_sem.at[15],
            device_id=partner,
            device_id_type=MESH,
        ).wait_recv()
        store(back, 1 - core)

    def run(order):
        held = ()
        for stage, axis in enumerate(order):
            base = stage * 4
            src = view(held)
            out = [
                remote(src, view(held), base + 0, axis, 1),
                remote(src, view(held), base + 1, axis, -1),
            ]
            for copy in out:
                copy.start()
            if stage == 0:
                build()
            if stage == 1:
                acc[...] = jnp.zeros_like(acc)
            if stage == 2:
                lend.wait_send()
                pltpu.make_async_remote_copy(
                    src_ref=own_ref,
                    dst_ref=partner_ref,
                    send_sem=send_sem.at[14],
                    recv_sem=recv_sem.at[14],
                    device_id=partner,
                    device_id_type=MESH,
                ).wait_recv()
                compute_block(held)
            remote(src, view(held, axis, -1), base + 0, axis, -1).wait_recv()
            remote(src, view(held, axis, 1), base + 1, axis, 1).wait_recv()
            fwd = [
                remote(view(held, axis, 1, 0), view(held, axis, 1, 0), base + 2, axis, -1),
                remote(view(held, axis, -1, 1), view(held, axis, -1, 1), base + 3, axis, 1),
            ]
            for copy in fwd:
                copy.start()
            if stage == 2:
                compute_block(held, axis, -1)
                compute_block(held, axis, 1)
            remote(view(held, axis, 2, 0), view(held, axis, 2, 0), base + 2, axis, 1).wait_recv()
            remote(view(held, axis, 2, 1), view(held, axis, 2, 1), base + 3, axis, -1).wait_recv()
            for copy in out + fwd:
                copy.wait_send()
            if stage == 0:
                lend.start()
            if stage == 2:
                compute_block(held, axis, 2, (1,))
                finish(lambda: compute_block(held, axis, 2, (0,)))
            held = held + (axis,)

    for index, order in enumerate(ORDERS):
        @pl.when(core == index)
        def _():
            run(order)


def ring_rotate(ritz, orbitals, applied_orbitals):
    rows, band2 = 2 * orbitals.shape[0], 2 * orbitals.shape[2]
    own = orbitals
    units = (RING, 2, RING, 2, 2, ritz.shape[1], ritz.shape[2])
    width = ritz.shape[2] // 2
    out = jax.ShapeDtypeStruct((rows // 2, 2, band2 // 2), jnp.bfloat16)
    vmem = pl.BlockSpec(memory_space=pltpu.VMEM)
    flops = 2 * 2 * rows * band2 * 2 * ritz.shape[2] * 2 * RING
    return pl.pallas_call(
        ring_rotate_kernel,
        out_shape=[out, out],
        in_specs=[pl.BlockSpec(memory_space=pl.ANY), vmem, vmem],
        out_specs=[vmem, vmem],
        scratch_shapes=[
            pltpu.VMEM(units, ritz.dtype),
            pltpu.VMEM((rows, band2), own.dtype),
            pltpu.VMEM((rows, band2), own.dtype),
            pltpu.VMEM((2, 2, 2 * RING, rows, width), jnp.float32),
            pltpu.VMEM((2, 2 * RING, rows, width), jnp.bfloat16),
            pltpu.VMEM((2, 2 * RING, rows, width), jnp.bfloat16),
            pltpu.SemaphoreType.DMA((16,)),
            pltpu.SemaphoreType.DMA((16,)),
            pltpu.SemaphoreType.DMA((2,)),
        ],
        compiler_params=pltpu.CompilerParams(
            collective_id=0, has_side_effects=True, vmem_limit_bytes=60 * 1024 * 1024
        ),
        cost_estimate=pl.CostEstimate(flops=flops, transcendentals=0, bytes_accessed=8 * own.size * 2),
    )(ritz, orbitals, applied_orbitals)


def rotate_kernel(own_ref, partner_ref, ritz_ref, own_out, partner_out):
    band = own_ref.shape[1] // 2
    width = own_out.shape[-1]
    weights = ritz_ref[...].reshape(-1, 2 * width)
    for src, dst in ((own_ref, own_out), (partner_ref, partner_out)):
        first = jnp.dot(src[:, :band], weights, preferred_element_type=jnp.float32)
        second = jnp.dot(src[:, band:], weights, preferred_element_type=jnp.float32)
        real = first[:, :width] - second[:, width:]
        imag = first[:, width:] + second[:, :width]
        dst[0] = real.astype(dst.dtype)
        dst[1] = imag.astype(dst.dtype)


def rotate(own, partner, gathered):
    rows, band2 = own.shape
    rc, cb, co, k, width2 = gathered.shape
    width = width2 // 2
    x_spec = pl.BlockSpec((rows, band2), lambda c: (0, 0))
    g_spec = pl.BlockSpec((rc, None, co, k, width2), lambda c: (0, c, 0, 0, 0))
    o_spec = pl.BlockSpec((2, None, rows, width), lambda c: (0, c, 0, 0))
    out = jax.ShapeDtypeStruct((2, cb, rows, width), jnp.bfloat16)
    flops = 2 * 2 * rows * band2 * width2
    moved = 2 * own.size * 2 + gathered.size * 2 + 2 * own.size * 2
    return pl.pallas_call(
        rotate_kernel,
        grid=(cb,),
        in_specs=[x_spec, x_spec, g_spec],
        out_specs=[o_spec, o_spec],
        out_shape=[out, out],
        compiler_params=pltpu.CompilerParams(vmem_limit_bytes=48 * 1024 * 1024),
        cost_estimate=pl.CostEstimate(flops=flops, transcendentals=0, bytes_accessed=moved),
    )(own, partner, gathered)


def shards(rc_count, col_count, orbitals, applied_orbitals, ritz_matrix):
    me = lax.axis_index("core")
    rows = orbitals.shape[0]
    band_count = orbitals.shape[2]

    orb_out, app_out = ring_rotate(ritz_matrix, orbitals, applied_orbitals)
    return orb_out, app_out


def solution(mesh):
    devices = mesh.devices
    split = Mesh(
        devices.reshape(devices.shape[0] // 2, 2, devices.shape[1]), ("rc", "core", "col")
    )
    flat = ("rc", "core", "col")
    in_specs = (P(flat, None, None), P(flat, None, None), P(None, ("rc", "core"), "col"))
    out_specs = (P(flat, None, None), P(flat, None, None))
    body = functools.partial(shards, devices.shape[0] // 2, devices.shape[1])
    return jax.shard_map(body, mesh=split, in_specs=in_specs, out_specs=out_specs, check_vma=False)
```

```python
import functools

import jax
import jax.numpy as jnp
from jax import lax
from jax.experimental import pallas as pl
from jax.experimental.pallas import tpu as pltpu
from jax.sharding import Mesh
from jax.sharding import PartitionSpec as P

SWAP = [(0, 1), (1, 0)]
AXES = ("rc", "core", "col")
MESH = pl.DeviceIdType.MESH


RING = 4
ORDERS = (("x", "y", "z"), ("y", "z", "x"))
DIMS = ("y", "z_hi", "x", "z_lo")


def ring_rotate_kernel(
    x_ref, orb_ref, app_ref, own_out, back_out, g_ref, own_ref, partner_ref, acc, lent, back, send_sem, recv_sem,
    local_sem,
):
    rc = lax.axis_index("rc")
    core = lax.axis_index("core")
    col = lax.axis_index("col")
    here = {"y": rc // 2, "z": (rc % 2) * 2 + col % 2, "x": col // 2}

    def device(axis, delta):
        at = dict(here)
        at[axis] = lax.rem(at[axis] + delta + RING, RING)
        return (at["y"] * 2 + at["z"] // 2, core, at["x"] * 2 + at["z"] % 2)

    def view(held, axis=None, delta=0, half=None):
        at = dict(here)
        if axis is not None:
            at[axis] = lax.rem(at[axis] + delta + RING, RING)
        index = []
        split = half is not None
        for dim in DIMS:
            phys = "z" if dim.startswith("z") else dim
            if phys in held:
                size = 2 if phys == "z" else RING
                if split:
                    index.append(pl.ds(half * (size // 2), size // 2))
                    split = False
                else:
                    index.append(slice(None))
            elif dim == "z_hi":
                index.append(at["z"] // 2)
            elif dim == "z_lo":
                index.append(at["z"] % 2)
            else:
                index.append(at[phys])
        if split:
            index.append(pl.ds(half, 1))
        return g_ref.at[tuple(index)]

    def remote(src, dst, slot, axis, delta):
        return pltpu.make_async_remote_copy(
            src_ref=src,
            dst_ref=dst,
            send_sem=send_sem.at[slot],
            recv_sem=recv_sem.at[slot],
            device_id=device(axis, delta),
            device_id_type=MESH,
        )

    partner = (rc, 1 - core, col)
    barrier = pltpu.get_barrier_semaphore()
    for axis in ("x", "y", "z"):
        for delta in (1, -1):
            pl.semaphore_signal(barrier, 1, device_id=device(axis, delta), device_id_type=MESH)
    pl.semaphore_signal(barrier, 1, device_id=partner, device_id_type=MESH)
    pl.semaphore_wait(barrier, 7)

    lend = pltpu.make_async_remote_copy(
        src_ref=own_ref,
        dst_ref=partner_ref,
        send_sem=send_sem.at[14],
        recv_sem=recv_sem.at[14],
        device_id=partner,
        device_id_type=MESH,
    )

    def build():
        count = orb_ref.shape[0]
        step = 32
        for a, raw in enumerate((orb_ref, app_ref)):
            for n in range(0, count, step):
                v = raw[pl.ds(n, step)]
                for q in range(2):
                    own_ref[pl.ds(a * count + n, step), pl.ds(q * band, band)] = v[:, q, :]

    band = own_ref.shape[1] // 2
    width = x_ref.shape[2] // 2
    depth = 2 * x_ref.shape[1]

    def compute(y, z, x):
        w = g_ref[y, z // 2, x, z % 2].reshape(depth, 2 * width)
        koff = pl.multiple_of((y * 2 + z // 2) * depth, depth)
        block = x * 2 + z % 2
        for src, rows in enumerate((own_ref, partner_ref)):
            first = jnp.dot(rows[:, pl.ds(koff, depth)], w, preferred_element_type=jnp.float32)
            second = jnp.dot(rows[:, pl.ds(band + koff, depth)], w, preferred_element_type=jnp.float32)
            acc[src, 0, block] += first[:, :width] - second[:, width:]
            acc[src, 1, block] += first[:, width:] + second[:, :width]

    def compute_block(held, axis=None, delta=0):
        at = dict(here)
        if axis is not None:
            at[axis] = lax.rem(at[axis] + delta + RING, RING)
        full = [d for d in ("y", "z", "x") if d in held]

        def body(i, carry):
            c = dict(at)
            rest = i
            for d in full:
                c[d] = rest % RING
                rest = rest // RING
            compute(c["y"], c["z"], c["x"])
            return carry

        lax.fori_loop(0, RING ** len(full), body, 0)

    unit = view(())
    keep = pl.multiple_of(core * width, width)
    give = pl.multiple_of((1 - core) * width, width)
    moves = []
    for p in range(2):
        dst = unit.at[core, :, pl.ds(p * width, width)]
        local = pltpu.make_async_copy(x_ref.at[p, :, pl.ds(keep, width)], dst, local_sem.at[p])
        local.start()
        swap = pltpu.make_async_remote_copy(
            src_ref=x_ref.at[p, :, pl.ds(give, width)],
            dst_ref=dst,
            send_sem=send_sem.at[12 + p],
            recv_sem=recv_sem.at[12 + p],
            device_id=partner,
            device_id_type=MESH,
        )
        swap.start()
        moves.append((local, swap, unit.at[1 - core, :, pl.ds(p * width, width)], p))
    for local, swap, dst, p in moves:
        local.wait()
        swap.wait_send()
        pltpu.make_async_remote_copy(
            src_ref=x_ref.at[p, :, pl.ds(give, width)],
            dst_ref=dst,
            send_sem=send_sem.at[12 + p],
            recv_sem=recv_sem.at[12 + p],
            device_id=partner,
            device_id_type=MESH,
        ).wait_recv()

    def run(order):
        held = ()
        for stage, axis in enumerate(order):
            base = stage * 4
            src = view(held)
            out = [
                remote(src, view(held), base + 0, axis, 1),
                remote(src, view(held), base + 1, axis, -1),
            ]
            for copy in out:
                copy.start()
            if stage == 0:
                build()
            if stage == 1:
                acc[...] = jnp.zeros_like(acc)
            if stage == 2:
                lend.wait_send()
                pltpu.make_async_remote_copy(
                    src_ref=own_ref,
                    dst_ref=partner_ref,
                    send_sem=send_sem.at[14],
                    recv_sem=recv_sem.at[14],
                    device_id=partner,
                    device_id_type=MESH,
                ).wait_recv()
                compute_block(held)
            remote(src, view(held, axis, -1), base + 0, axis, -1).wait_recv()
            remote(src, view(held, axis, 1), base + 1, axis, 1).wait_recv()
            fwd = [
                remote(view(held, axis, 1, 0), view(held, axis, 1, 0), base + 2, axis, -1),
                remote(view(held, axis, -1, 1), view(held, axis, -1, 1), base + 3, axis, 1),
            ]
            for copy in fwd:
                copy.start()
            if stage == 2:
                compute_block(held, axis, -1)
                compute_block(held, axis, 1)
            remote(view(held, axis, 2, 0), view(held, axis, 2, 0), base + 2, axis, 1).wait_recv()
            remote(view(held, axis, 2, 1), view(held, axis, 2, 1), base + 3, axis, -1).wait_recv()
            for copy in out + fwd:
                copy.wait_send()
            if stage == 0:
                lend.start()
            if stage == 2:
                compute_block(held, axis, 2)
            held = held + (axis,)

    for index, order in enumerate(ORDERS):
        @pl.when(core == index)
        def _():
            run(order)

    lent[...] = acc[1].astype(lent.dtype)
    give_back = pltpu.make_async_remote_copy(
        src_ref=lent,
        dst_ref=back,
        send_sem=send_sem.at[15],
        recv_sem=recv_sem.at[15],
        device_id=partner,
        device_id_type=MESH,
    )
    give_back.start()
    own_out[...] = acc[0].astype(own_out.dtype)
    give_back.wait_send()
    pltpu.make_async_remote_copy(
        src_ref=lent,
        dst_ref=back,
        send_sem=send_sem.at[15],
        recv_sem=recv_sem.at[15],
        device_id=partner,
        device_id_type=MESH,
    ).wait_recv()
    back_out[...] = back[...]


def store_kernel(own_ref, back_ref, orb_out, app_out):
    core = lax.axis_index("core")
    rows = orb_out.shape[0]
    width = own_ref.shape[-1]
    for h, values in ((core, own_ref), (1 - core, back_ref)):
        for a, out in enumerate((orb_out, app_out)):
            for c in range(own_ref.shape[1]):
                lane = pl.multiple_of(c * 2 * width + h * width, width)
                part = [values[p, c, pl.ds(a * rows, rows), :] for p in range(2)]
                out[:, :, pl.ds(lane, width)] = jnp.stack(part, axis=1)


def ring_rotate(ritz, orbitals, applied_orbitals):
    rows, band2 = 2 * orbitals.shape[0], 2 * orbitals.shape[2]
    own = orbitals
    units = (RING, 2, RING, 2, 2, ritz.shape[1], ritz.shape[2])
    width = ritz.shape[2] // 2
    out = jax.ShapeDtypeStruct((2, 2 * RING, rows, width), jnp.bfloat16)
    vmem = pl.BlockSpec(memory_space=pltpu.VMEM)
    flops = 2 * 2 * rows * band2 * 2 * ritz.shape[2] * 2 * RING
    return pl.pallas_call(
        ring_rotate_kernel,
        out_shape=[out, out],
        in_specs=[pl.BlockSpec(memory_space=pl.ANY), vmem, vmem],
        out_specs=[vmem, vmem],
        scratch_shapes=[
            pltpu.VMEM(units, ritz.dtype),
            pltpu.VMEM((rows, band2), own.dtype),
            pltpu.VMEM((rows, band2), own.dtype),
            pltpu.VMEM((2, 2, 2 * RING, rows, width), jnp.float32),
            pltpu.VMEM((2, 2 * RING, rows, width), jnp.bfloat16),
            pltpu.VMEM((2, 2 * RING, rows, width), jnp.bfloat16),
            pltpu.SemaphoreType.DMA((16,)),
            pltpu.SemaphoreType.DMA((16,)),
            pltpu.SemaphoreType.DMA((2,)),
        ],
        compiler_params=pltpu.CompilerParams(
            collective_id=0, has_side_effects=True, vmem_limit_bytes=60 * 1024 * 1024
        ),
        cost_estimate=pl.CostEstimate(flops=flops, transcendentals=0, bytes_accessed=8 * own.size * 2),
    )(ritz, orbitals, applied_orbitals)


def rotate_kernel(own_ref, partner_ref, ritz_ref, own_out, partner_out):
    band = own_ref.shape[1] // 2
    width = own_out.shape[-1]
    weights = ritz_ref[...].reshape(-1, 2 * width)
    for src, dst in ((own_ref, own_out), (partner_ref, partner_out)):
        first = jnp.dot(src[:, :band], weights, preferred_element_type=jnp.float32)
        second = jnp.dot(src[:, band:], weights, preferred_element_type=jnp.float32)
        real = first[:, :width] - second[:, width:]
        imag = first[:, width:] + second[:, :width]
        dst[0] = real.astype(dst.dtype)
        dst[1] = imag.astype(dst.dtype)


def rotate(own, partner, gathered):
    rows, band2 = own.shape
    rc, cb, co, k, width2 = gathered.shape
    width = width2 // 2
    x_spec = pl.BlockSpec((rows, band2), lambda c: (0, 0))
    g_spec = pl.BlockSpec((rc, None, co, k, width2), lambda c: (0, c, 0, 0, 0))
    o_spec = pl.BlockSpec((2, None, rows, width), lambda c: (0, c, 0, 0))
    out = jax.ShapeDtypeStruct((2, cb, rows, width), jnp.bfloat16)
    flops = 2 * 2 * rows * band2 * width2
    moved = 2 * own.size * 2 + gathered.size * 2 + 2 * own.size * 2
    return pl.pallas_call(
        rotate_kernel,
        grid=(cb,),
        in_specs=[x_spec, x_spec, g_spec],
        out_specs=[o_spec, o_spec],
        out_shape=[out, out],
        compiler_params=pltpu.CompilerParams(vmem_limit_bytes=48 * 1024 * 1024),
        cost_estimate=pl.CostEstimate(flops=flops, transcendentals=0, bytes_accessed=moved),
    )(own, partner, gathered)


def shards(rc_count, col_count, orbitals, applied_orbitals, ritz_matrix):
    me = lax.axis_index("core")
    rows = orbitals.shape[0]
    band_count = orbitals.shape[2]

    own_half, back_half = ring_rotate(ritz_matrix, orbitals, applied_orbitals)
    vmem = pl.BlockSpec(memory_space=pltpu.VMEM)
    final = jax.ShapeDtypeStruct(orbitals.shape, orbitals.dtype)
    orb_out, app_out = pl.pallas_call(
        store_kernel,
        out_shape=[final, final],
        in_specs=[vmem, vmem],
        out_specs=[vmem, vmem],
    )(own_half, back_half)
    return orb_out, app_out


def solution(mesh):
    devices = mesh.devices
    split = Mesh(
        devices.reshape(devices.shape[0] // 2, 2, devices.shape[1]), ("rc", "core", "col")
    )
    flat = ("rc", "core", "col")
    in_specs = (P(flat, None, None), P(flat, None, None), P(None, ("rc", "core"), "col"))
    out_specs = (P(flat, None, None), P(flat, None, None))
    body = functools.partial(shards, devices.shape[0] // 2, devices.shape[1])
    return jax.shard_map(body, mesh=split, in_specs=in_specs, out_specs=out_specs, check_vma=False)
```

```python
import functools

import jax
import jax.numpy as jnp
from jax import lax
from jax.experimental import pallas as pl
from jax.experimental.pallas import tpu as pltpu
from jax.sharding import Mesh
from jax.sharding import PartitionSpec as P

SWAP = [(0, 1), (1, 0)]
AXES = ("rc", "core", "col")
MESH = pl.DeviceIdType.MESH


RING = 4
ORDERS = (("x", "y", "z"), ("y", "z", "x"))
DIMS = ("y", "z_hi", "x", "z_lo")


def ring_rotate_kernel(
    x_ref, orb_ref, app_ref, orb_out, app_out, g_ref, own_ref, partner_ref, acc, lent, back, send_sem, recv_sem,
    local_sem, ring_send, ring_recv,
):
    rc = lax.axis_index("rc")
    core = lax.axis_index("core")
    col = lax.axis_index("col")
    here = {"y": rc // 2, "z": (rc % 2) * 2 + col % 2, "x": col // 2}

    def device(axis, delta):
        at = dict(here)
        at[axis] = lax.rem(at[axis] + delta + RING, RING)
        return (at["y"] * 2 + at["z"] // 2, core, at["x"] * 2 + at["z"] % 2)

    def view(held, axis=None, delta=0, half=None, pin=None):
        at = dict(here)
        pins = {} if pin is None else {pin[0]: pin[1]}
        if axis is not None:
            pins[axis] = delta
        for a, d in pins.items():
            at[a] = lax.rem(at[a] + d + RING, RING)
        held = tuple(h for h in held if h not in pins)
        index = []
        split = half is not None
        for dim in DIMS:
            phys = "z" if dim.startswith("z") else dim
            if phys in held:
                size = 2 if phys == "z" else RING
                if split:
                    index.append(pl.ds(half * (size // 2), size // 2))
                    split = False
                else:
                    index.append(slice(None))
            elif dim == "z_hi":
                index.append(at["z"] // 2)
            elif dim == "z_lo":
                index.append(at["z"] % 2)
            else:
                index.append(at[phys])
        if split:
            index.append(pl.ds(half, 1))
        return g_ref.at[tuple(index)]

    def remote(src, dst, slot, axis, delta):
        return pltpu.make_async_remote_copy(
            src_ref=src,
            dst_ref=dst,
            send_sem=send_sem.at[slot],
            recv_sem=recv_sem.at[slot],
            device_id=device(axis, delta),
            device_id_type=MESH,
        )

    partner = (rc, 1 - core, col)
    barrier = pltpu.get_barrier_semaphore()
    for axis in ("x", "y", "z"):
        for delta in (1, -1):
            pl.semaphore_signal(barrier, 1, device_id=device(axis, delta), device_id_type=MESH)
    pl.semaphore_signal(barrier, 1, device_id=partner, device_id_type=MESH)
    pl.semaphore_wait(barrier, 7)

    lend = pltpu.make_async_remote_copy(
        src_ref=own_ref,
        dst_ref=partner_ref,
        send_sem=send_sem.at[14],
        recv_sem=recv_sem.at[14],
        device_id=partner,
        device_id_type=MESH,
    )

    def build():
        count = orb_ref.shape[0]
        step = 32
        for a, raw in enumerate((orb_ref, app_ref)):
            for n in range(0, count, step):
                v = raw[pl.ds(n, step)]
                for q in range(2):
                    own_ref[pl.ds(a * count + n, step), pl.ds(q * band, band)] = v[:, q, :]

    band = own_ref.shape[1] // 2
    width = x_ref.shape[2] // 2
    depth = 2 * x_ref.shape[1]

    def compute(y, z, x):
        w = g_ref[y, z // 2, x, z % 2].reshape(depth, 2 * width)
        koff = pl.multiple_of((y * 2 + z // 2) * depth, depth)
        block = x * 2 + z % 2
        for src, rows in enumerate((own_ref, partner_ref)):
            first = jnp.dot(rows[:, pl.ds(koff, depth)], w, preferred_element_type=jnp.float32)
            second = jnp.dot(rows[:, pl.ds(band + koff, depth)], w, preferred_element_type=jnp.float32)
            acc[src, 0, block] += first[:, :width] - second[:, width:]
            acc[src, 1, block] += first[:, width:] + second[:, :width]

    def compute_block(held, axis=None, delta=0):
        at = dict(here)
        if axis is not None:
            at[axis] = lax.rem(at[axis] + delta + RING, RING)
        full = [d for d in ("y", "z", "x") if d in held]

        def body(i, carry):
            c = dict(at)
            rest = i
            for d in full:
                c[d] = rest % RING
                rest = rest // RING
            compute(c["y"], c["z"], c["x"])
            return carry

        lax.fori_loop(0, RING ** len(full), body, 0)

    unit = view(())
    keep = pl.multiple_of(core * width, width)
    give = pl.multiple_of((1 - core) * width, width)
    moves = []
    for p in range(2):
        dst = unit.at[core, :, pl.ds(p * width, width)]
        local = pltpu.make_async_copy(x_ref.at[p, :, pl.ds(keep, width)], dst, local_sem.at[p])
        local.start()
        swap = pltpu.make_async_remote_copy(
            src_ref=x_ref.at[p, :, pl.ds(give, width)],
            dst_ref=dst,
            send_sem=send_sem.at[12 + p],
            recv_sem=recv_sem.at[12 + p],
            device_id=partner,
            device_id_type=MESH,
        )
        swap.start()
        moves.append((local, swap, unit.at[1 - core, :, pl.ds(p * width, width)], p))
    for local, swap, dst, p in moves:
        local.wait()
        swap.wait_send()
        pltpu.make_async_remote_copy(
            src_ref=x_ref.at[p, :, pl.ds(give, width)],
            dst_ref=dst,
            send_sem=send_sem.at[12 + p],
            recv_sem=recv_sem.at[12 + p],
            device_id=partner,
            device_id_type=MESH,
        ).wait_recv()

    def ring(ref, slot, axis, delta):
        return pltpu.make_async_remote_copy(
            src_ref=ref,
            dst_ref=ref,
            send_sem=ring_send.at[slot],
            recv_sem=ring_recv.at[slot],
            device_id=device(axis, delta),
            device_id_type=MESH,
        )

    def run(order):
        held = ()
        sent = []
        pending = []
        for stage, axis in enumerate(order):
            base = stage * 10
            if stage == 0:
                parts = [None]
            else:
                prev = order[stage - 1]
                parts = [(prev, 0), (prev, -1), (prev, 1), (prev, 2)]

            def send_part(i):
                for j, delta in enumerate((1, -1)):
                    copy = ring(view(held, pin=parts[i]), base + 4 * j + i, axis, delta)
                    copy.start()
                    sent.append(copy)

            for i in range(max(1, len(parts) - 1)):
                send_part(i)
            if stage == 0:
                build()
            if stage == 1:
                acc[...] = jnp.zeros_like(acc)
            for copy in pending:
                copy.wait_recv()
            if stage > 0:
                send_part(3)
            if stage == 2:
                lend.wait_send()
                pltpu.make_async_remote_copy(
                    src_ref=own_ref,
                    dst_ref=partner_ref,
                    send_sem=send_sem.at[14],
                    recv_sem=recv_sem.at[14],
                    device_id=partner,
                    device_id_type=MESH,
                ).wait_recv()
                compute_block(held)
            for i in range(len(parts)):
                for j, delta in enumerate((1, -1)):
                    ring(view(held, axis, -delta, pin=parts[i]), base + 4 * j + i, axis, -delta).wait_recv()
            fwd = [
                ring(view(held, axis, 1, 0), base + 8, axis, -1),
                ring(view(held, axis, -1, 1), base + 9, axis, 1),
            ]
            for copy in fwd:
                copy.start()
            sent.extend(fwd)
            if stage == 2:
                compute_block(held, axis, -1)
                compute_block(held, axis, 1)
            pending = [
                ring(view(held, axis, 2, 0), base + 8, axis, 1),
                ring(view(held, axis, 2, 1), base + 9, axis, -1),
            ]
            if stage == 0:
                lend.start()
            held = held + (axis,)
        for copy in pending:
            copy.wait_recv()
        for copy in sent:
            copy.wait_send()
        compute_block(held[:-1], order[-1], 2)

    for index, order in enumerate(ORDERS):
        @pl.when(core == index)
        def _():
            run(order)

    lent[...] = acc[1].astype(lent.dtype)
    give_back = pltpu.make_async_remote_copy(
        src_ref=lent,
        dst_ref=back,
        send_sem=send_sem.at[15],
        recv_sem=recv_sem.at[15],
        device_id=partner,
        device_id_type=MESH,
    )
    give_back.start()
    rows = orb_out.shape[0]
    blocks = acc.shape[2]

    def store(values, h):
        for a, out in enumerate((orb_out, app_out)):
            for c in range(blocks):
                lane = pl.multiple_of(c * 2 * width + h * width, width)
                part = [values[p, c, pl.ds(a * rows, rows), :].astype(out.dtype) for p in range(2)]
                out[:, :, pl.ds(lane, width)] = jnp.stack(part, axis=1)

    store(acc.at[0], core)
    give_back.wait_send()
    pltpu.make_async_remote_copy(
        src_ref=lent,
        dst_ref=back,
        send_sem=send_sem.at[15],
        recv_sem=recv_sem.at[15],
        device_id=partner,
        device_id_type=MESH,
    ).wait_recv()
    store(back, 1 - core)


def ring_rotate(ritz, orbitals, applied_orbitals):
    rows, band2 = 2 * orbitals.shape[0], 2 * orbitals.shape[2]
    own = orbitals
    units = (RING, 2, RING, 2, 2, ritz.shape[1], ritz.shape[2])
    width = ritz.shape[2] // 2
    out = jax.ShapeDtypeStruct((rows // 2, 2, band2 // 2), jnp.bfloat16)
    vmem = pl.BlockSpec(memory_space=pltpu.VMEM)
    flops = 2 * 2 * rows * band2 * 2 * ritz.shape[2] * 2 * RING
    return pl.pallas_call(
        ring_rotate_kernel,
        out_shape=[out, out],
        in_specs=[pl.BlockSpec(memory_space=pl.ANY), vmem, vmem],
        out_specs=[vmem, vmem],
        scratch_shapes=[
            pltpu.VMEM(units, ritz.dtype),
            pltpu.VMEM((rows, band2), own.dtype),
            pltpu.VMEM((rows, band2), own.dtype),
            pltpu.VMEM((2, 2, 2 * RING, rows, width), jnp.float32),
            pltpu.VMEM((2, 2 * RING, rows, width), jnp.bfloat16),
            pltpu.VMEM((2, 2 * RING, rows, width), jnp.bfloat16),
            pltpu.SemaphoreType.DMA((16,)),
            pltpu.SemaphoreType.DMA((16,)),
            pltpu.SemaphoreType.DMA((2,)),
            pltpu.SemaphoreType.DMA((30,)),
            pltpu.SemaphoreType.DMA((30,)),
        ],
        compiler_params=pltpu.CompilerParams(
            collective_id=0, has_side_effects=True, vmem_limit_bytes=60 * 1024 * 1024
        ),
        cost_estimate=pl.CostEstimate(flops=flops, transcendentals=0, bytes_accessed=8 * own.size * 2),
    )(ritz, orbitals, applied_orbitals)


def rotate_kernel(own_ref, partner_ref, ritz_ref, own_out, partner_out):
    band = own_ref.shape[1] // 2
    width = own_out.shape[-1]
    weights = ritz_ref[...].reshape(-1, 2 * width)
    for src, dst in ((own_ref, own_out), (partner_ref, partner_out)):
        first = jnp.dot(src[:, :band], weights, preferred_element_type=jnp.float32)
        second = jnp.dot(src[:, band:], weights, preferred_element_type=jnp.float32)
        real = first[:, :width] - second[:, width:]
        imag = first[:, width:] + second[:, :width]
        dst[0] = real.astype(dst.dtype)
        dst[1] = imag.astype(dst.dtype)


def rotate(own, partner, gathered):
    rows, band2 = own.shape
    rc, cb, co, k, width2 = gathered.shape
    width = width2 // 2
    x_spec = pl.BlockSpec((rows, band2), lambda c: (0, 0))
    g_spec = pl.BlockSpec((rc, None, co, k, width2), lambda c: (0, c, 0, 0, 0))
    o_spec = pl.BlockSpec((2, None, rows, width), lambda c: (0, c, 0, 0))
    out = jax.ShapeDtypeStruct((2, cb, rows, width), jnp.bfloat16)
    flops = 2 * 2 * rows * band2 * width2
    moved = 2 * own.size * 2 + gathered.size * 2 + 2 * own.size * 2
    return pl.pallas_call(
        rotate_kernel,
        grid=(cb,),
        in_specs=[x_spec, x_spec, g_spec],
        out_specs=[o_spec, o_spec],
        out_shape=[out, out],
        compiler_params=pltpu.CompilerParams(vmem_limit_bytes=48 * 1024 * 1024),
        cost_estimate=pl.CostEstimate(flops=flops, transcendentals=0, bytes_accessed=moved),
    )(own, partner, gathered)


def shards(rc_count, col_count, orbitals, applied_orbitals, ritz_matrix):
    me = lax.axis_index("core")
    rows = orbitals.shape[0]
    band_count = orbitals.shape[2]

    orb_out, app_out = ring_rotate(ritz_matrix, orbitals, applied_orbitals)
    return orb_out, app_out


def solution(mesh):
    devices = mesh.devices
    split = Mesh(
        devices.reshape(devices.shape[0] // 2, 2, devices.shape[1]), ("rc", "core", "col")
    )
    flat = ("rc", "core", "col")
    in_specs = (P(flat, None, None), P(flat, None, None), P(None, ("rc", "core"), "col"))
    out_specs = (P(flat, None, None), P(flat, None, None))
    body = functools.partial(shards, devices.shape[0] // 2, devices.shape[1])
    return jax.shard_map(body, mesh=split, in_specs=in_specs, out_specs=out_specs, check_vma=False)
```

```python
import functools

import jax
import jax.numpy as jnp
from jax import lax
from jax.experimental import pallas as pl
from jax.experimental.pallas import tpu as pltpu
from jax.sharding import Mesh
from jax.sharding import PartitionSpec as P

SWAP = [(0, 1), (1, 0)]
AXES = ("rc", "core", "col")
MESH = pl.DeviceIdType.MESH


RING = 4
ORDERS = (("x", "y", "z"), ("y", "z", "x"))
DIMS = ("y", "z_hi", "x", "z_lo")


def ring_rotate_kernel(
    x_ref, orb_ref, app_ref, orb_out, app_out, g_ref, own_ref, partner_ref, acc, lent, back, send_sem, recv_sem,
    local_sem, ring_send, ring_recv,
):
    rc = lax.axis_index("rc")
    core = lax.axis_index("core")
    col = lax.axis_index("col")
    here = {"y": rc // 2, "z": (rc % 2) * 2 + col % 2, "x": col // 2}

    def device(axis, delta):
        at = dict(here)
        at[axis] = lax.rem(at[axis] + delta + RING, RING)
        return (at["y"] * 2 + at["z"] // 2, core, at["x"] * 2 + at["z"] % 2)

    def view(held, axis=None, delta=0, half=None, pin=None):
        at = dict(here)
        pins = {} if pin is None else {pin[0]: pin[1]}
        if axis is not None:
            pins[axis] = delta
        for a, d in pins.items():
            at[a] = lax.rem(at[a] + d + RING, RING)
        held = tuple(h for h in held if h not in pins)
        index = []
        split = half is not None
        for dim in DIMS:
            phys = "z" if dim.startswith("z") else dim
            if phys in held:
                size = 2 if phys == "z" else RING
                if split:
                    index.append(pl.ds(half * (size // 2), size // 2))
                    split = False
                else:
                    index.append(slice(None))
            elif dim == "z_hi":
                index.append(at["z"] // 2)
            elif dim == "z_lo":
                index.append(at["z"] % 2)
            else:
                index.append(at[phys])
        if split:
            index.append(pl.ds(half, 1))
        return g_ref.at[tuple(index)]

    def remote(src, dst, slot, axis, delta):
        return pltpu.make_async_remote_copy(
            src_ref=src,
            dst_ref=dst,
            send_sem=send_sem.at[slot],
            recv_sem=recv_sem.at[slot],
            device_id=device(axis, delta),
            device_id_type=MESH,
        )

    partner = (rc, 1 - core, col)
    barrier = pltpu.get_barrier_semaphore()
    for axis in ("x", "y", "z"):
        for delta in (1, -1):
            pl.semaphore_signal(barrier, 1, device_id=device(axis, delta), device_id_type=MESH)
    pl.semaphore_signal(barrier, 1, device_id=partner, device_id_type=MESH)
    pl.semaphore_wait(barrier, 7)

    lend = pltpu.make_async_remote_copy(
        src_ref=own_ref,
        dst_ref=partner_ref,
        send_sem=send_sem.at[14],
        recv_sem=recv_sem.at[14],
        device_id=partner,
        device_id_type=MESH,
    )

    def build():
        count = orb_ref.shape[0]
        step = 32
        for a, raw in enumerate((orb_ref, app_ref)):
            for n in range(0, count, step):
                v = raw[pl.ds(n, step)]
                for q in range(2):
                    own_ref[pl.ds(a * count + n, step), pl.ds(q * band, band)] = v[:, q, :]

    band = own_ref.shape[1] // 2
    width = x_ref.shape[2] // 2
    depth = 2 * x_ref.shape[1]

    def compute(y, z, x):
        w = g_ref[y, z // 2, x, z % 2].reshape(depth, 2 * width)
        koff = pl.multiple_of((y * 2 + z // 2) * depth, depth)
        block = x * 2 + z % 2
        for src, rows in enumerate((own_ref, partner_ref)):
            first = jnp.dot(rows[:, pl.ds(koff, depth)], w, preferred_element_type=jnp.float32)
            second = jnp.dot(rows[:, pl.ds(band + koff, depth)], w, preferred_element_type=jnp.float32)
            acc[src, 0, block] += first[:, :width] - second[:, width:]
            acc[src, 1, block] += first[:, width:] + second[:, :width]

    def compute_block(held, axis=None, delta=0):
        at = dict(here)
        if axis is not None:
            at[axis] = lax.rem(at[axis] + delta + RING, RING)
        full = [d for d in ("y", "z", "x") if d in held]

        def body(i, carry):
            c = dict(at)
            rest = i
            for d in full:
                c[d] = rest % RING
                rest = rest // RING
            compute(c["y"], c["z"], c["x"])
            return carry

        lax.fori_loop(0, RING ** len(full), body, 0)

    unit = view(())
    keep = pl.multiple_of(core * width, width)
    give = pl.multiple_of((1 - core) * width, width)
    moves = []
    for p in range(2):
        dst = unit.at[core, :, pl.ds(p * width, width)]
        local = pltpu.make_async_copy(x_ref.at[p, :, pl.ds(keep, width)], dst, local_sem.at[p])
        local.start()
        swap = pltpu.make_async_remote_copy(
            src_ref=x_ref.at[p, :, pl.ds(give, width)],
            dst_ref=dst,
            send_sem=send_sem.at[12 + p],
            recv_sem=recv_sem.at[12 + p],
            device_id=partner,
            device_id_type=MESH,
        )
        swap.start()
        moves.append((local, swap, unit.at[1 - core, :, pl.ds(p * width, width)], p))
    for local, swap, dst, p in moves:
        local.wait()
        swap.wait_send()
        pltpu.make_async_remote_copy(
            src_ref=x_ref.at[p, :, pl.ds(give, width)],
            dst_ref=dst,
            send_sem=send_sem.at[12 + p],
            recv_sem=recv_sem.at[12 + p],
            device_id=partner,
            device_id_type=MESH,
        ).wait_recv()

    def ring(ref, slot, axis, delta):
        return pltpu.make_async_remote_copy(
            src_ref=ref,
            dst_ref=ref,
            send_sem=ring_send.at[slot],
            recv_sem=ring_recv.at[slot],
            device_id=device(axis, delta),
            device_id_type=MESH,
        )

    def run(order):
        held = ()
        sent = []
        pending = []
        for stage, axis in enumerate(order):
            base = stage * 10
            if stage == 0:
                parts = [None]
            else:
                prev = order[stage - 1]
                parts = [(prev, 0), (prev, -1), (prev, 1), (prev, 2)]

            def send_part(i):
                for j, delta in enumerate((1, -1)):
                    copy = ring(view(held, pin=parts[i]), base + 4 * j + i, axis, delta)
                    copy.start()
                    sent.append(copy)

            for i in range(max(1, len(parts) - 1)):
                send_part(i)
            if stage == 0:
                build()
            if stage == 1:
                acc[...] = jnp.zeros_like(acc)
            for copy in pending:
                copy.wait_recv()
            if stage > 0:
                send_part(3)
            if stage == 2:
                lend.wait_send()
                pltpu.make_async_remote_copy(
                    src_ref=own_ref,
                    dst_ref=partner_ref,
                    send_sem=send_sem.at[14],
                    recv_sem=recv_sem.at[14],
                    device_id=partner,
                    device_id_type=MESH,
                ).wait_recv()
                compute_block(held)
            fwd_base = 30 + stage * 8
            for i in range(len(parts)):
                for j, delta in enumerate((1, -1)):
                    ring(view(held, axis, -delta, pin=parts[i]), base + 4 * j + i, axis, -delta).wait_recv()
                    half = 0 if delta == -1 else 1
                    copy = ring(view(held, axis, -delta, half, parts[i]), fwd_base + 2 * i + j, axis, delta)
                    copy.start()
                    sent.append(copy)
            if stage == 2:
                compute_block(held, axis, -1)
                compute_block(held, axis, 1)
            pending = []
            for i in range(len(parts)):
                for j, delta in enumerate((1, -1)):
                    half = 0 if delta == -1 else 1
                    pending.append(ring(view(held, axis, 2, half, parts[i]), fwd_base + 2 * i + j, axis, -delta))
            if stage == 0:
                lend.start()
            held = held + (axis,)
        for copy in pending:
            copy.wait_recv()
        for copy in sent:
            copy.wait_send()
        compute_block(held[:-1], order[-1], 2)

    for index, order in enumerate(ORDERS):
        @pl.when(core == index)
        def _():
            run(order)

    lent[...] = acc[1].astype(lent.dtype)
    give_back = pltpu.make_async_remote_copy(
        src_ref=lent,
        dst_ref=back,
        send_sem=send_sem.at[15],
        recv_sem=recv_sem.at[15],
        device_id=partner,
        device_id_type=MESH,
    )
    give_back.start()
    rows = orb_out.shape[0]
    blocks = acc.shape[2]

    def store(values, h):
        for a, out in enumerate((orb_out, app_out)):
            for c in range(blocks):
                lane = pl.multiple_of(c * 2 * width + h * width, width)
                part = [values[p, c, pl.ds(a * rows, rows), :].astype(out.dtype) for p in range(2)]
                out[:, :, pl.ds(lane, width)] = jnp.stack(part, axis=1)

    store(acc.at[0], core)
    give_back.wait_send()
    pltpu.make_async_remote_copy(
        src_ref=lent,
        dst_ref=back,
        send_sem=send_sem.at[15],
        recv_sem=recv_sem.at[15],
        device_id=partner,
        device_id_type=MESH,
    ).wait_recv()
    store(back, 1 - core)


def ring_rotate(ritz, orbitals, applied_orbitals):
    rows, band2 = 2 * orbitals.shape[0], 2 * orbitals.shape[2]
    own = orbitals
    units = (RING, 2, RING, 2, 2, ritz.shape[1], ritz.shape[2])
    width = ritz.shape[2] // 2
    out = jax.ShapeDtypeStruct((rows // 2, 2, band2 // 2), jnp.bfloat16)
    vmem = pl.BlockSpec(memory_space=pltpu.VMEM)
    flops = 2 * 2 * rows * band2 * 2 * ritz.shape[2] * 2 * RING
    return pl.pallas_call(
        ring_rotate_kernel,
        out_shape=[out, out],
        in_specs=[pl.BlockSpec(memory_space=pl.ANY), vmem, vmem],
        out_specs=[vmem, vmem],
        scratch_shapes=[
            pltpu.VMEM(units, ritz.dtype),
            pltpu.VMEM((rows, band2), own.dtype),
            pltpu.VMEM((rows, band2), own.dtype),
            pltpu.VMEM((2, 2, 2 * RING, rows, width), jnp.float32),
            pltpu.VMEM((2, 2 * RING, rows, width), jnp.bfloat16),
            pltpu.VMEM((2, 2 * RING, rows, width), jnp.bfloat16),
            pltpu.SemaphoreType.DMA((16,)),
            pltpu.SemaphoreType.DMA((16,)),
            pltpu.SemaphoreType.DMA((2,)),
            pltpu.SemaphoreType.DMA((54,)),
            pltpu.SemaphoreType.DMA((54,)),
        ],
        compiler_params=pltpu.CompilerParams(
            collective_id=0, has_side_effects=True, vmem_limit_bytes=60 * 1024 * 1024
        ),
        cost_estimate=pl.CostEstimate(flops=flops, transcendentals=0, bytes_accessed=8 * own.size * 2),
    )(ritz, orbitals, applied_orbitals)


def rotate_kernel(own_ref, partner_ref, ritz_ref, own_out, partner_out):
    band = own_ref.shape[1] // 2
    width = own_out.shape[-1]
    weights = ritz_ref[...].reshape(-1, 2 * width)
    for src, dst in ((own_ref, own_out), (partner_ref, partner_out)):
        first = jnp.dot(src[:, :band], weights, preferred_element_type=jnp.float32)
        second = jnp.dot(src[:, band:], weights, preferred_element_type=jnp.float32)
        real = first[:, :width] - second[:, width:]
        imag = first[:, width:] + second[:, :width]
        dst[0] = real.astype(dst.dtype)
        dst[1] = imag.astype(dst.dtype)


def rotate(own, partner, gathered):
    rows, band2 = own.shape
    rc, cb, co, k, width2 = gathered.shape
    width = width2 // 2
    x_spec = pl.BlockSpec((rows, band2), lambda c: (0, 0))
    g_spec = pl.BlockSpec((rc, None, co, k, width2), lambda c: (0, c, 0, 0, 0))
    o_spec = pl.BlockSpec((2, None, rows, width), lambda c: (0, c, 0, 0))
    out = jax.ShapeDtypeStruct((2, cb, rows, width), jnp.bfloat16)
    flops = 2 * 2 * rows * band2 * width2
    moved = 2 * own.size * 2 + gathered.size * 2 + 2 * own.size * 2
    return pl.pallas_call(
        rotate_kernel,
        grid=(cb,),
        in_specs=[x_spec, x_spec, g_spec],
        out_specs=[o_spec, o_spec],
        out_shape=[out, out],
        compiler_params=pltpu.CompilerParams(vmem_limit_bytes=48 * 1024 * 1024),
        cost_estimate=pl.CostEstimate(flops=flops, transcendentals=0, bytes_accessed=moved),
    )(own, partner, gathered)


def shards(rc_count, col_count, orbitals, applied_orbitals, ritz_matrix):
    me = lax.axis_index("core")
    rows = orbitals.shape[0]
    band_count = orbitals.shape[2]

    orb_out, app_out = ring_rotate(ritz_matrix, orbitals, applied_orbitals)
    return orb_out, app_out


def solution(mesh):
    devices = mesh.devices
    split = Mesh(
        devices.reshape(devices.shape[0] // 2, 2, devices.shape[1]), ("rc", "core", "col")
    )
    flat = ("rc", "core", "col")
    in_specs = (P(flat, None, None), P(flat, None, None), P(None, ("rc", "core"), "col"))
    out_specs = (P(flat, None, None), P(flat, None, None))
    body = functools.partial(shards, devices.shape[0] // 2, devices.shape[1])
    return jax.shard_map(body, mesh=split, in_specs=in_specs, out_specs=out_specs, check_vma=False)
```

```python
import functools

import jax
import jax.numpy as jnp
from jax import lax
from jax.experimental import pallas as pl
from jax.experimental.pallas import tpu as pltpu
from jax.sharding import Mesh
from jax.sharding import PartitionSpec as P

SWAP = [(0, 1), (1, 0)]
AXES = ("rc", "core", "col")
MESH = pl.DeviceIdType.MESH


RING = 4
ORDERS = (("x", "y", "z"), ("y", "z", "x"))
DIMS = ("y", "z_hi", "x", "z_lo")


def ring_rotate_kernel(
    x_ref, orb_ref, app_ref, orb_out, app_out, g_ref, own_ref, partner_ref, acc, lent, back, send_sem, recv_sem,
    local_sem, ring_send, ring_recv,
):
    rc = lax.axis_index("rc")
    core = lax.axis_index("core")
    col = lax.axis_index("col")
    here = {"y": rc // 2, "z": (rc % 2) * 2 + col % 2, "x": col // 2}

    def device(axis, delta):
        at = dict(here)
        at[axis] = lax.rem(at[axis] + delta + RING, RING)
        return (at["y"] * 2 + at["z"] // 2, core, at["x"] * 2 + at["z"] % 2)

    def view(held, axis=None, delta=0, half=None, pin=None):
        at = dict(here)
        pins = {} if pin is None else {pin[0]: pin[1]}
        if axis is not None:
            pins[axis] = delta
        for a, d in pins.items():
            at[a] = lax.rem(at[a] + d + RING, RING)
        held = tuple(h for h in held if h not in pins)
        index = []
        split = half is not None
        for dim in DIMS:
            phys = "z" if dim.startswith("z") else dim
            if phys in held:
                size = 2 if phys == "z" else RING
                if split:
                    index.append(pl.ds(half * (size // 2), size // 2))
                    split = False
                else:
                    index.append(slice(None))
            elif dim == "z_hi":
                index.append(at["z"] // 2)
            elif dim == "z_lo":
                index.append(at["z"] % 2)
            else:
                index.append(at[phys])
        if split:
            index.append(pl.ds(half, 1))
        return g_ref.at[tuple(index)]

    def remote(src, dst, slot, axis, delta):
        return pltpu.make_async_remote_copy(
            src_ref=src,
            dst_ref=dst,
            send_sem=send_sem.at[slot],
            recv_sem=recv_sem.at[slot],
            device_id=device(axis, delta),
            device_id_type=MESH,
        )

    partner = (rc, 1 - core, col)
    barrier = pltpu.get_barrier_semaphore()
    for axis in ("x", "y", "z"):
        for delta in (1, -1):
            pl.semaphore_signal(barrier, 1, device_id=device(axis, delta), device_id_type=MESH)
    pl.semaphore_signal(barrier, 1, device_id=partner, device_id_type=MESH)
    pl.semaphore_wait(barrier, 7)

    lend = pltpu.make_async_remote_copy(
        src_ref=own_ref,
        dst_ref=partner_ref,
        send_sem=send_sem.at[14],
        recv_sem=recv_sem.at[14],
        device_id=partner,
        device_id_type=MESH,
    )

    def build():
        count = orb_ref.shape[0]
        step = 32
        for a, raw in enumerate((orb_ref, app_ref)):
            for n in range(0, count, step):
                v = raw[pl.ds(n, step)]
                for q in range(2):
                    own_ref[pl.ds(a * count + n, step), pl.ds(q * band, band)] = v[:, q, :]

    band = own_ref.shape[1] // 2
    width = x_ref.shape[2] // 2
    depth = 2 * x_ref.shape[1]

    def compute(y, z, x):
        w = g_ref[y, z // 2, x, z % 2].reshape(depth, 2 * width)
        koff = pl.multiple_of((y * 2 + z // 2) * depth, depth)
        block = x * 2 + z % 2
        for src, rows in enumerate((own_ref, partner_ref)):
            first = jnp.dot(rows[:, pl.ds(koff, depth)], w, preferred_element_type=jnp.float32)
            second = jnp.dot(rows[:, pl.ds(band + koff, depth)], w, preferred_element_type=jnp.float32)
            acc[src, 0, block] += first[:, :width] - second[:, width:]
            acc[src, 1, block] += first[:, width:] + second[:, :width]

    def compute_block(held, axis=None, delta=0, pin=None):
        at = dict(here)
        pins = {} if pin is None else {pin[0]: pin[1]}
        if axis is not None:
            pins[axis] = delta
        for a, d in pins.items():
            at[a] = lax.rem(at[a] + d + RING, RING)
        full = [d for d in ("y", "z", "x") if d in held and d not in pins]

        def body(i, carry):
            c = dict(at)
            rest = i
            for d in full:
                c[d] = rest % RING
                rest = rest // RING
            compute(c["y"], c["z"], c["x"])
            return carry

        lax.fori_loop(0, RING ** len(full), body, 0)

    unit = view(())
    keep = pl.multiple_of(core * width, width)
    give = pl.multiple_of((1 - core) * width, width)
    moves = []
    for p in range(2):
        dst = unit.at[core, :, pl.ds(p * width, width)]
        local = pltpu.make_async_copy(x_ref.at[p, :, pl.ds(keep, width)], dst, local_sem.at[p])
        local.start()
        swap = pltpu.make_async_remote_copy(
            src_ref=x_ref.at[p, :, pl.ds(give, width)],
            dst_ref=dst,
            send_sem=send_sem.at[12 + p],
            recv_sem=recv_sem.at[12 + p],
            device_id=partner,
            device_id_type=MESH,
        )
        swap.start()
        moves.append((local, swap, unit.at[1 - core, :, pl.ds(p * width, width)], p))
    for local, swap, dst, p in moves:
        local.wait()
        swap.wait_send()
        pltpu.make_async_remote_copy(
            src_ref=x_ref.at[p, :, pl.ds(give, width)],
            dst_ref=dst,
            send_sem=send_sem.at[12 + p],
            recv_sem=recv_sem.at[12 + p],
            device_id=partner,
            device_id_type=MESH,
        ).wait_recv()

    def ring(ref, slot, axis, delta):
        return pltpu.make_async_remote_copy(
            src_ref=ref,
            dst_ref=ref,
            send_sem=ring_send.at[slot],
            recv_sem=ring_recv.at[slot],
            device_id=device(axis, delta),
            device_id_type=MESH,
        )

    def run(order):
        held = ()
        sent = []
        pending = []
        for stage, axis in enumerate(order):
            base = stage * 10
            if stage == 0:
                parts = [None]
            else:
                prev = order[stage - 1]
                parts = [(prev, 0), (prev, -1), (prev, 1), (prev, 2)]

            def send_part(i):
                for j, delta in enumerate((1, -1)):
                    copy = ring(view(held, pin=parts[i]), base + 4 * j + i, axis, delta)
                    copy.start()
                    sent.append(copy)

            for i in range(max(1, len(parts) - 1)):
                send_part(i)
            if stage == 0:
                build()
            if stage == 1:
                acc[...] = jnp.zeros_like(acc)
            for copy in pending:
                copy.wait_recv()
            if stage > 0:
                send_part(3)
            if stage == 2:
                lend.wait_send()
                pltpu.make_async_remote_copy(
                    src_ref=own_ref,
                    dst_ref=partner_ref,
                    send_sem=send_sem.at[14],
                    recv_sem=recv_sem.at[14],
                    device_id=partner,
                    device_id_type=MESH,
                ).wait_recv()
                compute_block(held)
            fwd_base = 30 + stage * 8
            for i in range(len(parts)):
                for j, delta in enumerate((1, -1)):
                    ring(view(held, axis, -delta, pin=parts[i]), base + 4 * j + i, axis, -delta).wait_recv()
                    half = 0 if delta == -1 else 1
                    copy = ring(view(held, axis, -delta, half, parts[i]), fwd_base + 2 * i + j, axis, delta)
                    copy.start()
                    sent.append(copy)
            if stage == 2:
                compute_block(held, axis, -1)
                compute_block(held, axis, 1)
            pending = []
            for i in range(len(parts)):
                for j, delta in enumerate((1, -1)):
                    half = 0 if delta == -1 else 1
                    pending.append(ring(view(held, axis, 2, half, parts[i]), fwd_base + 2 * i + j, axis, -delta))
            if stage == 0:
                lend.start()
            held = held + (axis,)
        for i in range(len(parts)):
            pending[2 * i].wait_recv()
            pending[2 * i + 1].wait_recv()
            compute_block(held[:-1], order[-1], 2, parts[i])
        for copy in sent:
            copy.wait_send()

    for index, order in enumerate(ORDERS):
        @pl.when(core == index)
        def _():
            run(order)

    lent[...] = acc[1].astype(lent.dtype)
    give_back = pltpu.make_async_remote_copy(
        src_ref=lent,
        dst_ref=back,
        send_sem=send_sem.at[15],
        recv_sem=recv_sem.at[15],
        device_id=partner,
        device_id_type=MESH,
    )
    give_back.start()
    rows = orb_out.shape[0]
    blocks = acc.shape[2]

    def store(values, h):
        for a, out in enumerate((orb_out, app_out)):
            for c in range(blocks):
                lane = pl.multiple_of(c * 2 * width + h * width, width)
                part = [values[p, c, pl.ds(a * rows, rows), :].astype(out.dtype) for p in range(2)]
                out[:, :, pl.ds(lane, width)] = jnp.stack(part, axis=1)

    store(acc.at[0], core)
    give_back.wait_send()
    pltpu.make_async_remote_copy(
        src_ref=lent,
        dst_ref=back,
        send_sem=send_sem.at[15],
        recv_sem=recv_sem.at[15],
        device_id=partner,
        device_id_type=MESH,
    ).wait_recv()
    store(back, 1 - core)


def ring_rotate(ritz, orbitals, applied_orbitals):
    rows, band2 = 2 * orbitals.shape[0], 2 * orbitals.shape[2]
    own = orbitals
    units = (RING, 2, RING, 2, 2, ritz.shape[1], ritz.shape[2])
    width = ritz.shape[2] // 2
    out = jax.ShapeDtypeStruct((rows // 2, 2, band2 // 2), jnp.bfloat16)
    vmem = pl.BlockSpec(memory_space=pltpu.VMEM)
    flops = 2 * 2 * rows * band2 * 2 * ritz.shape[2] * 2 * RING
    return pl.pallas_call(
        ring_rotate_kernel,
        out_shape=[out, out],
        in_specs=[pl.BlockSpec(memory_space=pl.ANY), vmem, vmem],
        out_specs=[vmem, vmem],
        scratch_shapes=[
            pltpu.VMEM(units, ritz.dtype),
            pltpu.VMEM((rows, band2), own.dtype),
            pltpu.VMEM((rows, band2), own.dtype),
            pltpu.VMEM((2, 2, 2 * RING, rows, width), jnp.float32),
            pltpu.VMEM((2, 2 * RING, rows, width), jnp.bfloat16),
            pltpu.VMEM((2, 2 * RING, rows, width), jnp.bfloat16),
            pltpu.SemaphoreType.DMA((16,)),
            pltpu.SemaphoreType.DMA((16,)),
            pltpu.SemaphoreType.DMA((2,)),
            pltpu.SemaphoreType.DMA((54,)),
            pltpu.SemaphoreType.DMA((54,)),
        ],
        compiler_params=pltpu.CompilerParams(
            collective_id=0, has_side_effects=True, vmem_limit_bytes=60 * 1024 * 1024
        ),
        cost_estimate=pl.CostEstimate(flops=flops, transcendentals=0, bytes_accessed=8 * own.size * 2),
    )(ritz, orbitals, applied_orbitals)


def rotate_kernel(own_ref, partner_ref, ritz_ref, own_out, partner_out):
    band = own_ref.shape[1] // 2
    width = own_out.shape[-1]
    weights = ritz_ref[...].reshape(-1, 2 * width)
    for src, dst in ((own_ref, own_out), (partner_ref, partner_out)):
        first = jnp.dot(src[:, :band], weights, preferred_element_type=jnp.float32)
        second = jnp.dot(src[:, band:], weights, preferred_element_type=jnp.float32)
        real = first[:, :width] - second[:, width:]
        imag = first[:, width:] + second[:, :width]
        dst[0] = real.astype(dst.dtype)
        dst[1] = imag.astype(dst.dtype)


def rotate(own, partner, gathered):
    rows, band2 = own.shape
    rc, cb, co, k, width2 = gathered.shape
    width = width2 // 2
    x_spec = pl.BlockSpec((rows, band2), lambda c: (0, 0))
    g_spec = pl.BlockSpec((rc, None, co, k, width2), lambda c: (0, c, 0, 0, 0))
    o_spec = pl.BlockSpec((2, None, rows, width), lambda c: (0, c, 0, 0))
    out = jax.ShapeDtypeStruct((2, cb, rows, width), jnp.bfloat16)
    flops = 2 * 2 * rows * band2 * width2
    moved = 2 * own.size * 2 + gathered.size * 2 + 2 * own.size * 2
    return pl.pallas_call(
        rotate_kernel,
        grid=(cb,),
        in_specs=[x_spec, x_spec, g_spec],
        out_specs=[o_spec, o_spec],
        out_shape=[out, out],
        compiler_params=pltpu.CompilerParams(vmem_limit_bytes=48 * 1024 * 1024),
        cost_estimate=pl.CostEstimate(flops=flops, transcendentals=0, bytes_accessed=moved),
    )(own, partner, gathered)


def shards(rc_count, col_count, orbitals, applied_orbitals, ritz_matrix):
    me = lax.axis_index("core")
    rows = orbitals.shape[0]
    band_count = orbitals.shape[2]

    orb_out, app_out = ring_rotate(ritz_matrix, orbitals, applied_orbitals)
    return orb_out, app_out


def solution(mesh):
    devices = mesh.devices
    split = Mesh(
        devices.reshape(devices.shape[0] // 2, 2, devices.shape[1]), ("rc", "core", "col")
    )
    flat = ("rc", "core", "col")
    in_specs = (P(flat, None, None), P(flat, None, None), P(None, ("rc", "core"), "col"))
    out_specs = (P(flat, None, None), P(flat, None, None))
    body = functools.partial(shards, devices.shape[0] // 2, devices.shape[1])
    return jax.shard_map(body, mesh=split, in_specs=in_specs, out_specs=out_specs, check_vma=False)
```

```python
import functools

import jax
import jax.numpy as jnp
from jax import lax
from jax.experimental import pallas as pl
from jax.experimental.pallas import tpu as pltpu
from jax.sharding import Mesh
from jax.sharding import PartitionSpec as P

SWAP = [(0, 1), (1, 0)]
AXES = ("rc", "core", "col")
MESH = pl.DeviceIdType.MESH


RING = 4
ORDERS = (("x", "y", "z"), ("y", "z", "x"))
DIMS = ("y", "z_hi", "x", "z_lo")


def ring_rotate_kernel(
    x_ref, orb_ref, app_ref, orb_out, app_out, g_ref, own_ref, partner_ref, acc, lent, back, send_sem, recv_sem,
    local_sem, ring_send, ring_recv,
):
    rc = lax.axis_index("rc")
    core = lax.axis_index("core")
    col = lax.axis_index("col")
    here = {"y": rc // 2, "z": (rc % 2) * 2 + col % 2, "x": col // 2}

    def device(axis, delta):
        at = dict(here)
        at[axis] = lax.rem(at[axis] + delta + RING, RING)
        return (at["y"] * 2 + at["z"] // 2, core, at["x"] * 2 + at["z"] % 2)

    def view(held, axis=None, delta=0, half=None, pin=None):
        at = dict(here)
        pins = {} if pin is None else {pin[0]: pin[1]}
        if axis is not None:
            pins[axis] = delta
        for a, d in pins.items():
            at[a] = lax.rem(at[a] + d + RING, RING)
        held = tuple(h for h in held if h not in pins)
        index = []
        split = half is not None
        for dim in DIMS:
            phys = "z" if dim.startswith("z") else dim
            if phys in held:
                size = 2 if phys == "z" else RING
                if split:
                    index.append(pl.ds(half * (size // 2), size // 2))
                    split = False
                else:
                    index.append(slice(None))
            elif dim == "z_hi":
                index.append(at["z"] // 2)
            elif dim == "z_lo":
                index.append(at["z"] % 2)
            else:
                index.append(at[phys])
        if split:
            index.append(pl.ds(half, 1))
        return g_ref.at[tuple(index)]

    def remote(src, dst, slot, axis, delta):
        return pltpu.make_async_remote_copy(
            src_ref=src,
            dst_ref=dst,
            send_sem=send_sem.at[slot],
            recv_sem=recv_sem.at[slot],
            device_id=device(axis, delta),
            device_id_type=MESH,
        )

    partner = (rc, 1 - core, col)
    barrier = pltpu.get_barrier_semaphore()
    for axis in ("x", "y", "z"):
        for delta in (1, -1):
            pl.semaphore_signal(barrier, 1, device_id=device(axis, delta), device_id_type=MESH)
    pl.semaphore_signal(barrier, 1, device_id=partner, device_id_type=MESH)
    pl.semaphore_wait(barrier, 7)

    lend = pltpu.make_async_remote_copy(
        src_ref=own_ref,
        dst_ref=partner_ref,
        send_sem=send_sem.at[14],
        recv_sem=recv_sem.at[14],
        device_id=partner,
        device_id_type=MESH,
    )

    def build():
        count = orb_ref.shape[0]
        step = 32
        for a, raw in enumerate((orb_ref, app_ref)):
            for n in range(0, count, step):
                v = raw[pl.ds(n, step)]
                for q in range(2):
                    own_ref[pl.ds(a * count + n, step), pl.ds(q * band, band)] = v[:, q, :]

    band = own_ref.shape[1] // 2
    width = x_ref.shape[2] // 2
    depth = 2 * x_ref.shape[1]

    def compute(y, z, x):
        w = g_ref[y, z // 2, x, z % 2].reshape(depth, 2 * width)
        koff = pl.multiple_of((y * 2 + z // 2) * depth, depth)
        block = x * 2 + z % 2
        for src, rows in enumerate((own_ref, partner_ref)):
            first = jnp.dot(rows[:, pl.ds(koff, depth)], w, preferred_element_type=jnp.float32)
            second = jnp.dot(rows[:, pl.ds(band + koff, depth)], w, preferred_element_type=jnp.float32)
            acc[src, 0, block] += first[:, :width] - second[:, width:]
            acc[src, 1, block] += first[:, width:] + second[:, :width]

    def compute_block(held, axis=None, delta=0):
        at = dict(here)
        if axis is not None:
            at[axis] = lax.rem(at[axis] + delta + RING, RING)
        full = [d for d in ("y", "z", "x") if d in held]

        def body(i, carry):
            c = dict(at)
            rest = i
            for d in full:
                c[d] = rest % RING
                rest = rest // RING
            compute(c["y"], c["z"], c["x"])
            return carry

        lax.fori_loop(0, RING ** len(full), body, 0)

    unit = view(())
    keep = pl.multiple_of(core * width, width)
    give = pl.multiple_of((1 - core) * width, width)
    moves = []
    for p in range(2):
        dst = unit.at[core, :, pl.ds(p * width, width)]
        local = pltpu.make_async_copy(x_ref.at[p, :, pl.ds(keep, width)], dst, local_sem.at[p])
        local.start()
        swap = pltpu.make_async_remote_copy(
            src_ref=x_ref.at[p, :, pl.ds(give, width)],
            dst_ref=dst,
            send_sem=send_sem.at[12 + p],
            recv_sem=recv_sem.at[12 + p],
            device_id=partner,
            device_id_type=MESH,
        )
        swap.start()
        moves.append((local, swap, unit.at[1 - core, :, pl.ds(p * width, width)], p))

    def settle():
        for local, swap, dst, p in moves:
            local.wait()
            swap.wait_send()
            pltpu.make_async_remote_copy(
                src_ref=x_ref.at[p, :, pl.ds(give, width)],
                dst_ref=dst,
                send_sem=send_sem.at[12 + p],
                recv_sem=recv_sem.at[12 + p],
                device_id=partner,
                device_id_type=MESH,
            ).wait_recv()

    def ring2(src, dst, slot, axis, delta):
        return pltpu.make_async_remote_copy(
            src_ref=src,
            dst_ref=dst,
            send_sem=ring_send.at[slot],
            recv_sem=ring_recv.at[slot],
            device_id=device(axis, delta),
            device_id_type=MESH,
        )

    def first_pieces(axis, delta, side):
        at = view((), axis, side) if side else unit
        return [
            (x_ref.at[p, :, pl.ds(keep, width)], at.at[core, :, pl.ds(p * width, width)], 4 * (0 if delta == 1 else 1) + p)
            for p in range(2)
        ] + [(at.at[1 - core], at.at[1 - core], 4 * (0 if delta == 1 else 1) + 2)]

    def ring(ref, slot, axis, delta):
        return pltpu.make_async_remote_copy(
            src_ref=ref,
            dst_ref=ref,
            send_sem=ring_send.at[slot],
            recv_sem=ring_recv.at[slot],
            device_id=device(axis, delta),
            device_id_type=MESH,
        )

    def run(order):
        held = ()
        sent = []
        pending = []
        for stage, axis in enumerate(order):
            base = stage * 10
            if stage == 0:
                parts = [None]
            else:
                prev = order[stage - 1]
                parts = [(prev, 0), (prev, -1), (prev, 1), (prev, 2)]

            def send_part(i):
                for j, delta in enumerate((1, -1)):
                    copy = ring(view(held, pin=parts[i]), base + 4 * j + i, axis, delta)
                    copy.start()
                    sent.append(copy)

            if stage == 0:
                for delta in (1, -1):
                    for src, dst, slot in first_pieces(axis, delta, 0)[:2]:
                        copy = ring2(src, dst, slot, axis, delta)
                        copy.start()
                        sent.append(copy)
                settle()
                for delta in (1, -1):
                    for src, dst, slot in first_pieces(axis, delta, 0)[2:]:
                        copy = ring2(src, dst, slot, axis, delta)
                        copy.start()
                        sent.append(copy)
                build()
                for delta in (1, -1):
                    for src, dst, slot in first_pieces(axis, delta, -delta):
                        ring2(src, dst, slot, axis, -delta).wait_recv()
            for i in range(len(parts) - 1):
                send_part(i)
            if stage == 1:
                acc[...] = jnp.zeros_like(acc)
            for copy in pending:
                copy.wait_recv()
            if stage > 0:
                send_part(3)
            if stage == 2:
                lend.wait_send()
                pltpu.make_async_remote_copy(
                    src_ref=own_ref,
                    dst_ref=partner_ref,
                    send_sem=send_sem.at[14],
                    recv_sem=recv_sem.at[14],
                    device_id=partner,
                    device_id_type=MESH,
                ).wait_recv()
                compute_block(held)
            fwd_base = 30 + stage * 8
            for i in range(len(parts)):
                for j, delta in enumerate((1, -1)):
                    if stage > 0:
                        ring(view(held, axis, -delta, pin=parts[i]), base + 4 * j + i, axis, -delta).wait_recv()
                    half = 0 if delta == -1 else 1
                    copy = ring(view(held, axis, -delta, half, parts[i]), fwd_base + 2 * i + j, axis, delta)
                    copy.start()
                    sent.append(copy)
            if stage == 2:
                compute_block(held, axis, -1)
                compute_block(held, axis, 1)
            pending = []
            for i in range(len(parts)):
                for j, delta in enumerate((1, -1)):
                    half = 0 if delta == -1 else 1
                    pending.append(ring(view(held, axis, 2, half, parts[i]), fwd_base + 2 * i + j, axis, -delta))
            if stage == 0:
                lend.start()
            held = held + (axis,)
        for copy in pending:
            copy.wait_recv()
        for copy in sent:
            copy.wait_send()
        compute_block(held[:-1], order[-1], 2)

    for index, order in enumerate(ORDERS):
        @pl.when(core == index)
        def _():
            run(order)

    lent[...] = acc[1].astype(lent.dtype)
    give_back = pltpu.make_async_remote_copy(
        src_ref=lent,
        dst_ref=back,
        send_sem=send_sem.at[15],
        recv_sem=recv_sem.at[15],
        device_id=partner,
        device_id_type=MESH,
    )
    give_back.start()
    rows = orb_out.shape[0]
    blocks = acc.shape[2]

    def store(values, h):
        for a, out in enumerate((orb_out, app_out)):
            for c in range(blocks):
                lane = pl.multiple_of(c * 2 * width + h * width, width)
                part = [values[p, c, pl.ds(a * rows, rows), :].astype(out.dtype) for p in range(2)]
                out[:, :, pl.ds(lane, width)] = jnp.stack(part, axis=1)

    store(acc.at[0], core)
    give_back.wait_send()
    pltpu.make_async_remote_copy(
        src_ref=lent,
        dst_ref=back,
        send_sem=send_sem.at[15],
        recv_sem=recv_sem.at[15],
        device_id=partner,
        device_id_type=MESH,
    ).wait_recv()
    store(back, 1 - core)


def ring_rotate(ritz, orbitals, applied_orbitals):
    rows, band2 = 2 * orbitals.shape[0], 2 * orbitals.shape[2]
    own = orbitals
    units = (RING, 2, RING, 2, 2, ritz.shape[1], ritz.shape[2])
    width = ritz.shape[2] // 2
    out = jax.ShapeDtypeStruct((rows // 2, 2, band2 // 2), jnp.bfloat16)
    vmem = pl.BlockSpec(memory_space=pltpu.VMEM)
    flops = 2 * 2 * rows * band2 * 2 * ritz.shape[2] * 2 * RING
    return pl.pallas_call(
        ring_rotate_kernel,
        out_shape=[out, out],
        in_specs=[pl.BlockSpec(memory_space=pl.ANY), vmem, vmem],
        out_specs=[vmem, vmem],
        scratch_shapes=[
            pltpu.VMEM(units, ritz.dtype),
            pltpu.VMEM((rows, band2), own.dtype),
            pltpu.VMEM((rows, band2), own.dtype),
            pltpu.VMEM((2, 2, 2 * RING, rows, width), jnp.float32),
            pltpu.VMEM((2, 2 * RING, rows, width), jnp.bfloat16),
            pltpu.VMEM((2, 2 * RING, rows, width), jnp.bfloat16),
            pltpu.SemaphoreType.DMA((16,)),
            pltpu.SemaphoreType.DMA((16,)),
            pltpu.SemaphoreType.DMA((2,)),
            pltpu.SemaphoreType.DMA((54,)),
            pltpu.SemaphoreType.DMA((54,)),
        ],
        compiler_params=pltpu.CompilerParams(
            collective_id=0, has_side_effects=True, vmem_limit_bytes=60 * 1024 * 1024
        ),
        cost_estimate=pl.CostEstimate(flops=flops, transcendentals=0, bytes_accessed=8 * own.size * 2),
    )(ritz, orbitals, applied_orbitals)


def rotate_kernel(own_ref, partner_ref, ritz_ref, own_out, partner_out):
    band = own_ref.shape[1] // 2
    width = own_out.shape[-1]
    weights = ritz_ref[...].reshape(-1, 2 * width)
    for src, dst in ((own_ref, own_out), (partner_ref, partner_out)):
        first = jnp.dot(src[:, :band], weights, preferred_element_type=jnp.float32)
        second = jnp.dot(src[:, band:], weights, preferred_element_type=jnp.float32)
        real = first[:, :width] - second[:, width:]
        imag = first[:, width:] + second[:, :width]
        dst[0] = real.astype(dst.dtype)
        dst[1] = imag.astype(dst.dtype)


def rotate(own, partner, gathered):
    rows, band2 = own.shape
    rc, cb, co, k, width2 = gathered.shape
    width = width2 // 2
    x_spec = pl.BlockSpec((rows, band2), lambda c: (0, 0))
    g_spec = pl.BlockSpec((rc, None, co, k, width2), lambda c: (0, c, 0, 0, 0))
    o_spec = pl.BlockSpec((2, None, rows, width), lambda c: (0, c, 0, 0))
    out = jax.ShapeDtypeStruct((2, cb, rows, width), jnp.bfloat16)
    flops = 2 * 2 * rows * band2 * width2
    moved = 2 * own.size * 2 + gathered.size * 2 + 2 * own.size * 2
    return pl.pallas_call(
        rotate_kernel,
        grid=(cb,),
        in_specs=[x_spec, x_spec, g_spec],
        out_specs=[o_spec, o_spec],
        out_shape=[out, out],
        compiler_params=pltpu.CompilerParams(vmem_limit_bytes=48 * 1024 * 1024),
        cost_estimate=pl.CostEstimate(flops=flops, transcendentals=0, bytes_accessed=moved),
    )(own, partner, gathered)


def shards(rc_count, col_count, orbitals, applied_orbitals, ritz_matrix):
    me = lax.axis_index("core")
    rows = orbitals.shape[0]
    band_count = orbitals.shape[2]

    orb_out, app_out = ring_rotate(ritz_matrix, orbitals, applied_orbitals)
    return orb_out, app_out


def solution(mesh):
    devices = mesh.devices
    split = Mesh(
        devices.reshape(devices.shape[0] // 2, 2, devices.shape[1]), ("rc", "core", "col")
    )
    flat = ("rc", "core", "col")
    in_specs = (P(flat, None, None), P(flat, None, None), P(None, ("rc", "core"), "col"))
    out_specs = (P(flat, None, None), P(flat, None, None))
    body = functools.partial(shards, devices.shape[0] // 2, devices.shape[1])
    return jax.shard_map(body, mesh=split, in_specs=in_specs, out_specs=out_specs, check_vma=False)
```

```python
import functools

import jax
import jax.numpy as jnp
from jax import lax
from jax.experimental import pallas as pl
from jax.experimental.pallas import tpu as pltpu
from jax.sharding import Mesh
from jax.sharding import PartitionSpec as P

SWAP = [(0, 1), (1, 0)]
AXES = ("rc", "core", "col")
MESH = pl.DeviceIdType.MESH


RING = 4
ORDERS = (("x", "y", "z"), ("y", "z", "x"))
DIMS = ("y", "z_hi", "x", "z_lo")


def ring_rotate_kernel(
    x_ref, orb_ref, app_ref, orb_out, app_out, g_ref, own_ref, partner_ref, acc, lent, back, send_sem, recv_sem,
    local_sem, ring_send, ring_recv,
):
    rc = lax.axis_index("rc")
    core = lax.axis_index("core")
    col = lax.axis_index("col")
    here = {"y": rc // 2, "z": (rc % 2) * 2 + col % 2, "x": col // 2}

    def device(axis, delta):
        at = dict(here)
        at[axis] = lax.rem(at[axis] + delta + RING, RING)
        return (at["y"] * 2 + at["z"] // 2, core, at["x"] * 2 + at["z"] % 2)

    def view(held, axis=None, delta=0, half=None, pin=None):
        at = dict(here)
        pins = {} if pin is None else {pin[0]: pin[1]}
        if axis is not None:
            pins[axis] = delta
        for a, d in pins.items():
            at[a] = lax.rem(at[a] + d + RING, RING)
        held = tuple(h for h in held if h not in pins)
        index = []
        split = half is not None
        for dim in DIMS:
            phys = "z" if dim.startswith("z") else dim
            if phys in held:
                size = 2 if phys == "z" else RING
                if split:
                    index.append(pl.ds(half * (size // 2), size // 2))
                    split = False
                else:
                    index.append(slice(None))
            elif dim == "z_hi":
                index.append(at["z"] // 2)
            elif dim == "z_lo":
                index.append(at["z"] % 2)
            else:
                index.append(at[phys])
        if split:
            index.append(pl.ds(half, 1))
        return g_ref.at[tuple(index)]

    def remote(src, dst, slot, axis, delta):
        return pltpu.make_async_remote_copy(
            src_ref=src,
            dst_ref=dst,
            send_sem=send_sem.at[slot],
            recv_sem=recv_sem.at[slot],
            device_id=device(axis, delta),
            device_id_type=MESH,
        )

    partner = (rc, 1 - core, col)
    barrier = pltpu.get_barrier_semaphore()
    for axis in ("x", "y", "z"):
        for delta in (1, -1):
            pl.semaphore_signal(barrier, 1, device_id=device(axis, delta), device_id_type=MESH)
    pl.semaphore_signal(barrier, 1, device_id=partner, device_id_type=MESH)
    pl.semaphore_wait(barrier, 7)

    lend = pltpu.make_async_remote_copy(
        src_ref=own_ref,
        dst_ref=partner_ref,
        send_sem=send_sem.at[14],
        recv_sem=recv_sem.at[14],
        device_id=partner,
        device_id_type=MESH,
    )

    def build():
        count = orb_ref.shape[0]
        step = 32
        for a, raw in enumerate((orb_ref, app_ref)):
            for n in range(0, count, step):
                v = raw[pl.ds(n, step)]
                for q in range(2):
                    own_ref[pl.ds(a * count + n, step), pl.ds(q * band, band)] = v[:, q, :]

    band = own_ref.shape[1] // 2
    width = x_ref.shape[2] // 2
    depth = 2 * x_ref.shape[1]

    def compute(y, z, x):
        w = g_ref[y, z // 2, x, z % 2].reshape(depth, 2 * width)
        koff = pl.multiple_of((y * 2 + z // 2) * depth, depth)
        block = x * 2 + z % 2
        for src, rows in enumerate((own_ref, partner_ref)):
            first = jnp.dot(rows[:, pl.ds(koff, depth)], w, preferred_element_type=jnp.float32)
            second = jnp.dot(rows[:, pl.ds(band + koff, depth)], w, preferred_element_type=jnp.float32)
            acc[src, 0, block] += first[:, :width] - second[:, width:]
            acc[src, 1, block] += first[:, width:] + second[:, :width]

    def compute_block(held, axis=None, delta=0, pin=None):
        at = dict(here)
        pins = {} if pin is None else {pin[0]: pin[1]}
        if axis is not None:
            pins[axis] = delta
        for a, d in pins.items():
            at[a] = lax.rem(at[a] + d + RING, RING)
        full = [d for d in ("y", "z", "x") if d in held and d not in pins]

        def body(i, carry):
            c = dict(at)
            rest = i
            for d in full:
                c[d] = rest % RING
                rest = rest // RING
            compute(c["y"], c["z"], c["x"])
            return carry

        lax.fori_loop(0, RING ** len(full), body, 0)

    unit = view(())
    keep = pl.multiple_of(core * width, width)
    give = pl.multiple_of((1 - core) * width, width)
    moves = []
    for p in range(2):
        dst = unit.at[core, :, pl.ds(p * width, width)]
        local = pltpu.make_async_copy(x_ref.at[p, :, pl.ds(keep, width)], dst, local_sem.at[p])
        local.start()
        swap = pltpu.make_async_remote_copy(
            src_ref=x_ref.at[p, :, pl.ds(give, width)],
            dst_ref=dst,
            send_sem=send_sem.at[12 + p],
            recv_sem=recv_sem.at[12 + p],
            device_id=partner,
            device_id_type=MESH,
        )
        swap.start()
        moves.append((local, swap, unit.at[1 - core, :, pl.ds(p * width, width)], p))
    for local, swap, dst, p in moves:
        local.wait()
        swap.wait_send()
        pltpu.make_async_remote_copy(
            src_ref=x_ref.at[p, :, pl.ds(give, width)],
            dst_ref=dst,
            send_sem=send_sem.at[12 + p],
            recv_sem=recv_sem.at[12 + p],
            device_id=partner,
            device_id_type=MESH,
        ).wait_recv()

    def ring(ref, slot, axis, delta):
        return pltpu.make_async_remote_copy(
            src_ref=ref,
            dst_ref=ref,
            send_sem=ring_send.at[slot],
            recv_sem=ring_recv.at[slot],
            device_id=device(axis, delta),
            device_id_type=MESH,
        )

    def run(order):
        held = ()
        sent = []
        pending = []
        for stage, axis in enumerate(order):
            base = stage * 10
            if stage == 0:
                parts = [None]
            else:
                prev = order[stage - 1]
                parts = [(prev, 0), (prev, -1), (prev, 1), (prev, 2)]

            def send_part(i):
                for j, delta in enumerate((1, -1)):
                    copy = ring(view(held, pin=parts[i]), base + 4 * j + i, axis, delta)
                    copy.start()
                    sent.append(copy)

            for i in range(max(1, len(parts) - 1)):
                send_part(i)
            if stage == 0:
                build()
            if stage == 1:
                acc[...] = jnp.zeros_like(acc)
            for copy in pending:
                copy.wait_recv()
            if stage > 0:
                send_part(3)
            if stage == 2:
                lend.wait_send()
                pltpu.make_async_remote_copy(
                    src_ref=own_ref,
                    dst_ref=partner_ref,
                    send_sem=send_sem.at[14],
                    recv_sem=recv_sem.at[14],
                    device_id=partner,
                    device_id_type=MESH,
                ).wait_recv()
            fwd_base = 30 + stage * 8
            for i in range(len(parts)):
                for j, delta in enumerate((1, -1)):
                    ring(view(held, axis, -delta, pin=parts[i]), base + 4 * j + i, axis, -delta).wait_recv()
                    half = 0 if delta == -1 else 1
                    copy = ring(view(held, axis, -delta, half, parts[i]), fwd_base + 2 * i + j, axis, delta)
                    copy.start()
                    sent.append(copy)
                if stage == 2:
                    compute_block(held, pin=parts[i])
            if stage == 2:
                compute_block(held, axis, -1)
                compute_block(held, axis, 1)
            pending = []
            for i in range(len(parts)):
                for j, delta in enumerate((1, -1)):
                    half = 0 if delta == -1 else 1
                    pending.append(ring(view(held, axis, 2, half, parts[i]), fwd_base + 2 * i + j, axis, -delta))
            if stage == 0:
                lend.start()
            held = held + (axis,)
        for copy in pending:
            copy.wait_recv()
        for copy in sent:
            copy.wait_send()
        compute_block(held[:-1], order[-1], 2)

    for index, order in enumerate(ORDERS):
        @pl.when(core == index)
        def _():
            run(order)

    lent[...] = acc[1].astype(lent.dtype)
    give_back = pltpu.make_async_remote_copy(
        src_ref=lent,
        dst_ref=back,
        send_sem=send_sem.at[15],
        recv_sem=recv_sem.at[15],
        device_id=partner,
        device_id_type=MESH,
    )
    give_back.start()
    rows = orb_out.shape[0]
    blocks = acc.shape[2]

    def store(values, h):
        for a, out in enumerate((orb_out, app_out)):
            for c in range(blocks):
                lane = pl.multiple_of(c * 2 * width + h * width, width)
                part = [values[p, c, pl.ds(a * rows, rows), :].astype(out.dtype) for p in range(2)]
                out[:, :, pl.ds(lane, width)] = jnp.stack(part, axis=1)

    store(acc.at[0], core)
    give_back.wait_send()
    pltpu.make_async_remote_copy(
        src_ref=lent,
        dst_ref=back,
        send_sem=send_sem.at[15],
        recv_sem=recv_sem.at[15],
        device_id=partner,
        device_id_type=MESH,
    ).wait_recv()
    store(back, 1 - core)


def ring_rotate(ritz, orbitals, applied_orbitals):
    rows, band2 = 2 * orbitals.shape[0], 2 * orbitals.shape[2]
    own = orbitals
    units = (RING, 2, RING, 2, 2, ritz.shape[1], ritz.shape[2])
    width = ritz.shape[2] // 2
    out = jax.ShapeDtypeStruct((rows // 2, 2, band2 // 2), jnp.bfloat16)
    vmem = pl.BlockSpec(memory_space=pltpu.VMEM)
    flops = 2 * 2 * rows * band2 * 2 * ritz.shape[2] * 2 * RING
    return pl.pallas_call(
        ring_rotate_kernel,
        out_shape=[out, out],
        in_specs=[pl.BlockSpec(memory_space=pl.ANY), vmem, vmem],
        out_specs=[vmem, vmem],
        scratch_shapes=[
            pltpu.VMEM(units, ritz.dtype),
            pltpu.VMEM((rows, band2), own.dtype),
            pltpu.VMEM((rows, band2), own.dtype),
            pltpu.VMEM((2, 2, 2 * RING, rows, width), jnp.float32),
            pltpu.VMEM((2, 2 * RING, rows, width), jnp.bfloat16),
            pltpu.VMEM((2, 2 * RING, rows, width), jnp.bfloat16),
            pltpu.SemaphoreType.DMA((16,)),
            pltpu.SemaphoreType.DMA((16,)),
            pltpu.SemaphoreType.DMA((2,)),
            pltpu.SemaphoreType.DMA((54,)),
            pltpu.SemaphoreType.DMA((54,)),
        ],
        compiler_params=pltpu.CompilerParams(
            collective_id=0, has_side_effects=True, vmem_limit_bytes=60 * 1024 * 1024
        ),
        cost_estimate=pl.CostEstimate(flops=flops, transcendentals=0, bytes_accessed=8 * own.size * 2),
    )(ritz, orbitals, applied_orbitals)


def rotate_kernel(own_ref, partner_ref, ritz_ref, own_out, partner_out):
    band = own_ref.shape[1] // 2
    width = own_out.shape[-1]
    weights = ritz_ref[...].reshape(-1, 2 * width)
    for src, dst in ((own_ref, own_out), (partner_ref, partner_out)):
        first = jnp.dot(src[:, :band], weights, preferred_element_type=jnp.float32)
        second = jnp.dot(src[:, band:], weights, preferred_element_type=jnp.float32)
        real = first[:, :width] - second[:, width:]
        imag = first[:, width:] + second[:, :width]
        dst[0] = real.astype(dst.dtype)
        dst[1] = imag.astype(dst.dtype)


def rotate(own, partner, gathered):
    rows, band2 = own.shape
    rc, cb, co, k, width2 = gathered.shape
    width = width2 // 2
    x_spec = pl.BlockSpec((rows, band2), lambda c: (0, 0))
    g_spec = pl.BlockSpec((rc, None, co, k, width2), lambda c: (0, c, 0, 0, 0))
    o_spec = pl.BlockSpec((2, None, rows, width), lambda c: (0, c, 0, 0))
    out = jax.ShapeDtypeStruct((2, cb, rows, width), jnp.bfloat16)
    flops = 2 * 2 * rows * band2 * width2
    moved = 2 * own.size * 2 + gathered.size * 2 + 2 * own.size * 2
    return pl.pallas_call(
        rotate_kernel,
        grid=(cb,),
        in_specs=[x_spec, x_spec, g_spec],
        out_specs=[o_spec, o_spec],
        out_shape=[out, out],
        compiler_params=pltpu.CompilerParams(vmem_limit_bytes=48 * 1024 * 1024),
        cost_estimate=pl.CostEstimate(flops=flops, transcendentals=0, bytes_accessed=moved),
    )(own, partner, gathered)


def shards(rc_count, col_count, orbitals, applied_orbitals, ritz_matrix):
    me = lax.axis_index("core")
    rows = orbitals.shape[0]
    band_count = orbitals.shape[2]

    orb_out, app_out = ring_rotate(ritz_matrix, orbitals, applied_orbitals)
    return orb_out, app_out


def solution(mesh):
    devices = mesh.devices
    split = Mesh(
        devices.reshape(devices.shape[0] // 2, 2, devices.shape[1]), ("rc", "core", "col")
    )
    flat = ("rc", "core", "col")
    in_specs = (P(flat, None, None), P(flat, None, None), P(None, ("rc", "core"), "col"))
    out_specs = (P(flat, None, None), P(flat, None, None))
    body = functools.partial(shards, devices.shape[0] // 2, devices.shape[1])
    return jax.shard_map(body, mesh=split, in_specs=in_specs, out_specs=out_specs, check_vma=False)
```

```python
import functools

import jax
import jax.numpy as jnp
from jax import lax
from jax.experimental import pallas as pl
from jax.experimental.pallas import tpu as pltpu
from jax.sharding import Mesh
from jax.sharding import PartitionSpec as P

SWAP = [(0, 1), (1, 0)]
AXES = ("rc", "core", "col")
MESH = pl.DeviceIdType.MESH


RING = 4
ORDERS = (("x", "y", "z"), ("y", "z", "x"))
DIMS = ("y", "z_hi", "x", "z_lo")


def ring_rotate_kernel(
    x_ref, orb_ref, app_ref, orb_out, app_out, g_ref, own_ref, partner_ref, acc, lent, back, send_sem, recv_sem,
    local_sem, ring_send, ring_recv,
):
    rc = lax.axis_index("rc")
    core = lax.axis_index("core")
    col = lax.axis_index("col")
    here = {"y": rc // 2, "z": (rc % 2) * 2 + col % 2, "x": col // 2}

    def device(axis, delta):
        at = dict(here)
        at[axis] = lax.rem(at[axis] + delta + RING, RING)
        return (at["y"] * 2 + at["z"] // 2, core, at["x"] * 2 + at["z"] % 2)

    def view(held, axis=None, delta=0, half=None, pin=None):
        at = dict(here)
        pins = {} if pin is None else {pin[0]: pin[1]}
        if axis is not None:
            pins[axis] = delta
        for a, d in pins.items():
            at[a] = lax.rem(at[a] + d + RING, RING)
        held = tuple(h for h in held if h not in pins)
        index = []
        split = half is not None
        for dim in DIMS:
            phys = "z" if dim.startswith("z") else dim
            if phys in held:
                size = 2 if phys == "z" else RING
                if split:
                    index.append(pl.ds(half * (size // 2), size // 2))
                    split = False
                else:
                    index.append(slice(None))
            elif dim == "z_hi":
                index.append(at["z"] // 2)
            elif dim == "z_lo":
                index.append(at["z"] % 2)
            else:
                index.append(at[phys])
        if split:
            index.append(pl.ds(half, 1))
        return g_ref.at[tuple(index)]

    def remote(src, dst, slot, axis, delta):
        return pltpu.make_async_remote_copy(
            src_ref=src,
            dst_ref=dst,
            send_sem=send_sem.at[slot],
            recv_sem=recv_sem.at[slot],
            device_id=device(axis, delta),
            device_id_type=MESH,
        )

    partner = (rc, 1 - core, col)
    barrier = pltpu.get_barrier_semaphore()
    for axis in ("x", "y", "z"):
        for delta in (1, -1):
            pl.semaphore_signal(barrier, 1, device_id=device(axis, delta), device_id_type=MESH)
    pl.semaphore_signal(barrier, 1, device_id=partner, device_id_type=MESH)
    pl.semaphore_wait(barrier, 7)

    lend = pltpu.make_async_remote_copy(
        src_ref=own_ref,
        dst_ref=partner_ref,
        send_sem=send_sem.at[14],
        recv_sem=recv_sem.at[14],
        device_id=partner,
        device_id_type=MESH,
    )

    def build():
        count = orb_ref.shape[0]
        step = 32
        for a, raw in enumerate((orb_ref, app_ref)):
            for n in range(0, count, step):
                v = raw[pl.ds(n, step)]
                for q in range(2):
                    own_ref[pl.ds(a * count + n, step), pl.ds(q * band, band)] = v[:, q, :]

    band = own_ref.shape[1] // 2
    width = x_ref.shape[2] // 2
    depth = 2 * x_ref.shape[1]

    def compute(y, z, x):
        w = g_ref[y, z // 2, x, z % 2].reshape(depth, 2 * width)
        koff = pl.multiple_of((y * 2 + z // 2) * depth, depth)
        block = x * 2 + z % 2
        for src, rows in enumerate((own_ref, partner_ref)):
            first = jnp.dot(rows[:, pl.ds(koff, depth)], w, preferred_element_type=jnp.float32)
            second = jnp.dot(rows[:, pl.ds(band + koff, depth)], w, preferred_element_type=jnp.float32)
            acc[src, 0, block] += first[:, :width] - second[:, width:]
            acc[src, 1, block] += first[:, width:] + second[:, :width]

    def compute_block(held, axis=None, delta=0):
        at = dict(here)
        if axis is not None:
            at[axis] = lax.rem(at[axis] + delta + RING, RING)
        full = [d for d in ("y", "z", "x") if d in held]

        def body(i, carry):
            c = dict(at)
            rest = i
            for d in full:
                c[d] = rest % RING
                rest = rest // RING
            compute(c["y"], c["z"], c["x"])
            return carry

        lax.fori_loop(0, RING ** len(full), body, 0)

    unit = view(())
    keep = pl.multiple_of(core * width, width)
    give = pl.multiple_of((1 - core) * width, width)
    moves = []
    for p in range(2):
        dst = unit.at[core, :, pl.ds(p * width, width)]
        local = pltpu.make_async_copy(x_ref.at[p, :, pl.ds(keep, width)], dst, local_sem.at[p])
        local.start()
        swap = pltpu.make_async_remote_copy(
            src_ref=x_ref.at[p, :, pl.ds(give, width)],
            dst_ref=dst,
            send_sem=send_sem.at[12 + p],
            recv_sem=recv_sem.at[12 + p],
            device_id=partner,
            device_id_type=MESH,
        )
        swap.start()
        moves.append((local, swap, unit.at[1 - core, :, pl.ds(p * width, width)], p))
    for local, swap, dst, p in moves:
        local.wait()
        swap.wait_send()
        pltpu.make_async_remote_copy(
            src_ref=x_ref.at[p, :, pl.ds(give, width)],
            dst_ref=dst,
            send_sem=send_sem.at[12 + p],
            recv_sem=recv_sem.at[12 + p],
            device_id=partner,
            device_id_type=MESH,
        ).wait_recv()

    def ring(ref, slot, axis, delta):
        return pltpu.make_async_remote_copy(
            src_ref=ref,
            dst_ref=ref,
            send_sem=ring_send.at[slot],
            recv_sem=ring_recv.at[slot],
            device_id=device(axis, delta),
            device_id_type=MESH,
        )

    def run(order):
        held = ()
        sent = []
        pending = []
        for stage, axis in enumerate(order):
            base = stage * 10
            if stage == 0:
                parts = [None]
            else:
                prev = order[stage - 1]
                parts = [(prev, 0), (prev, -1), (prev, 1), (prev, 2)]

            def send_part(i):
                for j, delta in enumerate((1, -1)):
                    copy = ring(view(held, pin=parts[i]), base + 4 * j + i, axis, delta)
                    copy.start()
                    sent.append(copy)

            for i in range(max(1, len(parts) - 1)):
                send_part(i)
            if stage == 1:
                build()
                lend.start()
                acc[...] = jnp.zeros_like(acc)
            for copy in pending:
                copy.wait_recv()
            if stage > 0:
                send_part(3)
            if stage == 2:
                lend.wait_send()
                pltpu.make_async_remote_copy(
                    src_ref=own_ref,
                    dst_ref=partner_ref,
                    send_sem=send_sem.at[14],
                    recv_sem=recv_sem.at[14],
                    device_id=partner,
                    device_id_type=MESH,
                ).wait_recv()
                compute_block(held)
            fwd_base = 30 + stage * 8
            for i in range(len(parts)):
                for j, delta in enumerate((1, -1)):
                    ring(view(held, axis, -delta, pin=parts[i]), base + 4 * j + i, axis, -delta).wait_recv()
                    half = 0 if delta == -1 else 1
                    copy = ring(view(held, axis, -delta, half, parts[i]), fwd_base + 2 * i + j, axis, delta)
                    copy.start()
                    sent.append(copy)
            if stage == 2:
                compute_block(held, axis, -1)
                compute_block(held, axis, 1)
            pending = []
            for i in range(len(parts)):
                for j, delta in enumerate((1, -1)):
                    half = 0 if delta == -1 else 1
                    pending.append(ring(view(held, axis, 2, half, parts[i]), fwd_base + 2 * i + j, axis, -delta))
            held = held + (axis,)
        for copy in pending:
            copy.wait_recv()
        for copy in sent:
            copy.wait_send()
        compute_block(held[:-1], order[-1], 2)

    for index, order in enumerate(ORDERS):
        @pl.when(core == index)
        def _():
            run(order)

    lent[...] = acc[1].astype(lent.dtype)
    give_back = pltpu.make_async_remote_copy(
        src_ref=lent,
        dst_ref=back,
        send_sem=send_sem.at[15],
        recv_sem=recv_sem.at[15],
        device_id=partner,
        device_id_type=MESH,
    )
    give_back.start()
    rows = orb_out.shape[0]
    blocks = acc.shape[2]

    def store(values, h):
        for a, out in enumerate((orb_out, app_out)):
            for c in range(blocks):
                lane = pl.multiple_of(c * 2 * width + h * width, width)
                part = [values[p, c, pl.ds(a * rows, rows), :].astype(out.dtype) for p in range(2)]
                out[:, :, pl.ds(lane, width)] = jnp.stack(part, axis=1)

    store(acc.at[0], core)
    give_back.wait_send()
    pltpu.make_async_remote_copy(
        src_ref=lent,
        dst_ref=back,
        send_sem=send_sem.at[15],
        recv_sem=recv_sem.at[15],
        device_id=partner,
        device_id_type=MESH,
    ).wait_recv()
    store(back, 1 - core)


def ring_rotate(ritz, orbitals, applied_orbitals):
    rows, band2 = 2 * orbitals.shape[0], 2 * orbitals.shape[2]
    own = orbitals
    units = (RING, 2, RING, 2, 2, ritz.shape[1], ritz.shape[2])
    width = ritz.shape[2] // 2
    out = jax.ShapeDtypeStruct((rows // 2, 2, band2 // 2), jnp.bfloat16)
    vmem = pl.BlockSpec(memory_space=pltpu.VMEM)
    flops = 2 * 2 * rows * band2 * 2 * ritz.shape[2] * 2 * RING
    return pl.pallas_call(
        ring_rotate_kernel,
        out_shape=[out, out],
        in_specs=[pl.BlockSpec(memory_space=pl.ANY), vmem, vmem],
        out_specs=[vmem, vmem],
        scratch_shapes=[
            pltpu.VMEM(units, ritz.dtype),
            pltpu.VMEM((rows, band2), own.dtype),
            pltpu.VMEM((rows, band2), own.dtype),
            pltpu.VMEM((2, 2, 2 * RING, rows, width), jnp.float32),
            pltpu.VMEM((2, 2 * RING, rows, width), jnp.bfloat16),
            pltpu.VMEM((2, 2 * RING, rows, width), jnp.bfloat16),
            pltpu.SemaphoreType.DMA((16,)),
            pltpu.SemaphoreType.DMA((16,)),
            pltpu.SemaphoreType.DMA((2,)),
            pltpu.SemaphoreType.DMA((54,)),
            pltpu.SemaphoreType.DMA((54,)),
        ],
        compiler_params=pltpu.CompilerParams(
            collective_id=0, has_side_effects=True, vmem_limit_bytes=60 * 1024 * 1024
        ),
        cost_estimate=pl.CostEstimate(flops=flops, transcendentals=0, bytes_accessed=8 * own.size * 2),
    )(ritz, orbitals, applied_orbitals)


def rotate_kernel(own_ref, partner_ref, ritz_ref, own_out, partner_out):
    band = own_ref.shape[1] // 2
    width = own_out.shape[-1]
    weights = ritz_ref[...].reshape(-1, 2 * width)
    for src, dst in ((own_ref, own_out), (partner_ref, partner_out)):
        first = jnp.dot(src[:, :band], weights, preferred_element_type=jnp.float32)
        second = jnp.dot(src[:, band:], weights, preferred_element_type=jnp.float32)
        real = first[:, :width] - second[:, width:]
        imag = first[:, width:] + second[:, :width]
        dst[0] = real.astype(dst.dtype)
        dst[1] = imag.astype(dst.dtype)


def rotate(own, partner, gathered):
    rows, band2 = own.shape
    rc, cb, co, k, width2 = gathered.shape
    width = width2 // 2
    x_spec = pl.BlockSpec((rows, band2), lambda c: (0, 0))
    g_spec = pl.BlockSpec((rc, None, co, k, width2), lambda c: (0, c, 0, 0, 0))
    o_spec = pl.BlockSpec((2, None, rows, width), lambda c: (0, c, 0, 0))
    out = jax.ShapeDtypeStruct((2, cb, rows, width), jnp.bfloat16)
    flops = 2 * 2 * rows * band2 * width2
    moved = 2 * own.size * 2 + gathered.size * 2 + 2 * own.size * 2
    return pl.pallas_call(
        rotate_kernel,
        grid=(cb,),
        in_specs=[x_spec, x_spec, g_spec],
        out_specs=[o_spec, o_spec],
        out_shape=[out, out],
        compiler_params=pltpu.CompilerParams(vmem_limit_bytes=48 * 1024 * 1024),
        cost_estimate=pl.CostEstimate(flops=flops, transcendentals=0, bytes_accessed=moved),
    )(own, partner, gathered)


def shards(rc_count, col_count, orbitals, applied_orbitals, ritz_matrix):
    me = lax.axis_index("core")
    rows = orbitals.shape[0]
    band_count = orbitals.shape[2]

    orb_out, app_out = ring_rotate(ritz_matrix, orbitals, applied_orbitals)
    return orb_out, app_out


def solution(mesh):
    devices = mesh.devices
    split = Mesh(
        devices.reshape(devices.shape[0] // 2, 2, devices.shape[1]), ("rc", "core", "col")
    )
    flat = ("rc", "core", "col")
    in_specs = (P(flat, None, None), P(flat, None, None), P(None, ("rc", "core"), "col"))
    out_specs = (P(flat, None, None), P(flat, None, None))
    body = functools.partial(shards, devices.shape[0] // 2, devices.shape[1])
    return jax.shard_map(body, mesh=split, in_specs=in_specs, out_specs=out_specs, check_vma=False)
```

```python
import functools

import jax
import jax.numpy as jnp
from jax import lax
from jax.experimental import pallas as pl
from jax.experimental.pallas import tpu as pltpu
from jax.sharding import Mesh
from jax.sharding import PartitionSpec as P

SWAP = [(0, 1), (1, 0)]
AXES = ("rc", "core", "col")
MESH = pl.DeviceIdType.MESH


RING = 4
ORDERS = (("x", "y", "z"), ("y", "z", "x"))
DIMS = ("y", "z_hi", "x", "z_lo")


def ring_rotate_kernel(
    x_ref, orb_ref, app_ref, orb_out, app_out, g_ref, own_ref, partner_ref, acc, lent, back, send_sem, recv_sem,
    local_sem, ring_send, ring_recv,
):
    rc = lax.axis_index("rc")
    core = lax.axis_index("core")
    col = lax.axis_index("col")
    here = {"y": rc // 2, "z": (rc % 2) * 2 + col % 2, "x": col // 2}

    def device(axis, delta):
        at = dict(here)
        at[axis] = lax.rem(at[axis] + delta + RING, RING)
        return (at["y"] * 2 + at["z"] // 2, core, at["x"] * 2 + at["z"] % 2)

    def view(held, axis=None, delta=0, half=None, pin=None):
        at = dict(here)
        pins = {} if pin is None else {pin[0]: pin[1]}
        if axis is not None:
            pins[axis] = delta
        for a, d in pins.items():
            at[a] = lax.rem(at[a] + d + RING, RING)
        held = tuple(h for h in held if h not in pins)
        index = []
        split = half is not None
        for dim in DIMS:
            phys = "z" if dim.startswith("z") else dim
            if phys in held:
                size = 2 if phys == "z" else RING
                if split:
                    index.append(pl.ds(half * (size // 2), size // 2))
                    split = False
                else:
                    index.append(slice(None))
            elif dim == "z_hi":
                index.append(at["z"] // 2)
            elif dim == "z_lo":
                index.append(at["z"] % 2)
            else:
                index.append(at[phys])
        if split:
            index.append(pl.ds(half, 1))
        return g_ref.at[tuple(index)]

    def remote(src, dst, slot, axis, delta):
        return pltpu.make_async_remote_copy(
            src_ref=src,
            dst_ref=dst,
            send_sem=send_sem.at[slot],
            recv_sem=recv_sem.at[slot],
            device_id=device(axis, delta),
            device_id_type=MESH,
        )

    partner = (rc, 1 - core, col)
    barrier = pltpu.get_barrier_semaphore()
    for axis in ("x", "y", "z"):
        for delta in (1, -1):
            pl.semaphore_signal(barrier, 1, device_id=device(axis, delta), device_id_type=MESH)
    pl.semaphore_signal(barrier, 1, device_id=partner, device_id_type=MESH)
    pl.semaphore_wait(barrier, 7)

    lend = pltpu.make_async_remote_copy(
        src_ref=own_ref,
        dst_ref=partner_ref,
        send_sem=send_sem.at[14],
        recv_sem=recv_sem.at[14],
        device_id=partner,
        device_id_type=MESH,
    )

    def build():
        count = orb_ref.shape[0]
        step = 32
        for a, raw in enumerate((orb_ref, app_ref)):
            for n in range(0, count, step):
                v = raw[pl.ds(n, step)]
                for q in range(2):
                    own_ref[pl.ds(a * count + n, step), pl.ds(q * band, band)] = v[:, q, :]

    band = own_ref.shape[1] // 2
    width = x_ref.shape[2] // 2
    depth = 2 * x_ref.shape[1]

    def compute(y, z, x):
        w = g_ref[y, z // 2, x, z % 2].reshape(depth, 2 * width)
        koff = pl.multiple_of((y * 2 + z // 2) * depth, depth)
        block = x * 2 + z % 2
        for src, rows in enumerate((own_ref, partner_ref)):
            first = jnp.dot(rows[:, pl.ds(koff, depth)], w, preferred_element_type=jnp.float32)
            second = jnp.dot(rows[:, pl.ds(band + koff, depth)], w, preferred_element_type=jnp.float32)
            acc[src, 0, block] += first[:, :width] - second[:, width:]
            acc[src, 1, block] += first[:, width:] + second[:, :width]

    def compute_block(held, axis=None, delta=0):
        at = dict(here)
        if axis is not None:
            at[axis] = lax.rem(at[axis] + delta + RING, RING)
        full = [d for d in ("y", "z", "x") if d in held]

        def body(i, carry):
            c = dict(at)
            rest = i
            for d in full:
                c[d] = rest % RING
                rest = rest // RING
            compute(c["y"], c["z"], c["x"])
            return carry

        lax.fori_loop(0, RING ** len(full), body, 0)

    unit = view(())
    keep = pl.multiple_of(core * width, width)
    give = pl.multiple_of((1 - core) * width, width)
    moves = []
    for p in range(2):
        dst = unit.at[core, :, pl.ds(p * width, width)]
        local = pltpu.make_async_copy(x_ref.at[p, :, pl.ds(keep, width)], dst, local_sem.at[p])
        local.start()
        swap = pltpu.make_async_remote_copy(
            src_ref=x_ref.at[p, :, pl.ds(give, width)],
            dst_ref=dst,
            send_sem=send_sem.at[12 + p],
            recv_sem=recv_sem.at[12 + p],
            device_id=partner,
            device_id_type=MESH,
        )
        swap.start()
        moves.append((local, swap, unit.at[1 - core, :, pl.ds(p * width, width)], p))
    for local, swap, dst, p in moves:
        local.wait()
        swap.wait_send()
        pltpu.make_async_remote_copy(
            src_ref=x_ref.at[p, :, pl.ds(give, width)],
            dst_ref=dst,
            send_sem=send_sem.at[12 + p],
            recv_sem=recv_sem.at[12 + p],
            device_id=partner,
            device_id_type=MESH,
        ).wait_recv()

    rows = orb_out.shape[0]
    blocks = acc.shape[2]

    def store_block(values, h, c):
        for a, out in enumerate((orb_out, app_out)):
            lane = pl.multiple_of(c * 2 * width + h * width, width)
            part = [values[p, c, pl.ds(a * rows, rows), :].astype(out.dtype) for p in range(2)]
            out[:, :, pl.ds(lane, width)] = jnp.stack(part, axis=1)

    def early(c, last):
        if last == "z":
            return c % 2 != here["z"] % 2
        if last == "x":
            return c // 2 != lax.rem(here["x"] + 2, RING)
        return core < 0

    def ring(ref, slot, axis, delta):
        return pltpu.make_async_remote_copy(
            src_ref=ref,
            dst_ref=ref,
            send_sem=ring_send.at[slot],
            recv_sem=ring_recv.at[slot],
            device_id=device(axis, delta),
            device_id_type=MESH,
        )

    def run(order):
        held = ()
        sent = []
        pending = []
        for stage, axis in enumerate(order):
            base = stage * 10
            if stage == 0:
                parts = [None]
            else:
                prev = order[stage - 1]
                parts = [(prev, 0), (prev, -1), (prev, 1), (prev, 2)]

            def send_part(i):
                for j, delta in enumerate((1, -1)):
                    copy = ring(view(held, pin=parts[i]), base + 4 * j + i, axis, delta)
                    copy.start()
                    sent.append(copy)

            for i in range(max(1, len(parts) - 1)):
                send_part(i)
            if stage == 1:
                build()
                lend.start()
                acc[...] = jnp.zeros_like(acc)
            for copy in pending:
                copy.wait_recv()
            if stage > 0:
                send_part(3)
            if stage == 2:
                lend.wait_send()
                pltpu.make_async_remote_copy(
                    src_ref=own_ref,
                    dst_ref=partner_ref,
                    send_sem=send_sem.at[14],
                    recv_sem=recv_sem.at[14],
                    device_id=partner,
                    device_id_type=MESH,
                ).wait_recv()
                compute_block(held)
            fwd_base = 30 + stage * 8
            for i in range(len(parts)):
                for j, delta in enumerate((1, -1)):
                    ring(view(held, axis, -delta, pin=parts[i]), base + 4 * j + i, axis, -delta).wait_recv()
                    half = 0 if delta == -1 else 1
                    copy = ring(view(held, axis, -delta, half, parts[i]), fwd_base + 2 * i + j, axis, delta)
                    copy.start()
                    sent.append(copy)
            if stage == 2:
                compute_block(held, axis, -1)
                compute_block(held, axis, 1)
            pending = []
            for i in range(len(parts)):
                for j, delta in enumerate((1, -1)):
                    half = 0 if delta == -1 else 1
                    pending.append(ring(view(held, axis, 2, half, parts[i]), fwd_base + 2 * i + j, axis, -delta))
            held = held + (axis,)
        for c in range(blocks):
            @pl.when(early(c, order[-1]))
            def _():
                store_block(acc.at[0], core, c)

        for copy in pending:
            copy.wait_recv()
        for copy in sent:
            copy.wait_send()
        compute_block(held[:-1], order[-1], 2)

    for index, order in enumerate(ORDERS):
        @pl.when(core == index)
        def _():
            run(order)

    lent[...] = acc[1].astype(lent.dtype)
    give_back = pltpu.make_async_remote_copy(
        src_ref=lent,
        dst_ref=back,
        send_sem=send_sem.at[15],
        recv_sem=recv_sem.at[15],
        device_id=partner,
        device_id_type=MESH,
    )
    give_back.start()
    for c in range(blocks):
        late = early(c, ORDERS[0][-1])
        for index, order in enumerate(ORDERS[1:], 1):
            late = jnp.where(core == index, early(c, order[-1]), late)

        @pl.when(jnp.logical_not(late))
        def _():
            store_block(acc.at[0], core, c)

    give_back.wait_send()
    pltpu.make_async_remote_copy(
        src_ref=lent,
        dst_ref=back,
        send_sem=send_sem.at[15],
        recv_sem=recv_sem.at[15],
        device_id=partner,
        device_id_type=MESH,
    ).wait_recv()
    for c in range(blocks):
        store_block(back, 1 - core, c)


def ring_rotate(ritz, orbitals, applied_orbitals):
    rows, band2 = 2 * orbitals.shape[0], 2 * orbitals.shape[2]
    own = orbitals
    units = (RING, 2, RING, 2, 2, ritz.shape[1], ritz.shape[2])
    width = ritz.shape[2] // 2
    out = jax.ShapeDtypeStruct((rows // 2, 2, band2 // 2), jnp.bfloat16)
    vmem = pl.BlockSpec(memory_space=pltpu.VMEM)
    flops = 2 * 2 * rows * band2 * 2 * ritz.shape[2] * 2 * RING
    return pl.pallas_call(
        ring_rotate_kernel,
        out_shape=[out, out],
        in_specs=[pl.BlockSpec(memory_space=pl.ANY), vmem, vmem],
        out_specs=[vmem, vmem],
        scratch_shapes=[
            pltpu.VMEM(units, ritz.dtype),
            pltpu.VMEM((rows, band2), own.dtype),
            pltpu.VMEM((rows, band2), own.dtype),
            pltpu.VMEM((2, 2, 2 * RING, rows, width), jnp.float32),
            pltpu.VMEM((2, 2 * RING, rows, width), jnp.bfloat16),
            pltpu.VMEM((2, 2 * RING, rows, width), jnp.bfloat16),
            pltpu.SemaphoreType.DMA((16,)),
            pltpu.SemaphoreType.DMA((16,)),
            pltpu.SemaphoreType.DMA((2,)),
            pltpu.SemaphoreType.DMA((54,)),
            pltpu.SemaphoreType.DMA((54,)),
        ],
        compiler_params=pltpu.CompilerParams(
            collective_id=0, has_side_effects=True, vmem_limit_bytes=60 * 1024 * 1024
        ),
        cost_estimate=pl.CostEstimate(flops=flops, transcendentals=0, bytes_accessed=8 * own.size * 2),
    )(ritz, orbitals, applied_orbitals)


def rotate_kernel(own_ref, partner_ref, ritz_ref, own_out, partner_out):
    band = own_ref.shape[1] // 2
    width = own_out.shape[-1]
    weights = ritz_ref[...].reshape(-1, 2 * width)
    for src, dst in ((own_ref, own_out), (partner_ref, partner_out)):
        first = jnp.dot(src[:, :band], weights, preferred_element_type=jnp.float32)
        second = jnp.dot(src[:, band:], weights, preferred_element_type=jnp.float32)
        real = first[:, :width] - second[:, width:]
        imag = first[:, width:] + second[:, :width]
        dst[0] = real.astype(dst.dtype)
        dst[1] = imag.astype(dst.dtype)


def rotate(own, partner, gathered):
    rows, band2 = own.shape
    rc, cb, co, k, width2 = gathered.shape
    width = width2 // 2
    x_spec = pl.BlockSpec((rows, band2), lambda c: (0, 0))
    g_spec = pl.BlockSpec((rc, None, co, k, width2), lambda c: (0, c, 0, 0, 0))
    o_spec = pl.BlockSpec((2, None, rows, width), lambda c: (0, c, 0, 0))
    out = jax.ShapeDtypeStruct((2, cb, rows, width), jnp.bfloat16)
    flops = 2 * 2 * rows * band2 * width2
    moved = 2 * own.size * 2 + gathered.size * 2 + 2 * own.size * 2
    return pl.pallas_call(
        rotate_kernel,
        grid=(cb,),
        in_specs=[x_spec, x_spec, g_spec],
        out_specs=[o_spec, o_spec],
        out_shape=[out, out],
        compiler_params=pltpu.CompilerParams(vmem_limit_bytes=48 * 1024 * 1024),
        cost_estimate=pl.CostEstimate(flops=flops, transcendentals=0, bytes_accessed=moved),
    )(own, partner, gathered)


def shards(rc_count, col_count, orbitals, applied_orbitals, ritz_matrix):
    me = lax.axis_index("core")
    rows = orbitals.shape[0]
    band_count = orbitals.shape[2]

    orb_out, app_out = ring_rotate(ritz_matrix, orbitals, applied_orbitals)
    return orb_out, app_out


def solution(mesh):
    devices = mesh.devices
    split = Mesh(
        devices.reshape(devices.shape[0] // 2, 2, devices.shape[1]), ("rc", "core", "col")
    )
    flat = ("rc", "core", "col")
    in_specs = (P(flat, None, None), P(flat, None, None), P(None, ("rc", "core"), "col"))
    out_specs = (P(flat, None, None), P(flat, None, None))
    body = functools.partial(shards, devices.shape[0] // 2, devices.shape[1])
    return jax.shard_map(body, mesh=split, in_specs=in_specs, out_specs=out_specs, check_vma=False)
```

```python
import functools

import jax
import jax.numpy as jnp
from jax import lax
from jax.experimental import pallas as pl
from jax.experimental.pallas import tpu as pltpu
from jax.sharding import Mesh
from jax.sharding import PartitionSpec as P

SWAP = [(0, 1), (1, 0)]
AXES = ("rc", "core", "col")
MESH = pl.DeviceIdType.MESH


RING = 4
ORDERS = (("x", "y", "z"), ("y", "z", "x"))
DIMS = ("y", "z_hi", "x", "z_lo")


def ring_rotate_kernel(
    x_ref, orb_ref, app_ref, orb_out, app_out, g_ref, own_ref, partner_ref, acc, lent, back, send_sem, recv_sem,
    local_sem, ring_send, ring_recv,
):
    rc = lax.axis_index("rc")
    core = lax.axis_index("core")
    col = lax.axis_index("col")
    here = {"y": rc // 2, "z": (rc % 2) * 2 + col % 2, "x": col // 2}

    def device(axis, delta):
        at = dict(here)
        at[axis] = lax.rem(at[axis] + delta + RING, RING)
        return (at["y"] * 2 + at["z"] // 2, core, at["x"] * 2 + at["z"] % 2)

    def view(held, axis=None, delta=0, half=None, pin=None):
        at = dict(here)
        pins = {} if pin is None else {pin[0]: pin[1]}
        if axis is not None:
            pins[axis] = delta
        for a, d in pins.items():
            at[a] = lax.rem(at[a] + d + RING, RING)
        held = tuple(h for h in held if h not in pins)
        index = []
        split = half is not None
        for dim in DIMS:
            phys = "z" if dim.startswith("z") else dim
            if phys in held:
                size = 2 if phys == "z" else RING
                if split:
                    index.append(pl.ds(half * (size // 2), size // 2))
                    split = False
                else:
                    index.append(slice(None))
            elif dim == "z_hi":
                index.append(at["z"] // 2)
            elif dim == "z_lo":
                index.append(at["z"] % 2)
            else:
                index.append(at[phys])
        if split:
            index.append(pl.ds(half, 1))
        return g_ref.at[tuple(index)]

    def remote(src, dst, slot, axis, delta):
        return pltpu.make_async_remote_copy(
            src_ref=src,
            dst_ref=dst,
            send_sem=send_sem.at[slot],
            recv_sem=recv_sem.at[slot],
            device_id=device(axis, delta),
            device_id_type=MESH,
        )

    partner = (rc, 1 - core, col)
    barrier = pltpu.get_barrier_semaphore()
    for axis in ("x", "y", "z"):
        for delta in (1, -1):
            pl.semaphore_signal(barrier, 1, device_id=device(axis, delta), device_id_type=MESH)
    pl.semaphore_signal(barrier, 1, device_id=partner, device_id_type=MESH)
    pl.semaphore_wait(barrier, 7)

    lend = pltpu.make_async_remote_copy(
        src_ref=own_ref,
        dst_ref=partner_ref,
        send_sem=send_sem.at[14],
        recv_sem=recv_sem.at[14],
        device_id=partner,
        device_id_type=MESH,
    )

    def build():
        count = orb_ref.shape[0]
        step = 32
        for a, raw in enumerate((orb_ref, app_ref)):
            for n in range(0, count, step):
                v = raw[pl.ds(n, step)]
                for q in range(2):
                    own_ref[pl.ds(a * count + n, step), pl.ds(q * band, band)] = v[:, q, :]

    band = own_ref.shape[1] // 2
    width = x_ref.shape[2] // 2
    depth = 2 * x_ref.shape[1]

    def compute(y, z, x):
        w = g_ref[y, z // 2, x, z % 2].reshape(depth, 2 * width)
        koff = pl.multiple_of((y * 2 + z // 2) * depth, depth)
        block = x * 2 + z % 2
        for src, rows in enumerate((own_ref, partner_ref)):
            first = jnp.dot(rows[:, pl.ds(koff, depth)], w, preferred_element_type=jnp.float32)
            second = jnp.dot(rows[:, pl.ds(band + koff, depth)], w, preferred_element_type=jnp.float32)
            acc[src, 0, block] += first[:, :width] - second[:, width:]
            acc[src, 1, block] += first[:, width:] + second[:, :width]

    def compute_block(held, axis=None, delta=0):
        at = dict(here)
        if axis is not None:
            at[axis] = lax.rem(at[axis] + delta + RING, RING)
        full = [d for d in ("y", "z", "x") if d in held]

        def body(i, carry):
            c = dict(at)
            rest = i
            for d in full:
                c[d] = rest % RING
                rest = rest // RING
            compute(c["y"], c["z"], c["x"])
            return carry

        lax.fori_loop(0, RING ** len(full), body, 0)

    unit = view(())
    keep = pl.multiple_of(core * width, width)
    give = pl.multiple_of((1 - core) * width, width)
    moves = []
    for p in range(2):
        dst = unit.at[core, :, pl.ds(p * width, width)]
        local = pltpu.make_async_copy(x_ref.at[p, :, pl.ds(keep, width)], dst, local_sem.at[p])
        local.start()
        swap = pltpu.make_async_remote_copy(
            src_ref=x_ref.at[p, :, pl.ds(give, width)],
            dst_ref=dst,
            send_sem=send_sem.at[12 + p],
            recv_sem=recv_sem.at[12 + p],
            device_id=partner,
            device_id_type=MESH,
        )
        swap.start()
        moves.append((local, swap, unit.at[1 - core, :, pl.ds(p * width, width)], p))
    for local, swap, dst, p in moves:
        local.wait()
        swap.wait_send()
        pltpu.make_async_remote_copy(
            src_ref=x_ref.at[p, :, pl.ds(give, width)],
            dst_ref=dst,
            send_sem=send_sem.at[12 + p],
            recv_sem=recv_sem.at[12 + p],
            device_id=partner,
            device_id_type=MESH,
        ).wait_recv()

    def ring(ref, slot, axis, delta):
        return pltpu.make_async_remote_copy(
            src_ref=ref,
            dst_ref=ref,
            send_sem=ring_send.at[slot],
            recv_sem=ring_recv.at[slot],
            device_id=device(axis, delta),
            device_id_type=MESH,
        )

    def run(order):
        held = ()
        sent = []
        pending = []
        for stage, axis in enumerate(order):
            base = stage * 10
            if stage == 0:
                parts = [None]
            else:
                prev = order[stage - 1]
                parts = [(prev, 0), (prev, -1), (prev, 1), (prev, 2)]

            def send_part(i):
                for j, delta in enumerate((1, -1)):
                    copy = ring(view(held, pin=parts[i]), base + 4 * j + i, axis, delta)
                    copy.start()
                    sent.append(copy)

            for i in range(max(1, len(parts) - 1)):
                send_part(i)
            if stage == 0:
                acc[...] = jnp.zeros_like(acc)
            if stage == 1:
                build()
                lend.start()
            for copy in pending:
                copy.wait_recv()
            if stage > 0:
                send_part(3)
            if stage == 2:
                lend.wait_send()
                pltpu.make_async_remote_copy(
                    src_ref=own_ref,
                    dst_ref=partner_ref,
                    send_sem=send_sem.at[14],
                    recv_sem=recv_sem.at[14],
                    device_id=partner,
                    device_id_type=MESH,
                ).wait_recv()
                compute_block(held)
            fwd_base = 30 + stage * 8
            for i in range(len(parts)):
                for j, delta in enumerate((1, -1)):
                    ring(view(held, axis, -delta, pin=parts[i]), base + 4 * j + i, axis, -delta).wait_recv()
                    half = 0 if delta == -1 else 1
                    copy = ring(view(held, axis, -delta, half, parts[i]), fwd_base + 2 * i + j, axis, delta)
                    copy.start()
                    sent.append(copy)
            if stage == 2:
                compute_block(held, axis, -1)
                compute_block(held, axis, 1)
            pending = []
            for i in range(len(parts)):
                for j, delta in enumerate((1, -1)):
                    half = 0 if delta == -1 else 1
                    pending.append(ring(view(held, axis, 2, half, parts[i]), fwd_base + 2 * i + j, axis, -delta))
            held = held + (axis,)
        for copy in pending:
            copy.wait_recv()
        for copy in sent:
            copy.wait_send()
        compute_block(held[:-1], order[-1], 2)

    for index, order in enumerate(ORDERS):
        @pl.when(core == index)
        def _():
            run(order)

    lent[...] = acc[1].astype(lent.dtype)
    give_back = pltpu.make_async_remote_copy(
        src_ref=lent,
        dst_ref=back,
        send_sem=send_sem.at[15],
        recv_sem=recv_sem.at[15],
        device_id=partner,
        device_id_type=MESH,
    )
    give_back.start()
    rows = orb_out.shape[0]
    blocks = acc.shape[2]

    def store(values, h):
        for a, out in enumerate((orb_out, app_out)):
            for c in range(blocks):
                lane = pl.multiple_of(c * 2 * width + h * width, width)
                part = [values[p, c, pl.ds(a * rows, rows), :].astype(out.dtype) for p in range(2)]
                out[:, :, pl.ds(lane, width)] = jnp.stack(part, axis=1)

    store(acc.at[0], core)
    give_back.wait_send()
    pltpu.make_async_remote_copy(
        src_ref=lent,
        dst_ref=back,
        send_sem=send_sem.at[15],
        recv_sem=recv_sem.at[15],
        device_id=partner,
        device_id_type=MESH,
    ).wait_recv()
    store(back, 1 - core)


def ring_rotate(ritz, orbitals, applied_orbitals):
    rows, band2 = 2 * orbitals.shape[0], 2 * orbitals.shape[2]
    own = orbitals
    units = (RING, 2, RING, 2, 2, ritz.shape[1], ritz.shape[2])
    width = ritz.shape[2] // 2
    out = jax.ShapeDtypeStruct((rows // 2, 2, band2 // 2), jnp.bfloat16)
    vmem = pl.BlockSpec(memory_space=pltpu.VMEM)
    flops = 2 * 2 * rows * band2 * 2 * ritz.shape[2] * 2 * RING
    return pl.pallas_call(
        ring_rotate_kernel,
        out_shape=[out, out],
        in_specs=[pl.BlockSpec(memory_space=pl.ANY), vmem, vmem],
        out_specs=[vmem, vmem],
        scratch_shapes=[
            pltpu.VMEM(units, ritz.dtype),
            pltpu.VMEM((rows, band2), own.dtype),
            pltpu.VMEM((rows, band2), own.dtype),
            pltpu.VMEM((2, 2, 2 * RING, rows, width), jnp.float32),
            pltpu.VMEM((2, 2 * RING, rows, width), jnp.bfloat16),
            pltpu.VMEM((2, 2 * RING, rows, width), jnp.bfloat16),
            pltpu.SemaphoreType.DMA((16,)),
            pltpu.SemaphoreType.DMA((16,)),
            pltpu.SemaphoreType.DMA((2,)),
            pltpu.SemaphoreType.DMA((54,)),
            pltpu.SemaphoreType.DMA((54,)),
        ],
        compiler_params=pltpu.CompilerParams(
            collective_id=0, has_side_effects=True, vmem_limit_bytes=60 * 1024 * 1024
        ),
        cost_estimate=pl.CostEstimate(flops=flops, transcendentals=0, bytes_accessed=8 * own.size * 2),
    )(ritz, orbitals, applied_orbitals)


def rotate_kernel(own_ref, partner_ref, ritz_ref, own_out, partner_out):
    band = own_ref.shape[1] // 2
    width = own_out.shape[-1]
    weights = ritz_ref[...].reshape(-1, 2 * width)
    for src, dst in ((own_ref, own_out), (partner_ref, partner_out)):
        first = jnp.dot(src[:, :band], weights, preferred_element_type=jnp.float32)
        second = jnp.dot(src[:, band:], weights, preferred_element_type=jnp.float32)
        real = first[:, :width] - second[:, width:]
        imag = first[:, width:] + second[:, :width]
        dst[0] = real.astype(dst.dtype)
        dst[1] = imag.astype(dst.dtype)


def rotate(own, partner, gathered):
    rows, band2 = own.shape
    rc, cb, co, k, width2 = gathered.shape
    width = width2 // 2
    x_spec = pl.BlockSpec((rows, band2), lambda c: (0, 0))
    g_spec = pl.BlockSpec((rc, None, co, k, width2), lambda c: (0, c, 0, 0, 0))
    o_spec = pl.BlockSpec((2, None, rows, width), lambda c: (0, c, 0, 0))
    out = jax.ShapeDtypeStruct((2, cb, rows, width), jnp.bfloat16)
    flops = 2 * 2 * rows * band2 * width2
    moved = 2 * own.size * 2 + gathered.size * 2 + 2 * own.size * 2
    return pl.pallas_call(
        rotate_kernel,
        grid=(cb,),
        in_specs=[x_spec, x_spec, g_spec],
        out_specs=[o_spec, o_spec],
        out_shape=[out, out],
        compiler_params=pltpu.CompilerParams(vmem_limit_bytes=48 * 1024 * 1024),
        cost_estimate=pl.CostEstimate(flops=flops, transcendentals=0, bytes_accessed=moved),
    )(own, partner, gathered)


def shards(rc_count, col_count, orbitals, applied_orbitals, ritz_matrix):
    me = lax.axis_index("core")
    rows = orbitals.shape[0]
    band_count = orbitals.shape[2]

    orb_out, app_out = ring_rotate(ritz_matrix, orbitals, applied_orbitals)
    return orb_out, app_out


def solution(mesh):
    devices = mesh.devices
    split = Mesh(
        devices.reshape(devices.shape[0] // 2, 2, devices.shape[1]), ("rc", "core", "col")
    )
    flat = ("rc", "core", "col")
    in_specs = (P(flat, None, None), P(flat, None, None), P(None, ("rc", "core"), "col"))
    out_specs = (P(flat, None, None), P(flat, None, None))
    body = functools.partial(shards, devices.shape[0] // 2, devices.shape[1])
    return jax.shard_map(body, mesh=split, in_specs=in_specs, out_specs=out_specs, check_vma=False)
```

```python
import functools

import jax
import jax.numpy as jnp
from jax import lax
from jax.experimental import pallas as pl
from jax.experimental.pallas import tpu as pltpu
from jax.sharding import Mesh
from jax.sharding import PartitionSpec as P

SWAP = [(0, 1), (1, 0)]
AXES = ("rc", "core", "col")
MESH = pl.DeviceIdType.MESH


RING = 4
ORDERS = (("x", "y", "z"), ("y", "z", "x"))
DIMS = ("y", "z_hi", "x", "z_lo")


def ring_rotate_kernel(
    x_ref, orb_ref, app_ref, orb_out, app_out, g_ref, own_ref, partner_ref, acc, lent, back, send_sem, recv_sem,
    local_sem, ring_send, ring_recv,
):
    rc = lax.axis_index("rc")
    core = lax.axis_index("core")
    col = lax.axis_index("col")
    here = {"y": rc // 2, "z": (rc % 2) * 2 + col % 2, "x": col // 2}

    def device(axis, delta):
        at = dict(here)
        at[axis] = lax.rem(at[axis] + delta + RING, RING)
        return (at["y"] * 2 + at["z"] // 2, core, at["x"] * 2 + at["z"] % 2)

    def view(held, axis=None, delta=0, half=None, pin=None):
        at = dict(here)
        pins = {} if pin is None else {pin[0]: pin[1]}
        if axis is not None:
            pins[axis] = delta
        for a, d in pins.items():
            at[a] = lax.rem(at[a] + d + RING, RING)
        held = tuple(h for h in held if h not in pins)
        index = []
        split = half is not None
        for dim in DIMS:
            phys = "z" if dim.startswith("z") else dim
            if phys in held:
                size = 2 if phys == "z" else RING
                if split:
                    index.append(pl.ds(half * (size // 2), size // 2))
                    split = False
                else:
                    index.append(slice(None))
            elif dim == "z_hi":
                index.append(at["z"] // 2)
            elif dim == "z_lo":
                index.append(at["z"] % 2)
            else:
                index.append(at[phys])
        if split:
            index.append(pl.ds(half, 1))
        return g_ref.at[tuple(index)]

    def remote(src, dst, slot, axis, delta):
        return pltpu.make_async_remote_copy(
            src_ref=src,
            dst_ref=dst,
            send_sem=send_sem.at[slot],
            recv_sem=recv_sem.at[slot],
            device_id=device(axis, delta),
            device_id_type=MESH,
        )

    partner = (rc, 1 - core, col)
    barrier = pltpu.get_barrier_semaphore()
    for axis in ("x", "y", "z"):
        for delta in (1, -1):
            pl.semaphore_signal(barrier, 1, device_id=device(axis, delta), device_id_type=MESH)
    pl.semaphore_signal(barrier, 1, device_id=partner, device_id_type=MESH)
    pl.semaphore_wait(barrier, 7)

    half_rows = own_ref.shape[0] // 2
    lend = pltpu.make_async_remote_copy(
        src_ref=own_ref.at[pl.ds(0, half_rows)],
        dst_ref=own_ref.at[pl.ds(half_rows, half_rows)],
        send_sem=send_sem.at[14],
        recv_sem=recv_sem.at[14],
        device_id=partner,
        device_id_type=MESH,
    )

    def build():
        count = orb_ref.shape[0]
        step = 32
        for a, raw in enumerate((orb_ref, app_ref)):
            for n in range(0, count, step):
                v = raw[pl.ds(n, step)]
                for q in range(2):
                    own_ref[pl.ds(a * count + n, step), pl.ds(q * band, band)] = v[:, q, :]

    band = own_ref.shape[1] // 2
    width = x_ref.shape[2] // 2
    depth = 2 * x_ref.shape[1]

    def compute(y, z, x):
        w = g_ref[y, z // 2, x, z % 2].reshape(depth, 2 * width)
        koff = pl.multiple_of((y * 2 + z // 2) * depth, depth)
        block = x * 2 + z % 2
        first = jnp.dot(own_ref[:, pl.ds(koff, depth)], w, preferred_element_type=jnp.float32)
        second = jnp.dot(own_ref[:, pl.ds(band + koff, depth)], w, preferred_element_type=jnp.float32)
        acc[0, block] += first[:, :width] - second[:, width:]
        acc[1, block] += first[:, width:] + second[:, :width]

    def compute_block(held, axis=None, delta=0):
        at = dict(here)
        if axis is not None:
            at[axis] = lax.rem(at[axis] + delta + RING, RING)
        full = [d for d in ("y", "z", "x") if d in held]

        def body(i, carry):
            c = dict(at)
            rest = i
            for d in full:
                c[d] = rest % RING
                rest = rest // RING
            compute(c["y"], c["z"], c["x"])
            return carry

        lax.fori_loop(0, RING ** len(full), body, 0)

    unit = view(())
    keep = pl.multiple_of(core * width, width)
    give = pl.multiple_of((1 - core) * width, width)
    moves = []
    for p in range(2):
        dst = unit.at[core, :, pl.ds(p * width, width)]
        local = pltpu.make_async_copy(x_ref.at[p, :, pl.ds(keep, width)], dst, local_sem.at[p])
        local.start()
        swap = pltpu.make_async_remote_copy(
            src_ref=x_ref.at[p, :, pl.ds(give, width)],
            dst_ref=dst,
            send_sem=send_sem.at[12 + p],
            recv_sem=recv_sem.at[12 + p],
            device_id=partner,
            device_id_type=MESH,
        )
        swap.start()
        moves.append((local, swap, unit.at[1 - core, :, pl.ds(p * width, width)], p))
    for local, swap, dst, p in moves:
        local.wait()
        swap.wait_send()
        pltpu.make_async_remote_copy(
            src_ref=x_ref.at[p, :, pl.ds(give, width)],
            dst_ref=dst,
            send_sem=send_sem.at[12 + p],
            recv_sem=recv_sem.at[12 + p],
            device_id=partner,
            device_id_type=MESH,
        ).wait_recv()

    def ring(ref, slot, axis, delta):
        return pltpu.make_async_remote_copy(
            src_ref=ref,
            dst_ref=ref,
            send_sem=ring_send.at[slot],
            recv_sem=ring_recv.at[slot],
            device_id=device(axis, delta),
            device_id_type=MESH,
        )

    def run(order):
        held = ()
        sent = []
        pending = []
        for stage, axis in enumerate(order):
            base = stage * 10
            if stage == 0:
                parts = [None]
            else:
                prev = order[stage - 1]
                parts = [(prev, 0), (prev, -1), (prev, 1), (prev, 2)]

            def send_part(i):
                for j, delta in enumerate((1, -1)):
                    copy = ring(view(held, pin=parts[i]), base + 4 * j + i, axis, delta)
                    copy.start()
                    sent.append(copy)

            for i in range(max(1, len(parts) - 1)):
                send_part(i)
            if stage == 0:
                acc[...] = jnp.zeros_like(acc)
            if stage == 1:
                build()
                lend.start()
            for copy in pending:
                copy.wait_recv()
            if stage > 0:
                send_part(3)
            if stage == 2:
                lend.wait_send()
                pltpu.make_async_remote_copy(
                    src_ref=own_ref.at[pl.ds(0, half_rows)],
                    dst_ref=own_ref.at[pl.ds(half_rows, half_rows)],
                    send_sem=send_sem.at[14],
                    recv_sem=recv_sem.at[14],
                    device_id=partner,
                    device_id_type=MESH,
                ).wait_recv()
                compute_block(held)
            fwd_base = 30 + stage * 8
            for i in range(len(parts)):
                for j, delta in enumerate((1, -1)):
                    ring(view(held, axis, -delta, pin=parts[i]), base + 4 * j + i, axis, -delta).wait_recv()
                    half = 0 if delta == -1 else 1
                    copy = ring(view(held, axis, -delta, half, parts[i]), fwd_base + 2 * i + j, axis, delta)
                    copy.start()
                    sent.append(copy)
            if stage == 2:
                compute_block(held, axis, -1)
                compute_block(held, axis, 1)
            pending = []
            for i in range(len(parts)):
                for j, delta in enumerate((1, -1)):
                    half = 0 if delta == -1 else 1
                    pending.append(ring(view(held, axis, 2, half, parts[i]), fwd_base + 2 * i + j, axis, -delta))
            held = held + (axis,)
        for copy in pending:
            copy.wait_recv()
        for copy in sent:
            copy.wait_send()
        compute_block(held[:-1], order[-1], 2)

    for index, order in enumerate(ORDERS):
        @pl.when(core == index)
        def _():
            run(order)

    lent[...] = acc[:, :, pl.ds(half_rows, half_rows), :].astype(lent.dtype)
    give_back = pltpu.make_async_remote_copy(
        src_ref=lent,
        dst_ref=back,
        send_sem=send_sem.at[15],
        recv_sem=recv_sem.at[15],
        device_id=partner,
        device_id_type=MESH,
    )
    give_back.start()
    rows = orb_out.shape[0]
    blocks = acc.shape[1]

    def store(values, h):
        for a, out in enumerate((orb_out, app_out)):
            for c in range(blocks):
                lane = pl.multiple_of(c * 2 * width + h * width, width)
                part = [values[p, c, pl.ds(a * rows, rows), :].astype(out.dtype) for p in range(2)]
                out[:, :, pl.ds(lane, width)] = jnp.stack(part, axis=1)

    store(acc, core)
    give_back.wait_send()
    pltpu.make_async_remote_copy(
        src_ref=lent,
        dst_ref=back,
        send_sem=send_sem.at[15],
        recv_sem=recv_sem.at[15],
        device_id=partner,
        device_id_type=MESH,
    ).wait_recv()
    store(back, 1 - core)


def ring_rotate(ritz, orbitals, applied_orbitals):
    rows, band2 = 2 * orbitals.shape[0], 2 * orbitals.shape[2]
    own = orbitals
    units = (RING, 2, RING, 2, 2, ritz.shape[1], ritz.shape[2])
    width = ritz.shape[2] // 2
    out = jax.ShapeDtypeStruct((rows // 2, 2, band2 // 2), jnp.bfloat16)
    vmem = pl.BlockSpec(memory_space=pltpu.VMEM)
    flops = 2 * 2 * rows * band2 * 2 * ritz.shape[2] * 2 * RING
    return pl.pallas_call(
        ring_rotate_kernel,
        out_shape=[out, out],
        in_specs=[pl.BlockSpec(memory_space=pl.ANY), vmem, vmem],
        out_specs=[vmem, vmem],
        scratch_shapes=[
            pltpu.VMEM(units, ritz.dtype),
            pltpu.VMEM((2 * rows, band2), own.dtype),
            pltpu.VMEM((rows, band2), own.dtype),
            pltpu.VMEM((2, 2 * RING, 2 * rows, width), jnp.float32),
            pltpu.VMEM((2, 2 * RING, rows, width), jnp.bfloat16),
            pltpu.VMEM((2, 2 * RING, rows, width), jnp.bfloat16),
            pltpu.SemaphoreType.DMA((16,)),
            pltpu.SemaphoreType.DMA((16,)),
            pltpu.SemaphoreType.DMA((2,)),
            pltpu.SemaphoreType.DMA((54,)),
            pltpu.SemaphoreType.DMA((54,)),
        ],
        compiler_params=pltpu.CompilerParams(
            collective_id=0, has_side_effects=True, vmem_limit_bytes=60 * 1024 * 1024
        ),
        cost_estimate=pl.CostEstimate(flops=flops, transcendentals=0, bytes_accessed=8 * own.size * 2),
    )(ritz, orbitals, applied_orbitals)


def rotate_kernel(own_ref, partner_ref, ritz_ref, own_out, partner_out):
    band = own_ref.shape[1] // 2
    width = own_out.shape[-1]
    weights = ritz_ref[...].reshape(-1, 2 * width)
    for src, dst in ((own_ref, own_out), (partner_ref, partner_out)):
        first = jnp.dot(src[:, :band], weights, preferred_element_type=jnp.float32)
        second = jnp.dot(src[:, band:], weights, preferred_element_type=jnp.float32)
        real = first[:, :width] - second[:, width:]
        imag = first[:, width:] + second[:, :width]
        dst[0] = real.astype(dst.dtype)
        dst[1] = imag.astype(dst.dtype)


def rotate(own, partner, gathered):
    rows, band2 = own.shape
    rc, cb, co, k, width2 = gathered.shape
    width = width2 // 2
    x_spec = pl.BlockSpec((rows, band2), lambda c: (0, 0))
    g_spec = pl.BlockSpec((rc, None, co, k, width2), lambda c: (0, c, 0, 0, 0))
    o_spec = pl.BlockSpec((2, None, rows, width), lambda c: (0, c, 0, 0))
    out = jax.ShapeDtypeStruct((2, cb, rows, width), jnp.bfloat16)
    flops = 2 * 2 * rows * band2 * width2
    moved = 2 * own.size * 2 + gathered.size * 2 + 2 * own.size * 2
    return pl.pallas_call(
        rotate_kernel,
        grid=(cb,),
        in_specs=[x_spec, x_spec, g_spec],
        out_specs=[o_spec, o_spec],
        out_shape=[out, out],
        compiler_params=pltpu.CompilerParams(vmem_limit_bytes=48 * 1024 * 1024),
        cost_estimate=pl.CostEstimate(flops=flops, transcendentals=0, bytes_accessed=moved),
    )(own, partner, gathered)


def shards(rc_count, col_count, orbitals, applied_orbitals, ritz_matrix):
    me = lax.axis_index("core")
    rows = orbitals.shape[0]
    band_count = orbitals.shape[2]

    orb_out, app_out = ring_rotate(ritz_matrix, orbitals, applied_orbitals)
    return orb_out, app_out


def solution(mesh):
    devices = mesh.devices
    split = Mesh(
        devices.reshape(devices.shape[0] // 2, 2, devices.shape[1]), ("rc", "core", "col")
    )
    flat = ("rc", "core", "col")
    in_specs = (P(flat, None, None), P(flat, None, None), P(None, ("rc", "core"), "col"))
    out_specs = (P(flat, None, None), P(flat, None, None))
    body = functools.partial(shards, devices.shape[0] // 2, devices.shape[1])
    return jax.shard_map(body, mesh=split, in_specs=in_specs, out_specs=out_specs, check_vma=False)
```
